32 devices in a mesh: dp: 8 (over y, x, core), tensor: 4 (over z).
Axes of the slice: x: 2, y: 2, z: 4, core: 2. Of those that a mesh axis runs over, the one named last changes fastest.
Arguments:
- tokens: bfloat16 [32768, 768], P(('dp', 'tensor')), may hold values from -6 to 6
- qkv_weight: bfloat16 [768, 3, 768], P('dp', None, 'tensor'), may hold values from -0.3125 to 0.3125
- qv_bias: float32 [2, 768], replicated, may hold values from -3 to 3
- out_weight: bfloat16 [768, 768], P('dp', 'tensor'), may hold values from -0.875 to 0.875
- out_bias: float32 [768], replicated, may hold values from -2 to 2
- norm1_gain: float32 [768], replicated, may hold values from 0.1 to 1.9
- norm1_shift: float32 [768], replicated, may hold values from -2 to 2
- in_weight: bfloat16 [768, 2, 3072], P('dp', None, 'tensor'), may hold values from -0.21875 to 0.21875
- down_weight: bfloat16 [768, 3072], P('dp', 'tensor'), may hold values from -0.15625 to 0.15625
- down_bias: float32 [768], replicated, may hold values from -2 to 2
- norm2_gain: float32 [768], replicated, may hold values from 0.1 to 1.9
- norm2_shift: float32 [768], replicated, may hold values from -2 to 2
- cotangent: bfloat16 [32768, 768], P(('dp', 'tensor')), may hold values from -6 to 6
Outputs:
- layer_out: bfloat16 [32768, 768], P(('dp', 'tensor'))
- tokens_grad: bfloat16 [32768, 768], P(('dp', 'tensor'))
- qkv_weight_grad: float32 [768, 3, 768], P('dp', None, 'tensor')
- qv_bias_grad: float32 [2, 768], replicated
- out_weight_grad: float32 [768, 768], P('dp', 'tensor')
- out_bias_grad: float32 [768], replicated
- norm1_gain_grad: float32 [768], replicated
- norm1_shift_grad: float32 [768], replicated
- in_weight_grad: float32 [768, 2, 3072], P('dp', None, 'tensor')
- down_weight_grad: float32 [768, 3072], P('dp', 'tensor')
- down_bias_grad: float32 [768], replicated
- norm2_gain_grad: float32 [768], replicated
- norm2_shift_grad: float32 [768], replicated
The draws below stay inside these ranges and needn't reach their ends.
All inputs are finite; a program needn't handle non-finite values.
Results may differ from the reference program's by a relative error of at most 0.02.
The reference program's roundings to bfloat16 on the way count: a program that leaves them out, or rounds other values in their place, can miss the bound.
Values may be sent and summed in bfloat16 or wider, within the bound.
No kernel may reach another device: no remote copies, remote signals or barrier semaphores. Data moves between devices by JAX's collectives and lax.ppermute only.
A program may use at most 192 MiB of HBM per device.

```python
import math
import jax
import jax.numpy as jnp
from jax import lax

D = 768
HEADS = 12
HEAD = 64
FF = 3072
SEQ = 1024
TOKENS = 32768
N_TENSOR = 4


def strengthened(entries, rng, source, target, shards_of, factor):
    def block_of(axis_at):
        return (jnp.arange(entries.shape[axis_at]) // (entries.shape[axis_at] // shards_of)).reshape((-1,) + (1,) * (entries.ndim - 1 - axis_at))

    near = jax.random.permutation(rng, shards_of)[block_of(target)]
    other_side = (block_of(target) + shards_of // 2) % shards_of
    return jnp.where((block_of(source) == near) | (block_of(source) == other_side), factor * entries, entries)


def levels(key, extent, split, least, high):
    factor_of, own = 1.0, jax.random.fold_in(key, 6)
    for dim, shards_of in split:
        steps = jnp.exp(jax.random.uniform(jax.random.fold_in(own, dim), (shards_of,), jnp.float32, least / len(split), high / len(split)))
        factor_of = factor_of * jnp.repeat(steps, extent[dim] // shards_of).reshape([-1 if axis == dim else 1 for axis in range(len(extent))])
    return factor_of


def bell_draw(own_key, dims, deviation, reach, split=(), kind=jnp.bfloat16):
    array = deviation * jax.random.normal(own_key, dims, jnp.float32)
    if split:
        array = array * levels(own_key, dims, split, -0.22, 0.18)
    return jnp.clip(array, -reach, reach).astype(kind)


def gaussian_with(key, dims, width, limit, cuts, heavy, held_as=jnp.bfloat16):
    drawn = width * jax.random.normal(key, dims, jnp.float32)
    if cuts:
        drawn = drawn * levels(key, dims, cuts, -0.22, 0.18)
    return jnp.clip(strengthened(drawn, jax.random.fold_in(key, 3), *heavy), -limit, limit).astype(held_as)


def setup_inputs(seed: int = 0) -> dict:
    keys = jax.random.split(jax.random.key(seed), 14)
    return {
        "tokens": bell_draw(keys[0], (TOKENS, D), 1.0, 6.0, ((0, 32),)),
        "qkv_weight": bell_draw(keys[1], (D, 3, D), (D // 2) ** -0.5, 0.3125, ((0, 8), (2, 4))),
        "qv_bias": bell_draw(keys[2], (2, D), 0.5, 3.0, (), jnp.float32),
        "out_weight": bell_draw(keys[3], (D, D), (D // 16) ** -0.5, 0.875, ((0, 8), (1, 4))),
        "out_bias": bell_draw(keys[4], (D,), 0.3, 2.0, (), jnp.float32),
        "norm1_gain": jnp.clip(1.0 + 0.18 * jax.random.normal(keys[5], (D,), jnp.float32), 0.1, 1.9),
        "norm1_shift": bell_draw(keys[6], (D,), 0.3, 2.0, (), jnp.float32),
        "in_weight": bell_draw(keys[7], (D, 2, FF), D ** -0.5, 0.21875, ((0, 8), (2, 4))),
        "down_weight": bell_draw(keys[8], (D, FF), (FF // 2) ** -0.5, 0.15625, ((0, 8), (1, 4))),
        "down_bias": bell_draw(keys[9], (D,), 0.3, 2.0, (), jnp.float32),
        "norm2_gain": jnp.clip(1.0 + 0.18 * jax.random.normal(keys[10], (D,), jnp.float32), 0.1, 1.9),
        "norm2_shift": bell_draw(keys[11], (D,), 0.3, 2.0, (), jnp.float32),
        "cotangent": gaussian_with(keys[12], (TOKENS, D), 1.0, 6.0, ((0, 32),), (0, 1, 32, 2.75)),
    }


@jax.custom_vjp
def low(v):
    return lax.optimization_barrier(v.astype(jnp.bfloat16)).astype(jnp.float32)

@jax.custom_vjp
def low_back(v):
    return v

def low_keep(v):
    return (low(v), None)

def low_pass(kept, grad):
    return (grad,)

def back_keep(v):
    return (v, None)

def back_low(kept, grad):
    return (low(grad),)
low.defvjp(low_keep, low_pass)
low_back.defvjp(back_keep, back_low)
NORM_EPS = 1e-12
HIGHEST = lax.Precision.HIGHEST

def head_slopes():
    head_ids = jnp.arange(HEADS, dtype=jnp.int32)
    powers = jnp.where(head_ids < 8, -(head_ids + 1).astype(jnp.float32), 7.5 - head_ids.astype(jnp.float32))
    return jnp.exp2(powers)

def layer_norm(resid, gain, shift):
    center = resid - lax.optimization_barrier(jnp.mean(resid, axis=1, keepdims=True))
    inverse = lax.rsqrt(lax.optimization_barrier(jnp.mean(center * center, axis=1, keepdims=True)) + NORM_EPS)
    return center * inverse * gain + shift

def attend_sequence(parts):
    queries, key_rows, value_rows = parts
    length = queries.shape[0]
    position = jnp.arange(length, dtype=jnp.float32)
    distance = jnp.abs(position[:, None] - position[None, :])
    scores = jnp.einsum('qhd,khd->hqk', queries, key_rows, precision=HIGHEST) * (1.0 / math.sqrt(HEAD))
    scores = low_back(scores - head_slopes()[:, None, None] * distance)
    probs = low(jax.nn.softmax(scores, axis=-1))
    context = jnp.einsum('hqk,khd->qhd', probs, value_rows, precision=HIGHEST)
    return low(low_back(context))

def layer_forward(params, row_block):
    qkv_weight, qv_bias, out_weight, out_bias, norm1_gain, norm1_shift, in_weight, down_weight, down_bias, norm2_gain, norm2_shift = params
    projected = jnp.dot(row_block, qkv_weight.reshape(D, 3 * D), precision=HIGHEST)
    queries = low(low_back(projected[:, :D]) + qv_bias[0])
    key_rows = low(low_back(projected[:, D:2 * D]))
    value_rows = low(low_back(projected[:, 2 * D:]) + qv_bias[1])
    seq_count = row_block.shape[0] // SEQ

    def by_sequence(matrix):
        return matrix.reshape(seq_count, SEQ, HEADS, HEAD)
    context = lax.map(jax.checkpoint(attend_sequence), (by_sequence(queries), by_sequence(key_rows), by_sequence(value_rows)))
    context = context.reshape(seq_count * SEQ, D)
    attention = low_back(jnp.dot(context, out_weight.T, precision=HIGHEST))
    resid1 = row_block + attention + out_bias
    hidden1 = layer_norm(resid1, norm1_gain, norm1_shift)
    hidden1_low = low(hidden1)
    gate_up = low_back(jnp.dot(hidden1_low, in_weight.reshape(D, 2 * FF), precision=HIGHEST))
    gated = low(jax.nn.gelu(gate_up[:, :FF], approximate=False) * gate_up[:, FF:])
    ffn_out = low_back(jnp.dot(gated, down_weight.T, precision=HIGHEST))
    resid2 = hidden1 + ffn_out + down_bias
    return layer_norm(resid2, norm2_gain, norm2_shift)

def reference(tokens, qkv_weight, qv_bias, out_weight, out_bias, norm1_gain, norm1_shift, in_weight, down_weight, down_bias, norm2_gain, norm2_shift, cotangent):
    params = tuple((item.astype(jnp.float32) for item in (qkv_weight, qv_bias, out_weight, out_bias, norm1_gain, norm1_shift, in_weight, down_weight, down_bias, norm2_gain, norm2_shift)))
    block_rows = N_TENSOR * SEQ
    block_count = tokens.shape[0] // block_rows
    rows_all = tokens.astype(jnp.float32).reshape(block_count, block_rows, D)
    grads_all = cotangent.astype(jnp.float32).reshape(block_count, block_rows, D)

    def step(summed, item):
        row_block, grad_block = item
        result, pull_back = jax.vjp(layer_forward, params, row_block)
        param_grads, row_grads = pull_back(grad_block)
        summed = jax.tree.map(lambda left, right: left + right, summed, param_grads)
        return (summed, (result.astype(jnp.bfloat16), row_grads.astype(jnp.bfloat16)))
    zeros_all = jax.tree.map(jnp.zeros_like, params)
    summed, (results, row_grads) = lax.scan(step, zeros_all, (rows_all, grads_all))
    return (results.reshape(-1, D), row_grads.reshape(-1, D), summed[0], summed[1], summed[2], summed[3], summed[4], summed[5], summed[6], summed[7], summed[8], summed[9], summed[10])
```

```python
import functools
import math

import jax
import jax.numpy as jnp
from jax import lax
from jax.experimental import pallas as pl
from jax.experimental.pallas import tpu as pltpu
from jax.sharding import PartitionSpec as P

HEAD = 64
SEQ = 1024
GROUP = 4
QB = 256
LOG2E = 1.4426950408889634
SCALE = LOG2E / math.sqrt(HEAD)
NT = (((1,), (1,)), ((), ()))
NN = (((1,), (0,)), ((), ()))


def mm(left, right, dims=NN):
    return lax.dot_general(left, right, dims, preferred_element_type=jnp.float32)


def fill_row_distance(dist_ref):
    shape = dist_ref.shape
    row = lax.broadcasted_iota(jnp.int32, shape, 0)
    col = lax.broadcasted_iota(jnp.int32, shape, 1)
    dist_ref[...] = jnp.abs(row - col + (SEQ - QB)).astype(jnp.float32) * LOG2E


def attend_kernel(slope_ref, qkv_ref, ctx_ref, lse_ref, dist_ref):
    hh = pl.program_id(0)
    width = GROUP * HEAD

    @pl.when(hh == 0)
    def _():
        fill_row_distance(dist_ref)

    lane = lax.broadcasted_iota(jnp.int32, (1, 128), 1)
    for pair in range(GROUP // 2):
        keys = qkv_ref[:, width + 128 * pair : width + 128 * pair + 128]
        values = qkv_ref[:, 2 * width + 128 * pair : 2 * width + 128 * pair + 128]
        for block in range(SEQ // QB):
            rows = slice(block * QB, (block + 1) * QB)
            q = qkv_ref[rows, 128 * pair : 128 * pair + 128]
            parts = []
            stats = []
            for side in range(2):
                own = (lane < HEAD) if side == 0 else (lane >= HEAD)
                slope = slope_ref[hh * GROUP + 2 * pair + side]
                s = mm(jnp.where(own, q, jnp.zeros_like(q)), keys, NT) * SCALE
                s = s - slope * dist_ref[:, SEQ - QB - block * QB : 2 * SEQ - QB - block * QB]
                top = jnp.max(s, axis=1, keepdims=True)
                w = jnp.exp2(s - top)
                total = jnp.sum(w, axis=1, keepdims=True)
                p = (w * (1.0 / total)).astype(jnp.bfloat16)
                parts.append(mm(p, values))
                stats.append(top + jnp.log2(total))
            ctx = jnp.where(lane < HEAD, parts[0], parts[1])
            ctx_ref[rows, 128 * pair : 128 * pair + 128] = ctx.astype(jnp.bfloat16)
            stat = jnp.where(lane < HEAD, stats[0], stats[1])
            flipped = stat.T
            lse_ref[2 * pair : 2 * pair + 1, rows] = flipped[0:1, :]
            lse_ref[2 * pair + 1 : 2 * pair + 2, rows] = flipped[HEAD : HEAD + 1, :]


def attend_forward(qkv, slopes):
    groups = qkv.shape[1] // (3 * GROUP * HEAD)
    return pl.pallas_call(
        attend_kernel,
        grid=(groups,),
        in_specs=[
            pl.BlockSpec(memory_space=pltpu.SMEM),
            pl.BlockSpec((SEQ, 3 * GROUP * HEAD), lambda g: (0, g)),
        ],
        out_specs=[
            pl.BlockSpec((SEQ, GROUP * HEAD), lambda g: (0, g)),
            pl.BlockSpec((None, GROUP, SEQ), lambda g: (g, 0, 0)),
        ],
        out_shape=[
            jax.ShapeDtypeStruct((SEQ, groups * GROUP * HEAD), jnp.bfloat16),
            jax.ShapeDtypeStruct((groups, GROUP, SEQ), jnp.float32),
        ],
        scratch_shapes=[pltpu.VMEM((QB, 2 * SEQ - QB), jnp.float32)],
        compiler_params=pltpu.CompilerParams(vmem_limit_bytes=40 << 20),
        name="attend_forward",
    )(slopes, qkv)


def fill_distance(dist_ref):
    row = lax.broadcasted_iota(jnp.int32, dist_ref.shape, 0)
    col = lax.broadcasted_iota(jnp.int32, dist_ref.shape, 1)
    dist_ref[...] = jnp.abs(row - col - (SEQ - QB)).astype(jnp.float32) * LOG2E


def attend_back_kernel(base, slope_ref, qkv_ref, lse_ref, dctx_ref, dqkv_ref, sums_ref, dist_ref, acc_ref, dqt_ref):
    width = GROUP * HEAD
    @pl.when(pl.program_id(0) == 0)
    def _():
        fill_distance(dist_ref)

    lane = lax.broadcasted_iota(jnp.int32, (1, 128), 1)
    for pair in range(GROUP // 2):
        cols = slice(128 * pair, 128 * pair + 128)
        keys = qkv_ref[:, width + 128 * pair : width + 128 * pair + 128]
        values = qkv_ref[:, 2 * width + 128 * pair : 2 * width + 128 * pair + 128]
        keys_t = keys.T
        for side in range(2):
            own = (lane < HEAD) if side == 0 else (lane >= HEAD)
            own_rows = slice(HEAD * side, HEAD * side + HEAD)
            slope = slope_ref[base + 2 * pair + side]
            for block in range(SEQ // QB):
                rows = slice(block * QB, (block + 1) * QB)
                q = qkv_ref[rows, 128 * pair : 128 * pair + 128]
                q = jnp.where(own, q, jnp.zeros_like(q))
                do = dctx_ref[rows, cols]
                do = jnp.where(own, do, jnp.zeros_like(do))
                s = mm(keys, q, NT) * SCALE
                start = SEQ - QB - block * QB
                s = s - slope * dist_ref[start : start + SEQ, :]
                p = jnp.exp2(s - lse_ref[2 * pair + side : 2 * pair + side + 1, rows])
                dp = mm(values, do, NT)
                inner = jnp.sum(p * dp, axis=0, keepdims=True)
                ds = (p * (dp - inner)).astype(jnp.bfloat16)
                p = p.astype(jnp.bfloat16)
                dv = mm(p, do)
                dk = mm(ds, q)
                if block == 0 and side == 0:
                    acc_ref[:, 0:128] = dk
                    acc_ref[:, 128:256] = dv
                else:
                    acc_ref[:, 0:128] += dk
                    acc_ref[:, 128:256] += dv
                dqt_ref[own_rows, rows] = mm(keys_t[own_rows], ds)
        dq = dqt_ref[...].T * (1.0 / math.sqrt(HEAD))
        dk = acc_ref[:, 0:128] * (1.0 / math.sqrt(HEAD))
        dv = acc_ref[:, 128:256]
        dqkv_ref[:, 128 * pair : 128 * pair + 128] = dq.astype(jnp.bfloat16)
        dqkv_ref[:, width + 128 * pair : width + 128 * pair + 128] = dk.astype(jnp.bfloat16)
        dqkv_ref[:, 2 * width + 128 * pair : 2 * width + 128 * pair + 128] = dv.astype(jnp.bfloat16)
        sums_ref[0:1, cols] = jnp.sum(dq, axis=0, keepdims=True)
        sums_ref[1:2, cols] = jnp.sum(dv, axis=0, keepdims=True)


def attend_backward(qkv, lse, dctx, slopes, group):
    width = GROUP * HEAD
    return pl.pallas_call(
        functools.partial(attend_back_kernel, group * GROUP),
        grid=(1,),
        in_specs=[
            pl.BlockSpec(memory_space=pltpu.SMEM),
            pl.BlockSpec((SEQ, 3 * width), lambda g: (0, group)),
            pl.BlockSpec((None, GROUP, SEQ), lambda g: (group, 0, 0)),
            pl.BlockSpec((SEQ, width), lambda g: (0, group)),
        ],
        out_specs=[
            pl.BlockSpec((SEQ, 3 * width), lambda g: (0, 0)),
            pl.BlockSpec((2, width), lambda g: (0, 0)),
        ],
        out_shape=[
            jax.ShapeDtypeStruct((SEQ, 3 * width), jnp.bfloat16),
            jax.ShapeDtypeStruct((2, width), jnp.float32),
        ],
        scratch_shapes=[
            pltpu.VMEM((2 * SEQ - QB, QB), jnp.float32),
            pltpu.VMEM((SEQ, 256), jnp.float32),
            pltpu.VMEM((128, SEQ), jnp.float32),
        ],
        compiler_params=pltpu.CompilerParams(vmem_limit_bytes=40 << 20),
        name="attend_backward",
    )(slopes, qkv, lse, dctx)


NORM_EPS = 1e-12
INV_ROOT_TWO = 0.7071067811865476
INV_ROOT_TWO_PI = 0.3989422804014327
FF_CHUNKS = 3


def norm_forward(resid, gain, shift):
    center = resid - jnp.mean(resid, axis=1, keepdims=True)
    inverse = lax.rsqrt(jnp.mean(center * center, axis=1, keepdims=True) + NORM_EPS)
    normed = center * inverse
    return (normed * gain + shift, normed, inverse)


def norm_backward(grad_rows, normed, inverse, gain):
    scaled = grad_rows * gain
    first_mean = jnp.mean(scaled, axis=1, keepdims=True)
    second_mean = jnp.mean(scaled * normed, axis=1, keepdims=True)
    d_resid = inverse * (scaled - first_mean - normed * second_mean)
    return (d_resid, jnp.sum(grad_rows * normed, axis=0), jnp.sum(grad_rows, axis=0))


def gelu_parts(gate_part):
    normal_cdf = 0.5 * (1.0 + lax.erf(gate_part * INV_ROOT_TWO))
    density = jnp.exp(-0.5 * gate_part * gate_part) * INV_ROOT_TWO_PI
    return (gate_part * normal_cdf, normal_cdf + gate_part * density)


class Links:
    def __init__(self, mesh_shape):
        self.dp = mesh_shape["dp"]
        self.tensor = mesh_shape["tensor"]
        self.paired = self.dp == 8 and self.tensor == 4

    def swap(self, value, axis, bit):
        size = self.dp if axis == "dp" else self.tensor
        return lax.ppermute(value, axis, [(i, i ^ bit) for i in range(size)])

    def tensor_order(self):
        places = jnp.arange(self.tensor, dtype=jnp.int32)
        return places ^ lax.axis_index("tensor") if self.paired else places

    def gather(self, piece, dp_bits):
        rows = piece.shape[0]
        if not self.paired:
            columns = lax.all_gather(piece, "tensor", axis=2)
            return lax.all_gather(columns, "dp", axis=0, tiled=True)
        second = self.swap(piece, "tensor", 2)
        pair = jnp.stack([piece, second])
        other = self.swap(pair, "tensor", 1)
        columns = jnp.stack([piece, other[0], second, other[1]], axis=2)
        held = {0: columns}
        for bit in dp_bits:
            for place in list(held):
                held[place | bit] = self.swap(held[place], "dp", bit)
        me = lax.axis_index("dp")
        whole = jnp.zeros((self.dp * rows,) + columns.shape[1:], piece.dtype)
        for place, value in held.items():
            whole = lax.dynamic_update_slice(whole, value, ((me ^ place) * rows, 0, 0, 0))
        return whole

    def scatter(self, grad, dp_bits):
        if not self.paired:
            mine = lax.psum_scatter(grad, "dp", scatter_dimension=0, tiled=True)
            return lax.psum_scatter(mine, "tensor", scatter_dimension=2, tiled=False).astype(jnp.float32)
        rows = grad.shape[0] // self.dp
        me = lax.axis_index("dp")
        held = {
            place: lax.dynamic_slice_in_dim(grad, (me ^ place) * rows, rows, 0)
            for place in range(self.dp)
        }
        for bit in dp_bits:
            for place in [p for p in held if p & bit]:
                arrived = self.swap(held.pop(place), "dp", bit)
                mine = held[place ^ bit].astype(jnp.float32) + arrived.astype(jnp.float32)
                held[place ^ bit] = mine.astype(jnp.bfloat16)
        mine = held[0]
        arrived = self.swap(mine[:, :, 1::2], "tensor", 1)
        mine = (mine[:, :, 0::2].astype(jnp.float32) + arrived.astype(jnp.float32)).astype(jnp.bfloat16)
        arrived = self.swap(mine[:, :, 1], "tensor", 2)
        return mine[:, :, 0].astype(jnp.float32) + arrived.astype(jnp.float32)

    def total(self, value):
        if not self.paired:
            return lax.psum(value, ("dp", "tensor"))
        for axis, bit in (("dp", 1), ("dp", 4), ("dp", 2), ("tensor", 1), ("tensor", 2)):
            value = value + self.swap(value, axis, bit)
        return value


def local(
    links,
    tokens,
    qkv_weight,
    qv_bias,
    out_weight,
    out_bias,
    norm1_gain,
    norm1_shift,
    in_weight,
    down_weight,
    down_bias,
    norm2_gain,
    norm2_shift,
    cotangent,
):
    width = tokens.shape[1]
    rows = qkv_weight.shape[0]
    n_tensor = links.tensor
    groups = qkv_weight.shape[2] // HEAD
    part = in_weight.shape[2] // FF_CHUNKS

    qkv_pieces = qkv_weight.reshape(rows, 3, groups, HEAD)
    qkv_full = [links.gather(qkv_pieces[:, :, g], (2, 4, 1)).reshape(width, -1) for g in range(groups)]
    qkv_full = jnp.concatenate(qkv_full, axis=1)
    out_full = links.gather(out_weight.reshape(rows, groups, HEAD), (4, 2, 1)).reshape(width, -1)
    in_full = []
    down_full = []
    for c in range(FF_CHUNKS):
        cols = slice(c * part, (c + 1) * part)
        piece = jnp.concatenate([in_weight[:, :, cols], down_weight[:, None, cols]], axis=1)
        full = links.gather(piece, (2, 4, 1) if c % 2 else (4, 2, 1))
        in_full.append(full[:, :2].reshape(width, -1))
        down_full.append(full[:, 2].reshape(width, -1))

    places = links.tensor_order()
    head_ids = (places[None, :] * groups + jnp.arange(groups, dtype=jnp.int32)[:, None]).reshape(-1)
    powers = jnp.where(
        head_ids < 8, -(head_ids + 1).astype(jnp.float32), 7.5 - head_ids.astype(jnp.float32)
    )
    slopes = jnp.exp2(powers)
    bias_cols = qv_bias.reshape(2, n_tensor, groups, HEAD)[:, places].transpose(0, 2, 1, 3)
    bias_cols = bias_cols.reshape(2, groups, n_tensor * HEAD)
    bias_row = jnp.stack([bias_cols[0], jnp.zeros_like(bias_cols[0]), bias_cols[1]], axis=1).reshape(-1)

    projected = jnp.dot(tokens, qkv_full, preferred_element_type=jnp.float32)
    qkv = (projected + bias_row).astype(jnp.bfloat16)
    context, lse = attend_forward(qkv, slopes)
    attention = jnp.einsum("rc,oc->ro", context, out_full, preferred_element_type=jnp.float32)
    resid1 = tokens.astype(jnp.float32) + attention + out_bias
    hidden1, normed1, inverse1 = norm_forward(resid1, norm1_gain, norm1_shift)
    hidden1_low = hidden1.astype(jnp.bfloat16)
    ffn_out = 0.0
    kept = []
    for c in range(FF_CHUNKS):
        gate_up = jnp.dot(hidden1_low, in_full[c], preferred_element_type=jnp.float32)
        gate_part = gate_up[:, : part * n_tensor]
        up_part = gate_up[:, part * n_tensor :]
        activated, slope_gelu = gelu_parts(gate_part)
        gated = (activated * up_part).astype(jnp.bfloat16)
        ffn_out = ffn_out + jnp.einsum(
            "rf,of->ro", gated, down_full[c], preferred_element_type=jnp.float32
        )
        kept.append((gated, (up_part * slope_gelu).astype(jnp.bfloat16), activated.astype(jnp.bfloat16)))
    resid2 = hidden1 + ffn_out + down_bias
    result, normed2, inverse2 = norm_forward(resid2, norm2_gain, norm2_shift)

    d_resid2, norm2_gain_grad, norm2_shift_grad = norm_backward(
        cotangent.astype(jnp.float32), normed2, inverse2, norm2_gain
    )
    down_bias_grad = jnp.sum(d_resid2, axis=0)
    d_ffn_low = d_resid2.astype(jnp.bfloat16)
    d_hidden1 = d_resid2
    in_grads = []
    down_grads = []
    for c in range(FF_CHUNKS):
        gated, slope_up, activated = kept[c]
        d_gated = jnp.dot(d_ffn_low, down_full[c], preferred_element_type=jnp.float32)
        d_gate_up = jnp.concatenate([d_gated * slope_up, d_gated * activated], axis=1)
        d_gate_up = d_gate_up.astype(jnp.bfloat16)
        down_grad = jnp.einsum("ro,rf->of", d_ffn_low, gated, preferred_element_type=jnp.float32)
        in_grad = jnp.einsum("rd,rc->dc", hidden1_low, d_gate_up, preferred_element_type=jnp.float32)
        d_hidden1 = d_hidden1 + jnp.einsum(
            "rc,dc->rd", d_gate_up, in_full[c], preferred_element_type=jnp.float32
        )
        grad = jnp.concatenate([in_grad, down_grad], axis=1).astype(jnp.bfloat16)
        mine = links.scatter(grad.reshape(width, 3, n_tensor, part), (1, 2, 4) if c % 2 else (1, 4, 2))
        in_grads.append(mine[:, :2])
        down_grads.append(mine[:, 2])
    d_resid1, norm1_gain_grad, norm1_shift_grad = norm_backward(
        d_hidden1, normed1, inverse1, norm1_gain
    )
    out_bias_grad = jnp.sum(d_resid1, axis=0)
    d_attn_low = d_resid1.astype(jnp.bfloat16)
    d_context = jnp.dot(d_attn_low, out_full, preferred_element_type=jnp.float32).astype(jnp.bfloat16)
    out_grad = jnp.einsum("ro,rc->oc", d_attn_low, context, preferred_element_type=jnp.float32)
    out_grad = links.scatter(
        out_grad.astype(jnp.bfloat16).reshape(width, groups, n_tensor, HEAD), (1, 2, 4)
    ).reshape(rows, -1)
    d_tokens = d_resid1
    qkv_grads = []
    bias_grads = []
    for g in range(groups):
        d_qkv, sums = attend_backward(qkv, lse, d_context, slopes, g)
        grad = jnp.einsum("rd,rc->dc", tokens, d_qkv, preferred_element_type=jnp.float32)
        grad = grad.astype(jnp.bfloat16).reshape(width, 3, n_tensor, HEAD)
        qkv_grads.append(links.scatter(grad, (1, 2, 4) if g % 2 else (1, 4, 2)))
        d_tokens = d_tokens + jnp.einsum(
            "rc,dc->rd",
            d_qkv,
            qkv_full[:, g * d_qkv.shape[1] : (g + 1) * d_qkv.shape[1]],
            preferred_element_type=jnp.float32,
        )
        bias_grads.append(sums.reshape(2, n_tensor, HEAD))
    tokens_grad = d_tokens.astype(jnp.bfloat16)
    qkv_grad = jnp.stack(qkv_grads, axis=2).reshape(rows, 3, -1)
    in_grad = jnp.concatenate(in_grads, axis=2)
    down_grad = jnp.concatenate(down_grads, axis=1)
    qv_grad = jnp.stack(bias_grads, axis=2)[:, places].reshape(2, width)
    sums = links.total(
        jnp.concatenate(
            [
                qv_grad,
                out_bias_grad[None],
                norm1_gain_grad[None],
                norm1_shift_grad[None],
                down_bias_grad[None],
                norm2_gain_grad[None],
                norm2_shift_grad[None],
            ]
        )
    )
    return (
        result.astype(jnp.bfloat16),
        tokens_grad,
        qkv_grad,
        sums[:2],
        out_grad,
        sums[2],
        sums[3],
        sums[4],
        in_grad,
        down_grad,
        sums[5],
        sums[6],
        sums[7],
    )


def solution(mesh):
    rows_all = P(("dp", "tensor"), None)
    return jax.shard_map(
        functools.partial(local, Links(mesh.shape)),
        mesh=mesh,
        in_specs=(
            rows_all,
            P("dp", None, "tensor"),
            P(),
            P("dp", "tensor"),
            P(),
            P(),
            P(),
            P("dp", None, "tensor"),
            P("dp", "tensor"),
            P(),
            P(),
            P(),
            rows_all,
        ),
        out_specs=(
            rows_all,
            rows_all,
            P("dp", None, "tensor"),
            P(),
            P("dp", "tensor"),
            P(),
            P(),
            P(),
            P("dp", None, "tensor"),
            P("dp", "tensor"),
            P(),
            P(),
            P(),
        ),
        check_vma=False,
    )
```

```python
import functools
import math

import jax
import jax.numpy as jnp
from jax import lax
from jax.experimental import pallas as pl
from jax.experimental.pallas import tpu as pltpu
from jax.sharding import PartitionSpec as P

HEAD = 64
SEQ = 1024
GROUP = 4
QB = 256
BLOCKS = 8
LOG2E = 1.4426950408889634
INV_ROOT_HEAD = 1.0 / math.sqrt(HEAD)
SCALE = LOG2E * INV_ROOT_HEAD
NORM_EPS = 1e-12
INV_ROOT_TWO = 0.7071067811865476
INV_ROOT_TWO_PI = 0.3989422804014327
FF_CHUNKS = 3
NT = (((1,), (1,)), ((), ()))
NN = (((1,), (0,)), ((), ()))
BF16 = jnp.bfloat16
F32 = jnp.float32


def mm(left, right, dims=NN):
    return lax.dot_general(left, right, dims, preferred_element_type=F32)


def params(**more):
    return pltpu.CompilerParams(vmem_limit_bytes=56 << 20, **more)


def cost(flops, nbytes, exps=0):
    return pl.CostEstimate(flops=flops, bytes_accessed=nbytes, transcendentals=exps)


SMEM = pl.BlockSpec(memory_space=pltpu.SMEM)


def whole(*shape):
    return pl.BlockSpec(shape, lambda *_: (0,) * len(shape))


def shaped(dtype, *shape):
    return jax.ShapeDtypeStruct(shape, dtype)


def assemble(place_ref, piece_refs, full_ref):
    rows = piece_refs[0].shape[0]
    for k, piece_ref in enumerate(piece_refs):
        start = pl.multiple_of(place_ref[k] * rows, rows)
        full_ref[pl.ds(start, rows), :] = piece_ref[...]


def deal(place_ref, full_ref, even_ref, odd_ref):
    rows = full_ref.shape[0] // BLOCKS
    for k in range(BLOCKS):
        start = pl.multiple_of(place_ref[k] * rows, rows)
        target = odd_ref if k % 2 else even_ref
        target[k // 2] = full_ref[pl.ds(start, rows), :]


def fill_row_distance(dist_ref):
    row = lax.broadcasted_iota(jnp.int32, dist_ref.shape, 0)
    col = lax.broadcasted_iota(jnp.int32, dist_ref.shape, 1)
    dist_ref[...] = jnp.abs(row - col + (SEQ - QB)).astype(F32) * LOG2E


def fill_distance(dist_ref):
    row = lax.broadcasted_iota(jnp.int32, dist_ref.shape, 0)
    col = lax.broadcasted_iota(jnp.int32, dist_ref.shape, 1)
    dist_ref[...] = jnp.abs(row - col - (SEQ - QB)).astype(F32) * LOG2E


def attend_kernel(base, place_ref, slope_ref, x_ref, bias_ref, *rest):
    piece_refs = rest[:BLOCKS]
    qkv_ref, ctx_ref, lse_ref, full_ref, dist_ref = rest[BLOCKS:]
    width = GROUP * HEAD
    assemble(place_ref, piece_refs, full_ref)
    fill_row_distance(dist_ref)
    for block in range(SEQ // QB):
        rows = slice(block * QB, (block + 1) * QB)
        qkv_ref[rows, :] = (mm(x_ref[rows, :], full_ref[...]) + bias_ref[...]).astype(BF16)
    lane = lax.broadcasted_iota(jnp.int32, (1, 128), 1)
    for pair in range(GROUP // 2):
        keys = qkv_ref[:, width + 128 * pair : width + 128 * pair + 128]
        values = qkv_ref[:, 2 * width + 128 * pair : 2 * width + 128 * pair + 128]
        for block in range(SEQ // QB):
            rows = slice(block * QB, (block + 1) * QB)
            start = SEQ - QB - block * QB
            q = qkv_ref[rows, 128 * pair : 128 * pair + 128]
            parts = []
            stats = []
            for side in range(2):
                own = (lane < HEAD) if side == 0 else (lane >= HEAD)
                slope = slope_ref[base + 2 * pair + side]
                s = mm(jnp.where(own, q, jnp.zeros_like(q)), keys, NT) * SCALE
                s = s - slope * dist_ref[:, start : start + SEQ]
                top = jnp.max(s, axis=1, keepdims=True)
                w = jnp.exp2(s - top)
                total = jnp.sum(w, axis=1, keepdims=True)
                p = (w * (1.0 / total)).astype(BF16)
                parts.append(mm(p, values))
                stats.append(top + jnp.log2(total))
            ctx = jnp.where(lane < HEAD, parts[0], parts[1])
            ctx_ref[rows, 128 * pair : 128 * pair + 128] = ctx.astype(BF16)
            flipped = jnp.where(lane < HEAD, stats[0], stats[1]).T
            lse_ref[2 * pair : 2 * pair + 1, rows] = flipped[0:1, :]
            lse_ref[2 * pair + 1 : 2 * pair + 2, rows] = flipped[HEAD : HEAD + 1, :]


def attend_forward(group, place, slopes, x, bias, pieces):
    width = GROUP * HEAD
    depth = x.shape[1]
    return pl.pallas_call(
        functools.partial(attend_kernel, group * GROUP),
        grid=(1,),
        in_specs=[SMEM, SMEM, whole(SEQ, depth), whole(1, 3 * width)]
        + [whole(depth // BLOCKS, 3 * width)] * BLOCKS,
        out_specs=[whole(SEQ, 3 * width), whole(SEQ, width), whole(GROUP, SEQ)],
        out_shape=[
            shaped(BF16, SEQ, 3 * width),
            shaped(BF16, SEQ, width),
            shaped(F32, GROUP, SEQ),
        ],
        scratch_shapes=[
            pltpu.VMEM((depth, 3 * width), BF16),
            pltpu.VMEM((QB, 2 * SEQ - QB), F32),
        ],
        compiler_params=params(),
        cost_estimate=cost(13_000_000_000, 8 << 20, 4 << 20),
        name="attend_forward",
    )(place, slopes, x, bias, *pieces)


def attend_back_kernel(
    base, last, place_ref, slope_ref, qkv_ref, lse_ref, dctx_ref, x_t_ref, acc_in_ref, *rest
):
    piece_refs = rest[:BLOCKS]
    (even_ref, odd_ref, sums_ref, acc_out_ref, full_ref, dist_ref, acc_ref, dqt_ref, dqkv_ref) = rest[
        BLOCKS:
    ]
    width = GROUP * HEAD
    fill_distance(dist_ref)
    assemble(place_ref, piece_refs, full_ref)
    lane = lax.broadcasted_iota(jnp.int32, (1, 128), 1)
    for pair in range(GROUP // 2):
        cols = slice(128 * pair, 128 * pair + 128)
        keys = qkv_ref[:, width + 128 * pair : width + 128 * pair + 128]
        values = qkv_ref[:, 2 * width + 128 * pair : 2 * width + 128 * pair + 128]
        keys_t = keys.T
        for side in range(2):
            own = (lane < HEAD) if side == 0 else (lane >= HEAD)
            own_rows = slice(HEAD * side, HEAD * side + HEAD)
            slope = slope_ref[base + 2 * pair + side]
            for block in range(SEQ // QB):
                rows = slice(block * QB, (block + 1) * QB)
                start = SEQ - QB - block * QB
                q = qkv_ref[rows, cols]
                q = jnp.where(own, q, jnp.zeros_like(q))
                do = dctx_ref[rows, cols]
                do = jnp.where(own, do, jnp.zeros_like(do))
                s = mm(keys, q, NT) * SCALE
                s = s - slope * dist_ref[start : start + SEQ, :]
                p = jnp.exp2(s - lse_ref[2 * pair + side : 2 * pair + side + 1, rows])
                dp = mm(values, do, NT)
                inner = jnp.sum(p * dp, axis=0, keepdims=True)
                ds = (p * (dp - inner)).astype(BF16)
                p = p.astype(BF16)
                dv = mm(p, do)
                dk = mm(ds, q)
                if block == 0 and side == 0:
                    acc_ref[:, 0:128] = dk
                    acc_ref[:, 128:256] = dv
                else:
                    acc_ref[:, 0:128] += dk
                    acc_ref[:, 128:256] += dv
                dqt_ref[own_rows, rows] = mm(keys_t[own_rows], ds)
        dq = dqt_ref[...].T * INV_ROOT_HEAD
        dk = acc_ref[:, 0:128] * INV_ROOT_HEAD
        dv = acc_ref[:, 128:256]
        dqkv_ref[:, 128 * pair : 128 * pair + 128] = dq.astype(BF16)
        dqkv_ref[:, width + 128 * pair : width + 128 * pair + 128] = dk.astype(BF16)
        dqkv_ref[:, 2 * width + 128 * pair : 2 * width + 128 * pair + 128] = dv.astype(BF16)
        sums_ref[0:1, cols] = jnp.sum(dq, axis=0, keepdims=True)
        sums_ref[1:2, cols] = jnp.sum(dv, axis=0, keepdims=True)
    for block in range(SEQ // QB):
        rows = slice(block * QB, (block + 1) * QB)
        d_rows = acc_in_ref[rows, :] + mm(dqkv_ref[rows, :], full_ref[...], NT)
        acc_out_ref[rows, :] = d_rows.astype(acc_out_ref.dtype)
    full_ref[...] = mm(x_t_ref[...], dqkv_ref[...]).astype(BF16)
    deal(place_ref, full_ref, even_ref, odd_ref)


def attend_backward(group, last, place, slopes, qkv, lse, d_context, x_t, d_tokens, pieces):
    width = GROUP * HEAD
    depth = x_t.shape[0]
    rows = depth // BLOCKS
    return pl.pallas_call(
        functools.partial(attend_back_kernel, group * GROUP, last),
        grid=(1,),
        in_specs=[
            SMEM,
            SMEM,
            whole(SEQ, 3 * width),
            whole(GROUP, SEQ),
            pl.BlockSpec((SEQ, width), lambda _: (0, group)),
            whole(depth, SEQ),
            whole(SEQ, depth),
        ]
        + [whole(rows, 3 * width)] * BLOCKS,
        out_specs=[
            whole(BLOCKS // 2, rows, 3 * width),
            whole(BLOCKS // 2, rows, 3 * width),
            whole(2, width),
            whole(SEQ, depth),
        ],
        out_shape=[
            shaped(BF16, BLOCKS // 2, rows, 3 * width),
            shaped(BF16, BLOCKS // 2, rows, 3 * width),
            shaped(F32, 2, width),
            shaped(BF16 if last else F32, SEQ, depth),
        ],
        scratch_shapes=[
            pltpu.VMEM((depth, 3 * width), BF16),
            pltpu.VMEM((2 * SEQ - QB, QB), F32),
            pltpu.VMEM((SEQ, 256), F32),
            pltpu.VMEM((128, SEQ), F32),
            pltpu.VMEM((SEQ, 3 * width), BF16),
        ],
        compiler_params=params(),
        cost_estimate=cost(19_000_000_000, 8 << 20, 4 << 20),
        name="attend_backward",
    )(place, slopes, qkv, lse, d_context, x_t, d_tokens, *pieces)


def row_mean(value):
    return jnp.mean(value, axis=1, keepdims=True)


def normalize(resid):
    center = resid - row_mean(resid)
    inverse = lax.rsqrt(row_mean(center * center) + NORM_EPS)
    return center * inverse, inverse


def norm_pull(grad_rows, normed, inverse, gain):
    scaled = grad_rows * gain
    return inverse * (scaled - row_mean(scaled) - normed * row_mean(scaled * normed))


def add_sums(sums_ref, values, first):
    for place, value in enumerate(values):
        row = jnp.sum(value, axis=0, keepdims=True)
        if first:
            sums_ref[place : place + 1, :] = row
        else:
            sums_ref[place : place + 1, :] += row


def join_kernel(place_ref, x_ref, vec_ref, *rest):
    ctx_refs = rest[:3]
    piece_refs = rest[3 : 3 + BLOCKS]
    normed_ref, inverse_ref, low_ref, low_t_ref, full_ref = rest[3 + BLOCKS :]
    assemble(place_ref, piece_refs, full_ref)
    width = ctx_refs[0].shape[1]
    for block in range(SEQ // QB):
        rows = slice(block * QB, (block + 1) * QB)
        total = x_ref[rows, :].astype(F32) + vec_ref[0:1, :]
        for g, ctx_ref in enumerate(ctx_refs):
            total += mm(ctx_ref[rows, :], full_ref[:, g * width : (g + 1) * width], NT)
        normed, inverse = normalize(total)
        normed_ref[rows, :] = normed
        inverse_ref[rows, :] = jnp.broadcast_to(inverse, (QB, 128))
        low = normed * vec_ref[1:2, :] + vec_ref[2:3, :]
        low_ref[rows, :] = low.astype(BF16)
        low_t_ref[:, rows] = low.T.astype(BF16)


def join(place, x, vec, ctx, pieces):
    depth = x.shape[1]
    rows = depth // BLOCKS
    return pl.pallas_call(
        join_kernel,
        grid=(1,),
        in_specs=[SMEM, whole(SEQ, depth), whole(8, depth)]
        + [whole(SEQ, ctx[0].shape[1])] * 3
        + [whole(rows, depth)] * BLOCKS,
        out_specs=[whole(SEQ, depth), whole(SEQ, 128), whole(SEQ, depth), whole(depth, SEQ)],
        out_shape=[
            shaped(F32, SEQ, depth),
            shaped(F32, SEQ, 128),
            shaped(BF16, SEQ, depth),
            shaped(BF16, depth, SEQ),
        ],
        scratch_shapes=[pltpu.VMEM((depth, depth), BF16)],
        compiler_params=params(),
        cost_estimate=cost(4_000_000_000, 10 << 20),
        name="join",
    )(place, x, vec, *ctx, *pieces)


def turn_kernel(ffn_ref, normed1_ref, cot_ref, vec_ref, out_ref, d_ref, low_ref, low_t_ref, sums_ref):
    for block in range(SEQ // QB):
        rows = slice(block * QB, (block + 1) * QB)
        hidden = normed1_ref[rows, :] * vec_ref[1:2, :] + vec_ref[2:3, :]
        normed, inverse = normalize(hidden + ffn_ref[rows, :] + vec_ref[3:4, :])
        out_ref[rows, :] = (normed * vec_ref[4:5, :] + vec_ref[5:6, :]).astype(BF16)
        grad = cot_ref[rows, :].astype(F32)
        d_resid = norm_pull(grad, normed, inverse, vec_ref[4:5, :])
        d_ref[rows, :] = d_resid
        low_ref[rows, :] = d_resid.astype(BF16)
        low_t_ref[:, rows] = d_resid.T.astype(BF16)
        add_sums(sums_ref, (grad * normed, grad, d_resid), block == 0)


def turn(ffn, normed1, cot, vec):
    depth = cot.shape[1]
    return pl.pallas_call(
        turn_kernel,
        grid=(1,),
        in_specs=[whole(SEQ, depth)] * 3 + [whole(8, depth)],
        out_specs=[whole(SEQ, depth)] * 3 + [whole(depth, SEQ), whole(3, depth)],
        out_shape=[
            shaped(BF16, SEQ, depth),
            shaped(F32, SEQ, depth),
            shaped(BF16, SEQ, depth),
            shaped(BF16, depth, SEQ),
            shaped(F32, 3, depth),
        ],
        compiler_params=params(),
        cost_estimate=cost(4_000_000_000, 16 << 20),
        name="turn",
    )(ffn, normed1, cot, vec)


def rejoin_kernel(place_ref, d_hidden_ref, normed_ref, inverse_ref, vec_ref, *rest):
    ctx_refs = rest[:3]
    piece_refs = rest[3 : 3 + BLOCKS]
    d_ref, dctx_ref, even_ref, odd_ref, sums_ref, full_ref, low_t_ref = rest[3 + BLOCKS :]
    width = ctx_refs[0].shape[1]
    assemble(place_ref, piece_refs, full_ref)
    for block in range(SEQ // QB):
        rows = slice(block * QB, (block + 1) * QB)
        normed = normed_ref[rows, :]
        grad = d_hidden_ref[rows, :]
        d_resid = norm_pull(grad, normed, inverse_ref[rows, 0:1], vec_ref[1:2, :])
        d_ref[rows, :] = d_resid
        low = d_resid.astype(BF16)
        low_t_ref[:, rows] = d_resid.T.astype(BF16)
        dctx_ref[rows, :] = mm(low, full_ref[...]).astype(BF16)
        add_sums(sums_ref, (grad * normed, grad, d_resid), block == 0)
    for g, ctx_ref in enumerate(ctx_refs):
        full_ref[:, g * width : (g + 1) * width] = mm(low_t_ref[...], ctx_ref[...]).astype(BF16)
    deal(place_ref, full_ref, even_ref, odd_ref)


def rejoin(place, d_hidden, normed, inverse, vec, ctx, pieces):
    depth = d_hidden.shape[1]
    rows = depth // BLOCKS
    return pl.pallas_call(
        rejoin_kernel,
        grid=(1,),
        in_specs=[SMEM, whole(SEQ, depth), whole(SEQ, depth), whole(SEQ, 128), whole(8, depth)]
        + [whole(SEQ, ctx[0].shape[1])] * 3
        + [whole(rows, depth)] * BLOCKS,
        out_specs=[
            whole(SEQ, depth),
            whole(SEQ, depth),
            whole(BLOCKS // 2, rows, depth),
            whole(BLOCKS // 2, rows, depth),
            whole(3, depth),
        ],
        out_shape=[
            shaped(F32, SEQ, depth),
            shaped(BF16, SEQ, depth),
            shaped(BF16, BLOCKS // 2, rows, depth),
            shaped(BF16, BLOCKS // 2, rows, depth),
            shaped(F32, 3, depth),
        ],
        scratch_shapes=[pltpu.VMEM((depth, depth), BF16), pltpu.VMEM((depth, SEQ), BF16)],
        compiler_params=params(),
        cost_estimate=cost(6_000_000_000, 14 << 20),
        name="rejoin",
    )(place, d_hidden, normed, inverse, vec, *ctx, *pieces)


def gelu_parts(gate):
    normal_cdf = 0.5 * (1.0 + lax.erf(gate * INV_ROOT_TWO))
    density = jnp.exp(-0.5 * gate * gate) * INV_ROOT_TWO_PI
    return gate * normal_cdf, normal_cdf + gate * density


def feed_kernel(first, place_ref, low_ref, *rest):
    if not first:
        acc_in_ref, *rest = rest
    piece_refs = rest[:BLOCKS]
    acc_ref, gated_ref, slope_ref, active_ref, full_ref = rest[BLOCKS:]
    part = gated_ref.shape[1]
    assemble(place_ref, piece_refs, full_ref)
    step = pl.program_id(0)
    for block in range(SEQ // QB):
        rows = slice(block * QB, (block + 1) * QB)
        both = mm(low_ref[rows, :], full_ref[:, : 2 * part])
        up = both[:, part:]
        active, slope = gelu_parts(both[:, :part])
        gated = (active * up).astype(BF16)
        gated_ref[rows, :] = gated
        slope_ref[rows, :] = (slope * up).astype(BF16)
        active_ref[rows, :] = active.astype(BF16)
        more = mm(gated, full_ref[:, 2 * part :], NT)

        @pl.when(step == 0)
        def _():
            acc_ref[rows, :] = more if first else acc_in_ref[rows, :] + more

        @pl.when(step > 0)
        def _():
            acc_ref[rows, :] += more


def feed(place, low, acc, pieces):
    depth = low.shape[1]
    steps, rows, lanes = pieces[0].shape
    part = lanes // 3
    columns = pl.BlockSpec((SEQ, part), lambda m: (0, m))
    first = acc is None
    return pl.pallas_call(
        functools.partial(feed_kernel, first),
        grid=(steps,),
        in_specs=[SMEM, whole(SEQ, depth)]
        + ([] if first else [whole(SEQ, depth)])
        + [pl.BlockSpec((None, rows, lanes), lambda m: (m, 0, 0))] * BLOCKS,
        out_specs=[whole(SEQ, depth), columns, columns, columns],
        out_shape=[shaped(F32, SEQ, depth)] + [shaped(BF16, SEQ, steps * part)] * 3,
        scratch_shapes=[pltpu.VMEM((depth, lanes), BF16)],
        compiler_params=params(),
        cost_estimate=cost(10_000_000_000, 16 << 20),
        name="feed",
    )(place, low, *([] if first else [acc]), *pieces)


def feed_back_kernel(
    place_ref, d_ref, d_t_ref, low_t_ref, acc_in_ref, gated_ref, slope_ref, active_ref, *rest
):
    piece_refs = rest[:BLOCKS]
    acc_ref, even_ref, odd_ref, full_ref, gate_up_ref = rest[BLOCKS:]
    part = gated_ref.shape[1]
    assemble(place_ref, piece_refs, full_ref)
    step = pl.program_id(0)
    for block in range(SEQ // QB):
        rows = slice(block * QB, (block + 1) * QB)
        d_gated = mm(d_ref[rows, :], full_ref[:, 2 * part :])
        gate_up_ref[rows, :part] = (d_gated * slope_ref[rows, :].astype(F32)).astype(BF16)
        gate_up_ref[rows, part:] = (d_gated * active_ref[rows, :].astype(F32)).astype(BF16)
        more = mm(gate_up_ref[rows, :], full_ref[:, : 2 * part], NT)

        @pl.when(step == 0)
        def _():
            acc_ref[rows, :] = acc_in_ref[rows, :] + more

        @pl.when(step > 0)
        def _():
            acc_ref[rows, :] += more

    full_ref[:, : 2 * part] = mm(low_t_ref[...], gate_up_ref[...]).astype(BF16)
    full_ref[:, 2 * part :] = mm(d_t_ref[...], gated_ref[...]).astype(BF16)
    deal(place_ref, full_ref, even_ref, odd_ref)


def feed_back(place, d_low, d_low_t, low_t, acc, gated, slope, active, pieces):
    depth = d_low.shape[1]
    steps, rows, lanes = pieces[0].shape
    part = lanes // 3
    columns = pl.BlockSpec((SEQ, part), lambda m: (0, m))
    dealt = pl.BlockSpec((BLOCKS // 2, None, rows, lanes), lambda m: (0, m, 0, 0))
    return pl.pallas_call(
        feed_back_kernel,
        grid=(steps,),
        in_specs=[SMEM, whole(SEQ, depth), whole(depth, SEQ), whole(depth, SEQ), whole(SEQ, depth)]
        + [columns] * 3
        + [pl.BlockSpec((None, rows, lanes), lambda m: (m, 0, 0))] * BLOCKS,
        out_specs=[whole(SEQ, depth), dealt, dealt],
        out_shape=[shaped(F32, SEQ, depth)] + [shaped(BF16, BLOCKS // 2, steps, rows, lanes)] * 2,
        scratch_shapes=[pltpu.VMEM((depth, lanes), BF16), pltpu.VMEM((SEQ, 2 * part), BF16)],
        compiler_params=params(),
        cost_estimate=cost(12_000_000_000, 30 << 20),
        name="feed_back",
    )(place, d_low, d_low_t, low_t, acc, gated, slope, active, *pieces)


class Links:
    def __init__(self, mesh_shape):
        self.dp = mesh_shape["dp"]
        self.tensor = mesh_shape["tensor"]
        self.paired = self.dp == 8 and self.tensor == 4

    def swap(self, value, axis, bit):
        size = self.dp if axis == "dp" else self.tensor
        return lax.ppermute(value, axis, [(i, i ^ bit) for i in range(size)])

    def tensor_order(self):
        if self.paired:
            return jnp.array([0, 2, 1, 3], jnp.int32) ^ lax.axis_index("tensor")
        return jnp.arange(self.tensor, dtype=jnp.int32)

    def tensor_places(self):
        index = jnp.arange(self.tensor, dtype=jnp.int32)
        if self.paired:
            index = index ^ lax.axis_index("tensor")
            return (index & 1) * 2 + (index >> 1)
        return index

    def row_order(self):
        blocks = jnp.arange(BLOCKS, dtype=jnp.int32)
        return blocks ^ lax.axis_index("dp") if self.paired else blocks

    def spread(self, value, bits):
        if not self.paired:
            gathered = lax.all_gather(value, "dp", axis=value.ndim - 2, tiled=True)
            return jnp.split(gathered, BLOCKS, axis=value.ndim - 2)
        held = {0: value}
        for bit in bits:
            for place in list(held):
                held[place | bit] = self.swap(held[place], "dp", bit)
        return [held[place] for place in range(BLOCKS)]

    def columns_of_heads(self, piece):
        rows, lanes = piece.shape
        if not self.paired:
            gathered = lax.all_gather(piece.reshape(rows, lanes // HEAD, 1, HEAD), "tensor", axis=2, tiled=True)
            return gathered.reshape(rows, -1)
        far = self.swap(piece, "tensor", 2)
        pair = jnp.concatenate(
            [part[:, i : i + HEAD] for i in range(0, lanes, HEAD) for part in (piece, far)], axis=1
        )
        near = self.swap(pair, "tensor", 1)
        return jnp.concatenate(
            [part[:, i : i + 128] for i in range(0, 2 * lanes, 128) for part in (pair, near)], axis=1
        )

    def columns_of_units(self, piece):
        if not self.paired:
            return lax.all_gather(piece, "tensor", axis=0)
        pair = jnp.stack([piece, self.swap(piece, "tensor", 2)])
        return jnp.concatenate([pair, self.swap(pair, "tensor", 1)])

    def sum_rows(self, even, odd, x_first):
        if not self.paired:
            whole_rows = jnp.stack([even, odd], axis=1)
            whole_rows = whole_rows.reshape((BLOCKS,) + even.shape[1:]).astype(F32)
            whole_rows = jnp.moveaxis(whole_rows, 0, -3)
            whole_rows = whole_rows.reshape(whole_rows.shape[:-3] + (-1, whole_rows.shape[-1]))
            return lax.psum_scatter(
                whole_rows, "dp", scatter_dimension=whole_rows.ndim - 2, tiled=True
            )
        arrived = self.swap(odd, "dp", 1)
        first, second = (2, 4) if x_first else (4, 2)
        out = (1, 3) if x_first else (2, 3)
        stay = (0, 2) if x_first else (0, 1)
        sent = add_low(
            jnp.stack([even[i] for i in out]), jnp.stack([arrived[i] for i in out])
        )
        mine = add_low(
            jnp.stack([even[i] for i in stay]), jnp.stack([arrived[i] for i in stay])
        )
        arrived = self.swap(sent, "dp", first)
        sent = add_low(mine[1], arrived[1])
        mine = add_low(mine[0], arrived[0])
        return add_low(mine, self.swap(sent, "dp", second))

    def sum_units(self, mine):
        if not self.paired:
            return lax.psum_scatter(mine, "tensor", scatter_dimension=0, tiled=False)
        arrived = self.swap(mine[2:], "tensor", 1)
        sent = add_low(mine[1], arrived[1])
        mine = add_low(mine[0], arrived[0])
        return mine.astype(F32) + self.swap(sent, "tensor", 2).astype(F32)

    def sum_heads(self, mine):
        rows, lanes = mine.shape
        if not self.paired:
            mine = mine.reshape(rows, lanes // 256, 4, HEAD)
            return lax.psum_scatter(mine, "tensor", scatter_dimension=2, tiled=True).reshape(rows, -1)

        def take(value, size, at):
            return jnp.concatenate(
                [value[:, i + at : i + at + size] for i in range(0, value.shape[1], 2 * size)], axis=1
            )

        arrived = self.swap(take(mine, 128, 128), "tensor", 1)
        mine = add_low(take(mine, 128, 0), arrived)
        arrived = self.swap(take(mine, HEAD, HEAD), "tensor", 2)
        return take(mine, HEAD, 0).astype(F32) + arrived.astype(F32)

    def total(self, value):
        if not self.paired:
            return lax.psum(value, ("dp", "tensor"))
        for axis, bit in (("dp", 1), ("dp", 4), ("dp", 2), ("tensor", 1), ("tensor", 2)):
            value = value + self.swap(value, axis, bit)
        return value


def add_low(left, right):
    return (left.astype(F32) + right.astype(F32)).astype(BF16)


def local(
    links,
    tokens,
    qkv_weight,
    qv_bias,
    out_weight,
    out_bias,
    norm1_gain,
    norm1_shift,
    in_weight,
    down_weight,
    down_bias,
    norm2_gain,
    norm2_shift,
    cotangent,
):
    depth = tokens.shape[1]
    rows = qkv_weight.shape[0]
    n_tensor = links.tensor
    groups = qkv_weight.shape[2] // HEAD
    part = in_weight.shape[2] // FF_CHUNKS
    place = links.row_order()

    heads = [
        qkv_weight[:, c, g * HEAD : (g + 1) * HEAD] for g in range(groups) for c in range(3)
    ]
    columns = links.columns_of_heads(jnp.concatenate(heads + [out_weight], axis=1))
    pieces = [columns[:, i * depth : (i + 1) * depth] for i in range(groups + 1)]
    qkv_pieces = [links.spread(pieces[g], (4, 2, 1) if g % 2 else (2, 4, 1)) for g in range(groups)]
    out_pieces = links.spread(pieces[groups], (4, 2, 1))
    ff_pieces = []
    for c in range(FF_CHUNKS):
        cols = slice(c * part, (c + 1) * part)
        piece = jnp.concatenate(
            [in_weight[:, 0, cols], in_weight[:, 1, cols], down_weight[:, cols]], axis=1
        )
        ff_pieces.append(
            links.spread(links.columns_of_units(piece), (4, 2, 1) if c % 2 else (2, 4, 1))
        )

    order = links.tensor_order()
    head_ids = (order[None, :] * groups + jnp.arange(groups, dtype=jnp.int32)[:, None]).reshape(-1)
    powers = jnp.where(head_ids < 8, -(head_ids + 1).astype(F32), 7.5 - head_ids.astype(F32))
    slopes = jnp.exp2(powers)
    bias = qv_bias.reshape(2, n_tensor, groups, HEAD)[:, order].transpose(2, 0, 1, 3)
    bias = bias.reshape(groups, 2, n_tensor * HEAD)
    bias = jnp.concatenate([bias[:, 0], jnp.zeros_like(bias[:, 0]), bias[:, 1]], axis=1)
    vec = jnp.stack(
        [out_bias, norm1_gain, norm1_shift, down_bias, norm2_gain, norm2_shift, out_bias, out_bias]
    )
    tokens_t = tokens.T

    qkv, ctx, lse = [], [], []
    for g in range(groups):
        got = attend_forward(g, place, slopes, tokens, bias[g : g + 1], qkv_pieces[g])
        qkv.append(got[0])
        ctx.append(got[1])
        lse.append(got[2])
    normed1, inverse1, low, low_t = join(place, tokens, vec, ctx, out_pieces)
    acc = None
    kept = []
    for c in range(FF_CHUNKS):
        acc, *saved = feed(place, low, acc, ff_pieces[c])
        kept.append(saved)
    result, d_hidden, d_low, d_low_t, sums2 = turn(acc, normed1, cotangent, vec)

    ff_grads = []
    for c in range(FF_CHUNKS):
        d_hidden, even, odd = feed_back(
            place, d_low, d_low_t, low_t, d_hidden, *kept[c], ff_pieces[c]
        )
        ff_grads.append(links.sum_units(links.sum_rows(even, odd, c % 2 == 0)))
    d_tokens, d_context, even, odd, sums1 = rejoin(
        place, d_hidden, normed1, inverse1, vec, ctx, out_pieces
    )
    out_grad = links.sum_heads(links.sum_rows(even, odd, True))
    qkv_grads = []
    bias_grads = []
    for g in range(groups):
        even, odd, sums, d_tokens = attend_backward(
            g,
            g == groups - 1,
            place,
            slopes,
            qkv[g],
            lse[g],
            d_context,
            tokens_t,
            d_tokens,
            qkv_pieces[g],
        )
        qkv_grads.append(links.sum_heads(links.sum_rows(even, odd, g % 2 == 0)).reshape(rows, 3, HEAD))
        bias_grads.append(sums.reshape(2, n_tensor, HEAD))
    qkv_grad = jnp.concatenate(qkv_grads, axis=2)
    in_grad = jnp.stack(
        [
            jnp.concatenate([g[:, i * part : (i + 1) * part] for g in ff_grads], axis=1)
            for i in range(2)
        ],
        axis=1,
    )
    down_grad = jnp.concatenate([g[:, 2 * part :] for g in ff_grads], axis=1)
    back = links.tensor_places()
    qv_grad = jnp.stack(bias_grads, axis=2)[:, back].reshape(2, depth)
    sums = links.total(jnp.concatenate([qv_grad, sums1, sums2]))
    return (
        result,
        d_tokens,
        qkv_grad,
        sums[:2],
        out_grad,
        sums[4],
        sums[2],
        sums[3],
        in_grad,
        down_grad,
        sums[7],
        sums[5],
        sums[6],
    )


def solution(mesh):
    rows_all = P(("dp", "tensor"), None)
    columns_3d = P("dp", None, "tensor")
    columns_2d = P("dp", "tensor")
    return jax.shard_map(
        functools.partial(local, Links(mesh.shape)),
        mesh=mesh,
        in_specs=(
            rows_all,
            columns_3d,
            P(),
            columns_2d,
            P(),
            P(),
            P(),
            columns_3d,
            columns_2d,
            P(),
            P(),
            P(),
            rows_all,
        ),
        out_specs=(
            rows_all,
            rows_all,
            columns_3d,
            P(),
            columns_2d,
            P(),
            P(),
            P(),
            columns_3d,
            columns_2d,
            P(),
            P(),
            P(),
        ),
        check_vma=False,
    )
```

```python
import functools
import math

import jax
import jax.numpy as jnp
from jax import lax
from jax.experimental import pallas as pl
from jax.experimental.pallas import tpu as pltpu
from jax.sharding import PartitionSpec as P

HEAD = 64
SEQ = 1024
GROUP = 4
QB = 256
AB = 512
FEED_ROWS = 1024
BLOCKS = 8
LOG2E = 1.4426950408889634
INV_ROOT_HEAD = 1.0 / math.sqrt(HEAD)
SCALE = LOG2E * INV_ROOT_HEAD
NORM_EPS = 1e-12
INV_ROOT_TWO = 0.7071067811865476
INV_ROOT_TWO_PI = 0.3989422804014327
FF_CHUNKS = 3
NT = (((1,), (1,)), ((), ()))
NN = (((1,), (0,)), ((), ()))
BF16 = jnp.bfloat16
F32 = jnp.float32


def mm(left, right, dims=NN):
    return lax.dot_general(left, right, dims, preferred_element_type=F32)


def params(**more):
    return pltpu.CompilerParams(vmem_limit_bytes=56 << 20, **more)


BRIEF = pl.CostEstimate(flops=1 << 20, bytes_accessed=1 << 16, transcendentals=0)


SMEM = pl.BlockSpec(memory_space=pltpu.SMEM)


def whole(*shape):
    return pl.BlockSpec(shape, lambda *_: (0,) * len(shape))


def shaped(dtype, *shape):
    return jax.ShapeDtypeStruct(shape, dtype)


def assemble(place_ref, piece_refs, full_ref):
    at = 0
    for piece_ref in piece_refs:
        for i in range(piece_ref.shape[0]):
            rows = piece_ref.shape[1]
            start = pl.multiple_of(place_ref[at] * rows, rows)
            full_ref[pl.ds(start, rows), :] = piece_ref[i]
            at += 1


def deal(place_ref, full_ref, even_ref, odd_ref):
    rows = full_ref.shape[0] // BLOCKS
    for at in range(BLOCKS):
        start = pl.multiple_of(place_ref[at] * rows, rows)
        target = odd_ref if at >= BLOCKS // 2 else even_ref
        target[at % (BLOCKS // 2)] = full_ref[pl.ds(start, rows), :]


def piece_specs(pieces):
    arrays, column = pieces
    specs = []
    for array in arrays:
        if column is None:
            specs.append(whole(*array.shape))
        else:
            count, _, rows, lanes = array.shape
            at = (lambda m: (0, m, 0, 0)) if column == "grid" else (lambda _: (0, column, 0, 0))
            specs.append(pl.BlockSpec((count, None, rows, lanes), at))
    return specs


def fill_row_distance(dist_ref):
    row = lax.broadcasted_iota(jnp.int32, dist_ref.shape, 0)
    col = lax.broadcasted_iota(jnp.int32, dist_ref.shape, 1)
    dist_ref[...] = jnp.abs(row - col + (SEQ - AB)).astype(F32) * LOG2E


def fill_distance(dist_ref):
    row = lax.broadcasted_iota(jnp.int32, dist_ref.shape, 0)
    col = lax.broadcasted_iota(jnp.int32, dist_ref.shape, 1)
    dist_ref[...] = jnp.abs(row - col - (SEQ - AB)).astype(F32) * LOG2E


def attend_kernel(base, count, place_ref, slope_ref, x_ref, bias_ref, *rest):
    piece_refs = rest[:count]
    qkv_ref, ctx_ref, lse_ref, full_ref, dist_ref = rest[count:]
    width = GROUP * HEAD
    assemble(place_ref, piece_refs, full_ref)
    fill_row_distance(dist_ref)
    for block in range(SEQ // AB):
        rows = slice(block * AB, (block + 1) * AB)
        qkv_ref[rows, :] = (mm(x_ref[rows, :], full_ref[...]) + bias_ref[...]).astype(BF16)
    lane = lax.broadcasted_iota(jnp.int32, (1, 128), 1)
    for pair in range(GROUP // 2):
        keys = qkv_ref[:, width + 128 * pair : width + 128 * pair + 128]
        values = qkv_ref[:, 2 * width + 128 * pair : 2 * width + 128 * pair + 128]
        for block in range(SEQ // AB):
            rows = slice(block * AB, (block + 1) * AB)
            start = SEQ - AB - block * AB
            q = qkv_ref[rows, 128 * pair : 128 * pair + 128]
            parts = []
            stats = []
            for side in range(2):
                own = (lane < HEAD) if side == 0 else (lane >= HEAD)
                slope = slope_ref[base + 2 * pair + side]
                s = mm(jnp.where(own, q, jnp.zeros_like(q)), keys, NT) * SCALE
                s = s - slope * dist_ref[:, start : start + SEQ]
                top = jnp.max(s, axis=1, keepdims=True)
                w = jnp.exp2(s - top)
                total = jnp.sum(w, axis=1, keepdims=True)
                p = (w * (1.0 / total)).astype(BF16)
                parts.append(mm(p, values))
                stats.append(top + jnp.log2(total))
            ctx = jnp.where(lane < HEAD, parts[0], parts[1])
            ctx_ref[rows, 128 * pair : 128 * pair + 128] = ctx.astype(BF16)
            flipped = jnp.where(lane < HEAD, stats[0], stats[1]).T
            lse_ref[2 * pair : 2 * pair + 1, rows] = flipped[0:1, :]
            lse_ref[2 * pair + 1 : 2 * pair + 2, rows] = flipped[HEAD : HEAD + 1, :]


def attend_forward(group, place, slopes, x, bias, pieces):
    width = GROUP * HEAD
    depth = x.shape[1]
    return pl.pallas_call(
        functools.partial(attend_kernel, group * GROUP, len(pieces[0])),
        grid=(1,),
        in_specs=[SMEM, SMEM, whole(SEQ, depth), whole(1, 3 * width)]
        + piece_specs(pieces),
        out_specs=[whole(SEQ, 3 * width), whole(SEQ, width), whole(GROUP, SEQ)],
        out_shape=[
            shaped(BF16, SEQ, 3 * width),
            shaped(BF16, SEQ, width),
            shaped(F32, GROUP, SEQ),
        ],
        scratch_shapes=[
            pltpu.VMEM((depth, 3 * width), BF16),
            pltpu.VMEM((AB, 2 * SEQ - AB), F32),
        ],
        compiler_params=params(),
        cost_estimate=BRIEF,
        name="attend_forward",
    )(place, slopes, x, bias, *pieces[0])


def attend_back_pair(pair, slopes, qkv_ref, lse_ref, dctx_ref, dist_ref, acc_ref, dqt_ref, sums_ref):
    width = GROUP * HEAD
    lane = lax.broadcasted_iota(jnp.int32, (1, 128), 1)
    cols = slice(128 * pair, 128 * pair + 128)
    keys = qkv_ref[:, width + 128 * pair : width + 128 * pair + 128]
    values = qkv_ref[:, 2 * width + 128 * pair : 2 * width + 128 * pair + 128]
    keys_t = keys.T
    for side in range(2):
        own = (lane < HEAD) if side == 0 else (lane >= HEAD)
        own_rows = slice(HEAD * side, HEAD * side + HEAD)
        for block in range(SEQ // AB):
            rows = slice(block * AB, (block + 1) * AB)
            start = SEQ - AB - block * AB
            q = qkv_ref[rows, cols]
            q = jnp.where(own, q, jnp.zeros_like(q))
            do = dctx_ref[rows, cols]
            do = jnp.where(own, do, jnp.zeros_like(do))
            s = mm(keys, q, NT) * SCALE
            s = s - slopes[side] * dist_ref[start : start + SEQ, :]
            p = jnp.exp2(s - lse_ref[2 * pair + side : 2 * pair + side + 1, rows])
            dp = mm(values, do, NT)
            inner = jnp.sum(p * dp, axis=0, keepdims=True)
            ds = (p * (dp - inner)).astype(BF16)
            p = p.astype(BF16)
            dv = mm(p, do)
            dk = mm(ds, q)
            if block == 0 and side == 0:
                acc_ref[:, 0:128] = dk
                acc_ref[:, 128:256] = dv
            else:
                acc_ref[:, 0:128] += dk
                acc_ref[:, 128:256] += dv
            dqt_ref[own_rows, rows] = mm(keys_t[own_rows], ds)
    dq = dqt_ref[...].T * INV_ROOT_HEAD
    dk = acc_ref[:, 0:128] * INV_ROOT_HEAD
    dv = acc_ref[:, 128:256]
    sums_ref[0:1, :] = jnp.sum(dq, axis=0, keepdims=True)
    sums_ref[1:2, :] = jnp.sum(dv, axis=0, keepdims=True)
    return dq.astype(BF16), dk.astype(BF16), dv.astype(BF16)


def attend_back_first(
    base, slope_ref, qkv_ref, lse_ref, dctx_ref, dqkv_ref, sums_ref, dist_ref, acc_ref, dqt_ref
):
    fill_distance(dist_ref)
    slopes = [slope_ref[base], slope_ref[base + 1]]
    got = attend_back_pair(
        0, slopes, qkv_ref, lse_ref, dctx_ref, dist_ref, acc_ref, dqt_ref, sums_ref
    )
    for i, value in enumerate(got):
        dqkv_ref[:, 128 * i : 128 * i + 128] = value


def attend_back_second(
    base, count, place_ref, slope_ref, qkv_ref, lse_ref, dctx_ref, x_t_ref, acc_in_ref, pair_ref, *rest
):
    piece_refs = rest[:count]
    (even_ref, odd_ref, sums_ref, acc_out_ref, full_ref, dist_ref, acc_ref, dqt_ref, dqkv_ref) = rest[
        count:
    ]
    width = GROUP * HEAD
    fill_distance(dist_ref)
    assemble(place_ref, piece_refs, full_ref)
    slopes = [slope_ref[base + 2], slope_ref[base + 3]]
    got = attend_back_pair(
        1, slopes, qkv_ref, lse_ref, dctx_ref, dist_ref, acc_ref, dqt_ref, sums_ref
    )
    for i, value in enumerate(got):
        dqkv_ref[:, width * i : width * i + 128] = pair_ref[:, 128 * i : 128 * i + 128]
        dqkv_ref[:, width * i + 128 : width * i + 256] = value
    for block in range(SEQ // AB):
        rows = slice(block * AB, (block + 1) * AB)
        d_rows = acc_in_ref[rows, :] + mm(dqkv_ref[rows, :], full_ref[...], NT)
        acc_out_ref[rows, :] = d_rows.astype(acc_out_ref.dtype)
    full_ref[...] = mm(x_t_ref[...], dqkv_ref[...]).astype(BF16)
    deal(place_ref, full_ref, even_ref, odd_ref)


def attend_scratch():
    return [
        pltpu.VMEM((2 * SEQ - AB, AB), F32),
        pltpu.VMEM((SEQ, 256), F32),
        pltpu.VMEM((128, SEQ), F32),
    ]


def attend_backward_first(group, slopes, qkv, lse, d_context):
    width = GROUP * HEAD
    return pl.pallas_call(
        functools.partial(attend_back_first, group * GROUP),
        grid=(1,),
        in_specs=[
            SMEM,
            whole(SEQ, 3 * width),
            whole(GROUP, SEQ),
            pl.BlockSpec((SEQ, width), lambda _: (0, group)),
        ],
        out_specs=[whole(SEQ, 3 * 128), whole(2, 128)],
        out_shape=[shaped(BF16, SEQ, 3 * 128), shaped(F32, 2, 128)],
        scratch_shapes=attend_scratch(),
        compiler_params=params(),
        cost_estimate=BRIEF,
        name="attend_backward_first",
    )(slopes, qkv, lse, d_context)


def attend_backward_second(
    group, last, place, slopes, qkv, lse, d_context, x_t, d_tokens, pair, pieces
):
    width = GROUP * HEAD
    depth = x_t.shape[0]
    rows = depth // BLOCKS
    return pl.pallas_call(
        functools.partial(attend_back_second, group * GROUP, len(pieces[0])),
        grid=(1,),
        in_specs=[
            SMEM,
            SMEM,
            whole(SEQ, 3 * width),
            whole(GROUP, SEQ),
            pl.BlockSpec((SEQ, width), lambda _: (0, group)),
            whole(depth, SEQ),
            whole(SEQ, depth),
            whole(SEQ, 3 * 128),
        ]
        + piece_specs(pieces),
        out_specs=[
            whole(BLOCKS // 2, rows, 3 * width),
            whole(BLOCKS // 2, rows, 3 * width),
            whole(2, 128),
            whole(SEQ, depth),
        ],
        out_shape=[
            shaped(BF16, BLOCKS // 2, rows, 3 * width),
            shaped(BF16, BLOCKS // 2, rows, 3 * width),
            shaped(F32, 2, 128),
            shaped(BF16 if last else F32, SEQ, depth),
        ],
        scratch_shapes=[pltpu.VMEM((depth, 3 * width), BF16)]
        + attend_scratch()
        + [pltpu.VMEM((SEQ, 3 * width), BF16)],
        compiler_params=params(),
        cost_estimate=BRIEF,
        name="attend_backward_second",
    )(place, slopes, qkv, lse, d_context, x_t, d_tokens, pair, *pieces[0])


def row_mean(value):
    return jnp.mean(value, axis=1, keepdims=True)


def normalize(resid):
    center = resid - row_mean(resid)
    inverse = lax.rsqrt(row_mean(center * center) + NORM_EPS)
    return center * inverse, inverse


def norm_pull(grad_rows, normed, inverse, gain):
    scaled = grad_rows * gain
    return inverse * (scaled - row_mean(scaled) - normed * row_mean(scaled * normed))


def add_sums(sums_ref, values, first):
    for place, value in enumerate(values):
        row = jnp.sum(value, axis=0, keepdims=True)
        if first:
            sums_ref[place : place + 1, :] = row
        else:
            sums_ref[place : place + 1, :] += row


def join_kernel(count, place_ref, x_ref, vec_ref, *rest):
    ctx_refs = rest[:3]
    piece_refs = rest[3 : 3 + count]
    normed_ref, inverse_ref, low_ref, low_t_ref, full_ref = rest[3 + count :]
    assemble(place_ref, piece_refs, full_ref)
    width = ctx_refs[0].shape[1]
    for block in range(SEQ // QB):
        rows = slice(block * QB, (block + 1) * QB)
        total = x_ref[rows, :].astype(F32) + vec_ref[0:1, :]
        for g, ctx_ref in enumerate(ctx_refs):
            total += mm(ctx_ref[rows, :], full_ref[:, g * width : (g + 1) * width], NT)
        normed, inverse = normalize(total)
        normed_ref[rows, :] = normed
        inverse_ref[rows, :] = jnp.broadcast_to(inverse, (QB, 128))
        low = normed * vec_ref[1:2, :] + vec_ref[2:3, :]
        low_ref[rows, :] = low.astype(BF16)
        low_t_ref[:, rows] = low.astype(BF16).T


def join(place, x, vec, ctx, pieces):
    depth = x.shape[1]
    rows = depth // BLOCKS
    return pl.pallas_call(
        functools.partial(join_kernel, len(pieces[0])),
        grid=(1,),
        in_specs=[SMEM, whole(SEQ, depth), whole(8, depth)]
        + [whole(SEQ, ctx[0].shape[1])] * 3
        + piece_specs(pieces),
        out_specs=[whole(SEQ, depth), whole(SEQ, 128), whole(SEQ, depth), whole(depth, SEQ)],
        out_shape=[
            shaped(F32, SEQ, depth),
            shaped(F32, SEQ, 128),
            shaped(BF16, SEQ, depth),
            shaped(BF16, depth, SEQ),
        ],
        scratch_shapes=[pltpu.VMEM((depth, depth), BF16)],
        compiler_params=params(),
        cost_estimate=BRIEF,
        name="join",
    )(place, x, vec, *ctx, *pieces[0])


def turn_kernel(ffn_ref, normed1_ref, cot_ref, vec_ref, out_ref, d_ref, low_ref, low_t_ref, sums_ref):
    for block in range(SEQ // QB):
        rows = slice(block * QB, (block + 1) * QB)
        hidden = normed1_ref[rows, :] * vec_ref[1:2, :] + vec_ref[2:3, :]
        normed, inverse = normalize(hidden + ffn_ref[rows, :] + vec_ref[3:4, :])
        out_ref[rows, :] = (normed * vec_ref[4:5, :] + vec_ref[5:6, :]).astype(BF16)
        grad = cot_ref[rows, :].astype(F32)
        d_resid = norm_pull(grad, normed, inverse, vec_ref[4:5, :])
        d_ref[rows, :] = d_resid
        low_ref[rows, :] = d_resid.astype(BF16)
        low_t_ref[:, rows] = d_resid.astype(BF16).T
        add_sums(sums_ref, (grad * normed, grad, d_resid), block == 0)


def turn(ffn, normed1, cot, vec):
    depth = cot.shape[1]
    return pl.pallas_call(
        turn_kernel,
        grid=(1,),
        in_specs=[whole(SEQ, depth)] * 3 + [whole(8, depth)],
        out_specs=[whole(SEQ, depth)] * 3 + [whole(depth, SEQ), whole(3, depth)],
        out_shape=[
            shaped(BF16, SEQ, depth),
            shaped(F32, SEQ, depth),
            shaped(BF16, SEQ, depth),
            shaped(BF16, depth, SEQ),
            shaped(F32, 3, depth),
        ],
        compiler_params=params(),
        cost_estimate=BRIEF,
        name="turn",
    )(ffn, normed1, cot, vec)


def rejoin_kernel(count, place_ref, d_hidden_ref, normed_ref, inverse_ref, vec_ref, *rest):
    ctx_refs = rest[:3]
    piece_refs = rest[3 : 3 + count]
    d_ref, dctx_ref, even_ref, odd_ref, sums_ref, full_ref, low_t_ref = rest[3 + count :]
    width = ctx_refs[0].shape[1]
    assemble(place_ref, piece_refs, full_ref)
    for block in range(SEQ // QB):
        rows = slice(block * QB, (block + 1) * QB)
        normed = normed_ref[rows, :]
        grad = d_hidden_ref[rows, :]
        d_resid = norm_pull(grad, normed, inverse_ref[rows, 0:1], vec_ref[1:2, :])
        d_ref[rows, :] = d_resid
        low = d_resid.astype(BF16)
        low_t_ref[:, rows] = d_resid.astype(BF16).T
        dctx_ref[rows, :] = mm(low, full_ref[...]).astype(BF16)
        add_sums(sums_ref, (grad * normed, grad, d_resid), block == 0)
    for g, ctx_ref in enumerate(ctx_refs):
        full_ref[:, g * width : (g + 1) * width] = mm(low_t_ref[...], ctx_ref[...]).astype(BF16)
    deal(place_ref, full_ref, even_ref, odd_ref)


def rejoin(place, d_hidden, normed, inverse, vec, ctx, pieces):
    depth = d_hidden.shape[1]
    rows = depth // BLOCKS
    return pl.pallas_call(
        functools.partial(rejoin_kernel, len(pieces[0])),
        grid=(1,),
        in_specs=[SMEM, whole(SEQ, depth), whole(SEQ, depth), whole(SEQ, 128), whole(8, depth)]
        + [whole(SEQ, ctx[0].shape[1])] * 3
        + piece_specs(pieces),
        out_specs=[
            whole(SEQ, depth),
            whole(SEQ, depth),
            whole(BLOCKS // 2, rows, depth),
            whole(BLOCKS // 2, rows, depth),
            whole(3, depth),
        ],
        out_shape=[
            shaped(F32, SEQ, depth),
            shaped(BF16, SEQ, depth),
            shaped(BF16, BLOCKS // 2, rows, depth),
            shaped(BF16, BLOCKS // 2, rows, depth),
            shaped(F32, 3, depth),
        ],
        scratch_shapes=[pltpu.VMEM((depth, depth), BF16), pltpu.VMEM((depth, SEQ), BF16)],
        compiler_params=params(),
        cost_estimate=BRIEF,
        name="rejoin",
    )(place, d_hidden, normed, inverse, vec, *ctx, *pieces[0])


def gelu_parts(gate):
    normal_cdf = 0.5 * (1.0 + lax.erf(gate * INV_ROOT_TWO))
    density = jnp.exp(-0.5 * gate * gate) * INV_ROOT_TWO_PI
    return gate * normal_cdf, normal_cdf + gate * density


def feed_kernel(first, count, place_ref, low_ref, *rest):
    if not first:
        acc_in_ref, *rest = rest
    piece_refs = rest[:count]
    acc_ref, gated_ref, slope_ref, active_ref, full_ref = rest[count:]
    part = gated_ref.shape[1]
    assemble(place_ref, piece_refs, full_ref)

    @pl.when(pl.program_id(0) == 0)
    def _():
        acc_ref[...] = jnp.zeros_like(acc_ref) if first else acc_in_ref[...]

    for block in range(SEQ // FEED_ROWS):
        rows = slice(block * FEED_ROWS, (block + 1) * FEED_ROWS)
        both = mm(low_ref[rows, :], full_ref[:, : 2 * part])
        up = both[:, part:]
        active, slope = gelu_parts(both[:, :part])
        gated = (active * up).astype(BF16)
        gated_ref[rows, :] = gated
        slope_ref[rows, :] = (slope * up).astype(BF16)
        active_ref[rows, :] = active.astype(BF16)
        acc_ref[rows, :] += mm(gated, full_ref[:, 2 * part :], NT)


def feed(place, low, acc, pieces):
    depth = low.shape[1]
    _, steps, rows, lanes = pieces[0][0].shape
    part = lanes // 3
    columns = pl.BlockSpec((SEQ, part), lambda m: (0, m))
    first = acc is None
    return pl.pallas_call(
        functools.partial(feed_kernel, first, len(pieces[0])),
        grid=(steps,),
        in_specs=[SMEM, whole(SEQ, depth)]
        + ([] if first else [whole(SEQ, depth)])
        + piece_specs(pieces),
        out_specs=[whole(SEQ, depth), columns, columns, columns],
        out_shape=[shaped(F32, SEQ, depth)] + [shaped(BF16, SEQ, steps * part)] * 3,
        scratch_shapes=[pltpu.VMEM((depth, lanes), BF16)],
        compiler_params=params(),
        cost_estimate=BRIEF,
        name="feed",
    )(place, low, *([] if first else [acc]), *pieces[0])


def feed_back_kernel(
    count, place_ref, d_ref, d_t_ref, low_t_ref, acc_in_ref, gated_ref, slope_ref, active_ref, *rest
):
    piece_refs = rest[:count]
    acc_ref, even_ref, odd_ref, full_ref, gate_up_ref, keep_ref = rest[count:]
    part = gated_ref.shape[1]
    assemble(place_ref, piece_refs, full_ref)
    step = pl.program_id(0)
    at = pl.ds(pl.multiple_of(step * 2 * part, part), 2 * part)
    keep_ref[:, at] = full_ref[:, : 2 * part]
    for block in range(SEQ // QB):
        rows = slice(block * QB, (block + 1) * QB)
        d_gated = mm(d_ref[rows, :], full_ref[:, 2 * part :])
        d_gate = (d_gated * slope_ref[rows, :].astype(F32)).astype(BF16)
        d_up = (d_gated * active_ref[rows, :].astype(F32)).astype(BF16)
        gate_up_ref[rows, at] = jnp.concatenate([d_gate, d_up], axis=1)
    full_ref[:, : 2 * part] = mm(low_t_ref[...], gate_up_ref[:, at]).astype(BF16)
    full_ref[:, 2 * part :] = mm(d_t_ref[...], gated_ref[...]).astype(BF16)
    deal(place_ref, full_ref, even_ref, odd_ref)

    @pl.when(step == pl.num_programs(0) - 1)
    def _():
        for block in range(SEQ // QB):
            rows = slice(block * QB, (block + 1) * QB)
            acc_ref[rows, :] = acc_in_ref[rows, :] + mm(gate_up_ref[rows, :], keep_ref[...], NT)


def feed_back(place, d_low, d_low_t, low_t, acc, gated, slope, active, pieces):
    depth = d_low.shape[1]
    _, steps, rows, lanes = pieces[0][0].shape
    part = lanes // 3
    columns = pl.BlockSpec((SEQ, part), lambda m: (0, m))
    dealt = pl.BlockSpec((BLOCKS // 2, None, rows, lanes), lambda m: (0, m, 0, 0))
    return pl.pallas_call(
        functools.partial(feed_back_kernel, len(pieces[0])),
        grid=(steps,),
        in_specs=[SMEM, whole(SEQ, depth), whole(depth, SEQ), whole(depth, SEQ), whole(SEQ, depth)]
        + [columns] * 3
        + piece_specs(pieces),
        out_specs=[whole(SEQ, depth), dealt, dealt],
        out_shape=[shaped(F32, SEQ, depth)] + [shaped(BF16, BLOCKS // 2, steps, rows, lanes)] * 2,
        scratch_shapes=[
            pltpu.VMEM((depth, lanes), BF16),
            pltpu.VMEM((SEQ, 2 * steps * part), BF16),
            pltpu.VMEM((depth, 2 * steps * part), BF16),
        ],
        compiler_params=params(),
        cost_estimate=BRIEF,
        name="feed_back",
    )(place, d_low, d_low_t, low_t, acc, gated, slope, active, *pieces[0])


def halves(value, size):
    blocks = [value[:, i : i + size] for i in range(0, value.shape[1], size)]
    return jnp.concatenate(blocks[1::2], axis=1), jnp.concatenate(blocks[0::2], axis=1)


def four(mine, first, second, both):
    values = [item.astype(F32) for item in (mine, first, second, both)]
    return (values[0] + values[1]) + (values[2] + values[3])


def after(value, *earlier):
    earlier = [item for item in jax.tree.leaves(earlier) if item is not value]
    if not earlier:
        return value
    return lax.optimization_barrier((value, *earlier))[0]


def after_all(values, tie):
    return [after(value, tie) for value in values]


def add_three(*values):
    values = [value.astype(F32) for value in values]
    return (values[0] + values[1] + values[2]).astype(BF16)


def add_low(left, right):
    return (left.astype(F32) + right.astype(F32)).astype(BF16)


def interleave(parts, size):
    lanes = parts[0].shape[1]
    return jnp.concatenate(
        [part[:, i : i + size] for i in range(0, lanes, size) for part in parts], axis=1
    )


def pick(value, size, at):
    return jnp.concatenate(
        [value[:, i : i + size] for i in range(at * size, value.shape[1], 4 * size)], axis=1
    )


class Layer:
    def __init__(self, values, order, places):
        (
            self.tokens,
            self.qkv_weight,
            qv_bias,
            self.out_weight,
            out_bias,
            norm1_gain,
            norm1_shift,
            self.in_weight,
            self.down_weight,
            down_bias,
            norm2_gain,
            norm2_shift,
            self.cotangent,
        ) = values
        self.depth = self.tokens.shape[1]
        self.rows = self.qkv_weight.shape[0]
        self.groups = self.qkv_weight.shape[2] // HEAD
        self.part = self.in_weight.shape[2] // FF_CHUNKS
        self.n_tensor = order.shape[0]
        self.places = places
        groups = self.groups
        head_ids = (order[None, :] * groups + jnp.arange(groups, dtype=jnp.int32)[:, None]).reshape(-1)
        powers = jnp.where(head_ids < 8, -(head_ids + 1).astype(F32), 7.5 - head_ids.astype(F32))
        self.slopes = jnp.exp2(powers)
        bias = qv_bias.reshape(2, self.n_tensor, groups, HEAD)[:, order].transpose(2, 0, 1, 3)
        bias = bias.reshape(groups, 2, self.n_tensor * HEAD)
        self.bias = jnp.concatenate([bias[:, 0], jnp.zeros_like(bias[:, 0]), bias[:, 1]], axis=1)
        self.vec = jnp.stack(
            [out_bias, norm1_gain, norm1_shift, down_bias, norm2_gain, norm2_shift, out_bias, out_bias]
        )
        self.tokens_t = self.tokens.T
        self.done = []
        self.kept = []
        self.bias_grads = []
        self.pieces = {}
        self.acc = None

    def head_columns(self, g):
        return [self.qkv_weight[:, c, g * HEAD : (g + 1) * HEAD] for c in range(3)]

    def unit_columns(self, c):
        cols = slice(c * self.part, (c + 1) * self.part)
        return jnp.concatenate(
            [self.in_weight[:, 0, cols], self.in_weight[:, 1, cols], self.down_weight[:, cols]], axis=1
        )

    def attend(self, g, *ready):
        got = attend_forward(
            g,
            self.places[g],
            self.slopes,
            after(self.tokens, *ready),
            self.bias[g : g + 1],
            self.pieces[g],
        )
        self.done.append(got)
        return got[2]

    def join(self, *ready):
        self.qkv, self.ctx, self.lse = zip(*self.done)
        tokens = after(self.tokens, *ready)
        self.normed1, self.inverse1, self.low, self.low_t = join(
            self.places["o"], tokens, self.vec, self.ctx, self.pieces["o"]
        )
        return self.inverse1

    def feed(self, c, *ready):
        low = after(self.low, *ready)
        name = f"u{c}"
        self.acc, *saved = feed(self.places[name], low, self.acc, self.pieces[name])
        self.kept.append(saved)
        return self.acc

    def turn(self):
        self.result, self.d_hidden, self.d_low, self.d_low_t, self.sums2 = turn(
            self.acc, self.normed1, self.cotangent, self.vec
        )

    def feed_back(self, c, *ready):
        d_hidden = after(self.d_hidden, *ready)
        name = f"u{c}"
        self.d_hidden, even, odd = feed_back(
            self.places[name],
            self.d_low,
            self.d_low_t,
            self.low_t,
            d_hidden,
            *self.kept[c],
            self.pieces[name],
        )
        return even, odd, self.d_hidden

    def rejoin(self, *ready):
        d_hidden = after(self.d_hidden, *ready)
        self.d_tokens, self.d_context, even, odd, self.sums1 = rejoin(
            self.places["o"],
            d_hidden,
            self.normed1,
            self.inverse1,
            self.vec,
            self.ctx,
            self.pieces["o"],
        )
        return even, odd, self.d_tokens

    def attend_back_first(self, g, *ready):
        self.d_context = after(self.d_context, *ready)
        self.pair, self.pair_sums = attend_backward_first(
            g, self.slopes, self.qkv[g], self.lse[g], self.d_context
        )
        return self.pair

    def attend_back_second(self, g, *ready):
        d_tokens = after(self.d_tokens, *ready)
        even, odd, sums, self.d_tokens = attend_backward_second(
            g,
            g == self.groups - 1,
            self.places[g],
            self.slopes,
            self.qkv[g],
            self.lse[g],
            self.d_context,
            self.tokens_t,
            d_tokens,
            self.pair,
            self.pieces[g],
        )
        sums = jnp.concatenate([self.pair_sums, sums], axis=1)
        self.bias_grads.append(sums.reshape(2, self.n_tensor, HEAD))
        return even, odd, self.d_tokens

    def small_sums(self, back):
        qv_grad = jnp.stack(self.bias_grads, axis=2)[:, back].reshape(2, self.depth)
        return jnp.concatenate([self.sums1, self.sums2, qv_grad])

    def outputs(self, grads, sums):
        part = self.part
        units = [grads[f"u{c}"] for c in range(FF_CHUNKS)]
        qkv = [grads[g].reshape(self.rows, 3, HEAD) for g in range(self.groups)]
        in_grad = jnp.stack(
            [
                jnp.concatenate([unit[:, i * part : (i + 1) * part] for unit in units], axis=1)
                for i in range(2)
            ],
            axis=1,
        )
        return (
            self.result,
            self.d_tokens,
            jnp.concatenate(qkv, axis=2),
            sums[6:],
            grads["o"],
            sums[2],
            sums[0],
            sums[1],
            in_grad,
            jnp.concatenate([unit[:, 2 * part :] for unit in units], axis=1),
            sums[5],
            sums[3],
            sums[4],
        )


def plain(*values):
    n_tensor = lax.axis_size("tensor")
    index = jnp.arange(n_tensor, dtype=jnp.int32)
    place = jnp.arange(BLOCKS, dtype=jnp.int32)
    names = [0, 1, 2, "o"] + [f"u{c}" for c in range(FF_CHUNKS)]
    layer = Layer(values, index, {name: place for name in names})
    depth = layer.depth

    def heads(piece):
        rows, lanes = piece.shape
        columns = lax.all_gather(
            piece.reshape(rows, lanes // HEAD, 1, HEAD), "tensor", axis=2, tiled=True
        )
        columns = lax.all_gather(columns.reshape(rows, -1), "dp", axis=0, tiled=True)
        return ([columns.reshape(BLOCKS, depth // BLOCKS, -1)], None)

    def units(piece):
        columns = lax.all_gather(lax.all_gather(piece, "tensor", axis=0), "dp", axis=1, tiled=True)
        blocks = columns.reshape(n_tensor, BLOCKS, depth // BLOCKS, -1)
        return ([jnp.moveaxis(blocks, 0, 1)], "grid")

    def total_rows(even, odd):
        blocks = jnp.concatenate([even, odd]).astype(F32)
        blocks = jnp.moveaxis(blocks, 0, -3)
        blocks = blocks.reshape(blocks.shape[:-3] + (-1, blocks.shape[-1]))
        return lax.psum_scatter(blocks, "dp", scatter_dimension=blocks.ndim - 2, tiled=True)

    def total_heads(even, odd):
        mine = total_rows(even, odd)
        rows = mine.shape[0]
        mine = mine.reshape(rows, -1, n_tensor, HEAD)
        mine = lax.psum_scatter(mine, "tensor", scatter_dimension=2, tiled=True)
        return mine.reshape(rows, -1)

    def total_units(even, odd):
        return lax.psum_scatter(total_rows(even, odd), "tensor", scatter_dimension=0, tiled=False)

    for g in range(layer.groups):
        layer.pieces[g] = heads(jnp.concatenate(layer.head_columns(g), axis=1))
        layer.attend(g)
    layer.pieces["o"] = heads(layer.out_weight)
    layer.join()
    for c in range(FF_CHUNKS):
        layer.pieces[f"u{c}"] = units(layer.unit_columns(c))
        layer.feed(c)
    layer.turn()
    grads = {}
    for c in range(FF_CHUNKS):
        grads[f"u{c}"] = total_units(*layer.feed_back(c)[:2])
    grads["o"] = total_heads(*layer.rejoin()[:2])
    for g in range(layer.groups):
        layer.attend_back_first(g)
        grads[g] = total_heads(*layer.attend_back_second(g)[:2])
    return layer.outputs(grads, lax.psum(layer.small_sums(index), ("dp", "tensor")))


def paired(*values):
    me = lax.axis_index("dp")
    at = lax.axis_index("tensor")

    def dp(value, bit):
        return lax.ppermute(value, "dp", [(i, i ^ bit) for i in range(8)])

    def tp(value, bit):
        return lax.ppermute(value, "tensor", [(i, i ^ bit) for i in range(4)])

    def stacked(left, right):
        return jnp.stack([left, right])

    x, y, core = 2, 4, 1
    order = jnp.array([0, 2, 1, 3], jnp.int32) ^ at
    back = jnp.arange(4, dtype=jnp.int32) ^ at
    back = (back & 1) * 2 + (back >> 1)
    place = jnp.array([0, x, y, x | y, 1, x | 1, y | 1, x | y | 1], jnp.int32) ^ me
    names = [0, 1, 2, "o"] + [f"u{c}" for c in range(FF_CHUNKS)]
    layer = Layer(values, order, {name: place for name in names})

    own = jnp.concatenate(layer.head_columns(0), axis=1)
    others = jnp.concatenate(layer.head_columns(1) + layer.head_columns(2) + [layer.out_weight], axis=1)
    units = [layer.unit_columns(c) for c in range(FF_CHUNKS)]
    got = [tp(own, 2), tp(own, 1), tp(own, 3)]
    u2_x, u2_y = dp(units[2], x), dp(units[2], y)
    q0 = interleave([own, *got], HEAD)[None]
    q0_got = [dp(q0, x), dp(q0, y), dp(q0, x | y)]
    others = after(others, q0)
    others = interleave([others, tp(others, 2)], HEAD)
    q0 = [q0, *q0_got]
    q0_core = [dp(value, core) for value in q0]
    others = interleave([others, tp(others, 1)], 128)
    layer.pieces[0] = (q0 + q0_core, None)
    q = jnp.stack([others[:, i * layer.depth : (i + 1) * layer.depth] for i in range(3)])
    q_x, q_y, q1_xy = dp(q, x), dp(q, y), dp(q[:1], x | y)
    u0 = after(units[0], others)
    u0 = stacked(u0, tp(u0, 2))
    u0_near = tp(u0, 1)
    u1_far = tp(after(units[1], u0), 2)

    tie = layer.attend(0, q, u0, u2_x, u2_y, layer.tokens_t)
    q_x, q_y, q1_xy = after(q_x, tie), after(q_y, tie), after(q1_xy, tie)
    q1 = [q[:1], q_x[:1], q_y[:1], q1_xy]
    layer.pieces[1] = (q1 + [dp(value, core) for value in q1], None)
    qo_xy = dp(q_x[1:], y)
    u0 = jnp.concatenate([u0, after(u0_near, tie)])
    u0_x = dp(u0, x)
    u1 = stacked(units[1], after(u1_far, tie))
    u1_near = tp(u1, 1)
    u2_left = stacked(units[2], u2_x)
    u2_xy = dp(after(u2_x, tie), y)
    u2_left_near = tp(after(u2_left, tie), 1)

    tie = layer.attend(1, u0, u1, u2_left)
    qo = [q[1:], q_x[1:], q_y[1:], after(qo_xy, tie)]
    qo = qo + [dp(value, core) for value in qo]
    qo = [value[None] for value in qo]
    layer.pieces[2], layer.pieces["o"] = (qo, 0), (qo, 1)
    u0_x = after(u0_x, tie)
    u0_y = dp(after(u0, u0_x), y)
    u0_core = [dp(after(u0, u0_x), core)]
    u1 = jnp.concatenate([u1, after(u1_near, tie)])
    u1_x = dp(u1, x)
    u2_right = stacked(u2_y, after(u2_xy, tie))
    u2_left_near = after(u2_left_near, tie)
    u2_left_far = tp(after(u2_left, u2_left_near), 2)

    tie = layer.attend(2, u0_x, u1, u2_right, u2_left_near)
    u0_y, u0_core[0] = after(u0_y, tie), after(u0_core[0], tie)
    u0_xy = dp(u0_y, x)
    u0_core += [dp(after(u0_x, tie), core), dp(u0_y, core)]
    u1_x = after(u1_x, tie)
    u1_y = dp(after(u1, u1_x), y)
    u2_left_far = after(u2_left_far, tie)
    u2_right_near = tp(after(u2_right, tie), 1)

    tie = layer.join(u0_y, u1_x, u2_left_far)
    u0_xy = after(u0_xy, tie)
    u0_core = [u0_core[0], *after_all(u0_core[1:], tie), dp(u0_xy, core)]
    layer.pieces["u0"] = ([value[None] for value in [u0, u0_x, u0_y, u0_xy, *u0_core]], "grid")
    u1_y = after(u1_y, tie)
    u1_xy = dp(after(u1_x, u1_y), y)
    u1_core = [dp(after(u1, u1_y), core), dp(after(u1_x, u1_y), core)]
    u2_right_near = after(u2_right_near, tie)
    u2_right_far = tp(after(u2_right, u2_right_near), 2)
    u2_left_both = tp(u2_left_far, 1)

    tie = layer.feed(0, u1_y, u2_right_near)
    u1_xy = after(u1_xy, tie)
    u1_core = after_all(u1_core, tie) + [dp(u1_y, core), dp(u1_xy, core)]
    layer.pieces["u1"] = ([value[None] for value in [u1, u1_x, u1_y, u1_xy, *u1_core]], "grid")
    u2_right_far = after(u2_right_far, tie)
    u2_right_both = tp(u2_right_far, 1)
    u2_left = [u2_left, u2_left_far, u2_left_near, after(u2_left_both, tie)]
    u2_left = jnp.stack(u2_left, axis=1)
    u2_left_core = dp(u2_left, core)

    tie = layer.feed(1, u2_right_far, u2_left)
    u2_right = [u2_right, u2_right_far, u2_right_near, after(u2_right_both, tie)]
    u2_right = jnp.stack(u2_right, axis=1)
    u2_core = [after(u2_left_core, tie), dp(u2_right, core)]
    layer.pieces["u2"] = ([u2_left, u2_right, *u2_core], "grid")
    layer.feed(2)
    layer.turn()

    grads = {}

    def add_core(even, odd, tie, blocks):
        odd = after(odd, tie)
        return [add_low(even[i], odd[i]) for i in blocks]

    even0, odd0, _ = layer.feed_back(0)
    odd0 = dp(odd0, core)

    even1, odd1, tie = layer.feed_back(1)
    f0 = add_core(even0, odd0, tie, range(4))
    f0_first = dp(f0[3], y)
    odd1 = dp(odd1, core)

    even2, odd2, tie = layer.feed_back(2, *f0)
    f0[1] = add_low(f0[1], after(f0_first, tie))
    f0_second = [dp(f0[2], y), dp(f0[1], x)]
    f1 = add_core(even1, odd1, tie, range(4))
    odd2 = dp(odd2, core)

    even_o, odd_o, tie = layer.rejoin(f0[1], *f1)
    f0_second = after_all(f0_second, tie)
    sent = add_three(f0[0][2:], f0_second[0][2:], f0_second[1][2:])
    f0 = add_three(f0[0][:2], f0_second[0][:2], f0_second[1][:2])
    f0_near = tp(sent, 1)
    odd2 = after(odd2, tie)
    f2_sent = [add_low(even2[i : i + 2, 2:], odd2[i : i + 2, 2:]) for i in (0, 2)]
    f2 = [add_low(even2[i : i + 2, :2], odd2[i : i + 2, :2]) for i in (0, 2)]
    f2_left = tp(f2_sent[0], 1)
    odd_o = dp(odd_o, core)

    tie = layer.attend_back_first(0, f0, sent, *f2, *f2_sent)
    f0_near = after(f0_near, tie)
    sent, f0 = add_low(f0[1], f0_near[1]), add_low(f0[0], f0_near[0])
    f0_far = tp(sent, 2)
    f1_first = dp(after(f1[3], tie), x)
    f2_left = after(f2_left, tie)
    f2_left_sent, f2_left = add_low(f2[0][:, 1], f2_left[:, 1]), add_low(f2[0][:, 0], f2_left[:, 0])
    f2_right = tp(after(f2_sent[1], tie), 1)
    o = add_core(even_o, odd_o, tie, range(4))
    o_sent = stacked(o[2], o[3])
    o_first = dp(o_sent, y)

    even_q0, odd_q0, tie = layer.attend_back_second(0, f0, sent, f2_left, f2_left_sent, o_sent, o[0], o[1])
    grads["u0"] = f0.astype(F32) + after(f0_far, tie).astype(F32)
    f1[2] = add_low(f1[2], after(f1_first, tie))
    f1_second = [dp(after(f1[1], tie), x), dp(f1[2], y)]
    f2_right = after(f2_right, tie)
    f2_right_sent, f2_right = add_low(f2[1][:, 1], f2_right[:, 1]), add_low(f2[1][:, 0], f2_right[:, 0])
    f2_left_far = tp(after(f2_left_sent, tie), 2)
    o_first = after(o_first, tie)
    o = [add_low(o[0], o_first[0]), add_low(o[1], o_first[1])]
    o_second = dp(o[1], x)
    odd_q0 = dp(odd_q0, core)

    tie = layer.attend_back_first(1, grads["u0"], f1[2], f2_right, f2_right_sent, *o)
    f1_second = after_all(f1_second, tie)
    sent = add_three(f1[0][2:], f1_second[0][2:], f1_second[1][2:])
    f1 = add_three(f1[0][:2], f1_second[0][:2], f1_second[1][:2])
    f1_near = tp(sent, 1)
    f2_left = add_low(f2_left, after(f2_left_far, tie))
    f2_right_far = tp(after(f2_right_sent, tie), 2)
    o_sent, o = halves(add_low(o[0], after(o_second, tie)), 128)
    o_near = tp(o_sent, 1)
    q0 = add_core(even_q0, odd_q0, tie, range(4))
    q0_sent = stacked(q0[1], q0[3])
    q0_first = dp(q0_sent, x)

    even_q1, odd_q1, tie = layer.attend_back_second(1, f1, sent, f2_left, o, o_sent, q0_sent, q0[0], q0[2])
    f1_near = after(f1_near, tie)
    sent, f1 = add_low(f1[1], f1_near[1]), add_low(f1[0], f1_near[0])
    f1_far = tp(sent, 2)
    f2_right = add_low(f2_right, after(f2_right_far, tie))
    f2_first = dp(f2_right, y)
    o_sent, o = halves(add_low(o, after(o_near, tie)), HEAD)
    o_far = tp(o_sent, 2)
    q0_first = after(q0_first, tie)
    q0 = [add_low(q0[0], q0_first[0]), add_low(q0[2], q0_first[1])]
    q0_second = dp(q0[1], y)
    odd_q1 = dp(odd_q1, core)

    tie = layer.attend_back_first(2, f1, sent, f2_right, o, o_sent, *q0)
    grads["u1"] = f1.astype(F32) + after(f1_far, tie).astype(F32)
    f2_first = after(f2_first, tie)
    f2 = [add_low(f2_left[0], f2_first[0]), add_low(f2_left[1], f2_first[1])]
    f2_second = dp(f2[1], x)
    grads["o"] = o.astype(F32) + after(o_far, tie).astype(F32)
    q0_sent, q0 = halves(add_low(q0[0], after(q0_second, tie)), 128)
    q0_near = tp(q0_sent, 1)
    q1 = add_core(even_q1, odd_q1, tie, range(4))
    q1_sent = stacked(q1[2], q1[3])
    q1_first = dp(q1_sent, y)

    even_q2, odd_q2, tie = layer.attend_back_second(
        2, grads["u1"], grads["o"], *f2, q0, q0_sent, q1_sent, q1[0], q1[1]
    )
    odd_q2 = dp(odd_q2, core)
    sums = layer.small_sums(back)
    sums_got = dp(sums, core)
    q0_sent, q0 = halves(add_low(q0, after(q0_near, tie)), HEAD)
    q0_far = tp(q0_sent, 2)
    q1_first = after(q1_first, tie)
    q1 = [add_low(q1[0], q1_first[0]), add_low(q1[1], q1_first[1])]
    q1_second = dp(q1[1], x)
    grads["u2"] = f2[0].astype(F32) + after(f2_second, tie).astype(F32)

    tie = q1
    q2 = add_core(even_q2, odd_q2, tie, range(4))
    q2_got = [dp(q2[1], x), dp(q2[2], y), dp(q2[3], x | y)]
    sums = sums + after(sums_got, tie)
    sums_got = dp(sums, x)
    q1_sent, q1 = halves(add_low(q1[0], after(q1_second, tie)), 128)
    q1_near = tp(q1_sent, 1)
    tie = [q1, sums]
    grads[0] = q0.astype(F32) + after(q0_far, tie).astype(F32)
    sums = sums + after(sums_got, tie)
    sums_got = dp(sums, y)
    q1_sent, q1 = halves(add_low(q1, after(q1_near, tie)), HEAD)
    q1_far = tp(q1_sent, 2)
    tie = [q1, sums]
    q2 = four(q2[0], *after_all(q2_got, tie)).astype(BF16)
    q2 = [pick(q2, HEAD, i) for i in range(4)]
    q2_got = [tp(q2[1], 2), tp(q2[2], 1), tp(q2[3], 3)]
    sums = sums + after(sums_got, tie)
    sums_got = tp(sums, 1)
    tie = [sums, *q2]
    grads[1] = q1.astype(F32) + after(q1_far, tie).astype(F32)
    sums = sums + after(sums_got, tie)
    sums_got = tp(sums, 2)
    grads[2] = four(q2[0], q2_got[1], q2_got[0], q2_got[2])
    return layer.outputs(grads, sums + sums_got)


def local(suits, *values):
    return paired(*values) if suits else plain(*values)


def solution(mesh):
    rows_all = P(("dp", "tensor"), None)
    columns_3d = P("dp", None, "tensor")
    columns_2d = P("dp", "tensor")
    return jax.shard_map(
        functools.partial(local, dict(mesh.shape) == {"dp": 8, "tensor": 4}),
        mesh=mesh,
        in_specs=(
            rows_all,
            columns_3d,
            P(),
            columns_2d,
            P(),
            P(),
            P(),
            columns_3d,
            columns_2d,
            P(),
            P(),
            P(),
            rows_all,
        ),
        out_specs=(
            rows_all,
            rows_all,
            columns_3d,
            P(),
            columns_2d,
            P(),
            P(),
            P(),
            columns_3d,
            columns_2d,
            P(),
            P(),
            P(),
        ),
        check_vma=False,
    )
```

```python
import functools
import math

import jax
import jax.numpy as jnp
from jax import lax
from jax.experimental import pallas as pl
from jax.experimental.pallas import tpu as pltpu
from jax.sharding import PartitionSpec as P

HEAD = 64
SEQ = 1024
GROUP = 4
QB = 256
AB = 512
FEED_ROWS = 1024
BLOCKS = 8
LOG2E = 1.4426950408889634
INV_ROOT_HEAD = 1.0 / math.sqrt(HEAD)
SCALE = LOG2E * INV_ROOT_HEAD
NORM_EPS = 1e-12
INV_ROOT_TWO = 0.7071067811865476
INV_ROOT_TWO_PI = 0.3989422804014327
FF_CHUNKS = 3
NT = (((1,), (1,)), ((), ()))
NN = (((1,), (0,)), ((), ()))
BF16 = jnp.bfloat16
F32 = jnp.float32


def mm(left, right, dims=NN):
    return lax.dot_general(left, right, dims, preferred_element_type=F32)


def params(**more):
    return pltpu.CompilerParams(vmem_limit_bytes=56 << 20, **more)


BRIEF = pl.CostEstimate(flops=1 << 20, bytes_accessed=1 << 16, transcendentals=0)


SMEM = pl.BlockSpec(memory_space=pltpu.SMEM)


def whole(*shape):
    return pl.BlockSpec(shape, lambda *_: (0,) * len(shape))


def shaped(dtype, *shape):
    return jax.ShapeDtypeStruct(shape, dtype)


def assemble(place_ref, piece_refs, full_ref):
    at = 0
    for piece_ref in piece_refs:
        for i in range(piece_ref.shape[0]):
            rows = piece_ref.shape[1]
            start = pl.multiple_of(place_ref[at] * rows, rows)
            full_ref[pl.ds(start, rows), :] = piece_ref[i]
            at += 1


def deal(place_ref, full_ref, *target_refs, base=0):
    rows = full_ref.shape[0] // BLOCKS
    each = BLOCKS // len(target_refs)
    for at in range(BLOCKS):
        start = pl.multiple_of(place_ref[base + at] * rows, rows)
        target_refs[at // each][at % each] = full_ref[pl.ds(start, rows), :]


def piece_specs(pieces):
    arrays, column = pieces
    specs = []
    for array in arrays:
        if column is None:
            specs.append(whole(*array.shape))
        else:
            count, _, rows, lanes = array.shape
            at = (lambda m: (0, m, 0, 0)) if column == "grid" else (lambda _: (0, column, 0, 0))
            specs.append(pl.BlockSpec((count, None, rows, lanes), at))
    return specs


def fill_row_distance(dist_ref):
    row = lax.broadcasted_iota(jnp.int32, dist_ref.shape, 0)
    col = lax.broadcasted_iota(jnp.int32, dist_ref.shape, 1)
    dist_ref[...] = jnp.abs(row - col + (SEQ - AB)).astype(F32) * LOG2E


def fill_distance(dist_ref):
    row = lax.broadcasted_iota(jnp.int32, dist_ref.shape, 0)
    col = lax.broadcasted_iota(jnp.int32, dist_ref.shape, 1)
    dist_ref[...] = jnp.abs(row - col - (SEQ - AB)).astype(F32) * LOG2E


def attend_kernel(base, count, place_ref, slope_ref, x_ref, bias_ref, *rest):
    piece_refs = rest[:count]
    qkv_ref, ctx_ref, lse_ref, full_ref, dist_ref = rest[count:]
    width = GROUP * HEAD
    assemble(place_ref, piece_refs, full_ref)
    fill_row_distance(dist_ref)
    for block in range(SEQ // AB):
        rows = slice(block * AB, (block + 1) * AB)
        qkv_ref[rows, :] = (mm(x_ref[rows, :], full_ref[...]) + bias_ref[...]).astype(BF16)
    lane = lax.broadcasted_iota(jnp.int32, (1, 128), 1)
    for pair in range(GROUP // 2):
        keys = qkv_ref[:, width + 128 * pair : width + 128 * pair + 128]
        values = qkv_ref[:, 2 * width + 128 * pair : 2 * width + 128 * pair + 128]
        for block in range(SEQ // AB):
            rows = slice(block * AB, (block + 1) * AB)
            start = SEQ - AB - block * AB
            q = qkv_ref[rows, 128 * pair : 128 * pair + 128]
            parts = []
            stats = []
            for side in range(2):
                own = (lane < HEAD) if side == 0 else (lane >= HEAD)
                slope = slope_ref[base + 2 * pair + side]
                s = mm(jnp.where(own, q, jnp.zeros_like(q)), keys, NT) * SCALE
                s = s - slope * dist_ref[:, start : start + SEQ]
                top = jnp.max(s, axis=1, keepdims=True)
                w = jnp.exp2(s - top)
                total = jnp.sum(w, axis=1, keepdims=True)
                p = (w * (1.0 / total)).astype(BF16)
                parts.append(mm(p, values))
                stats.append(top + jnp.log2(total))
            ctx = jnp.where(lane < HEAD, parts[0], parts[1])
            ctx_ref[rows, 128 * pair : 128 * pair + 128] = ctx.astype(BF16)
            flipped = jnp.where(lane < HEAD, stats[0], stats[1]).T
            lse_ref[2 * pair : 2 * pair + 1, rows] = flipped[0:1, :]
            lse_ref[2 * pair + 1 : 2 * pair + 2, rows] = flipped[HEAD : HEAD + 1, :]


def attend_forward(group, place, slopes, x, bias, pieces):
    width = GROUP * HEAD
    depth = x.shape[1]
    return pl.pallas_call(
        functools.partial(attend_kernel, group * GROUP, len(pieces[0])),
        grid=(1,),
        in_specs=[SMEM, SMEM, whole(SEQ, depth), whole(1, 3 * width)]
        + piece_specs(pieces),
        out_specs=[whole(SEQ, 3 * width), whole(SEQ, width), whole(GROUP, SEQ)],
        out_shape=[
            shaped(BF16, SEQ, 3 * width),
            shaped(BF16, SEQ, width),
            shaped(F32, GROUP, SEQ),
        ],
        scratch_shapes=[
            pltpu.VMEM((depth, 3 * width), BF16),
            pltpu.VMEM((AB, 2 * SEQ - AB), F32),
        ],
        compiler_params=params(),
        cost_estimate=BRIEF,
        name="attend_forward",
    )(place, slopes, x, bias, *pieces[0])


def attend_back_pair(pair, slopes, qkv_ref, lse_ref, dctx_ref, dist_ref, acc_ref, dqt_ref, sums_ref):
    width = GROUP * HEAD
    lane = lax.broadcasted_iota(jnp.int32, (1, 128), 1)
    cols = slice(128 * pair, 128 * pair + 128)
    keys = qkv_ref[:, width + 128 * pair : width + 128 * pair + 128]
    values = qkv_ref[:, 2 * width + 128 * pair : 2 * width + 128 * pair + 128]
    keys_t = keys.T
    for side in range(2):
        own = (lane < HEAD) if side == 0 else (lane >= HEAD)
        own_rows = slice(HEAD * side, HEAD * side + HEAD)
        for block in range(SEQ // AB):
            rows = slice(block * AB, (block + 1) * AB)
            start = SEQ - AB - block * AB
            q = qkv_ref[rows, cols]
            q = jnp.where(own, q, jnp.zeros_like(q))
            do = dctx_ref[rows, cols]
            do = jnp.where(own, do, jnp.zeros_like(do))
            s = mm(keys, q, NT) * SCALE
            s = s - slopes[side] * dist_ref[start : start + SEQ, :]
            p = jnp.exp2(s - lse_ref[2 * pair + side : 2 * pair + side + 1, rows])
            dp = mm(values, do, NT)
            inner = jnp.sum(p * dp, axis=0, keepdims=True)
            ds = (p * (dp - inner)).astype(BF16)
            p = p.astype(BF16)
            dv = mm(p, do)
            dk = mm(ds, q)
            if block == 0 and side == 0:
                acc_ref[:, 0:128] = dk
                acc_ref[:, 128:256] = dv
            else:
                acc_ref[:, 0:128] += dk
                acc_ref[:, 128:256] += dv
            dqt_ref[own_rows, rows] = mm(keys_t[own_rows], ds)
    dq = dqt_ref[...].T * INV_ROOT_HEAD
    dk = acc_ref[:, 0:128] * INV_ROOT_HEAD
    dv = acc_ref[:, 128:256]
    sums_ref[0:1, :] = jnp.sum(dq, axis=0, keepdims=True)
    sums_ref[1:2, :] = jnp.sum(dv, axis=0, keepdims=True)
    return dq.astype(BF16), dk.astype(BF16), dv.astype(BF16)


def attend_back_first(
    base, slope_ref, qkv_ref, lse_ref, dctx_ref, dqkv_ref, sums_ref, dist_ref, acc_ref, dqt_ref
):
    fill_distance(dist_ref)
    slopes = [slope_ref[base], slope_ref[base + 1]]
    got = attend_back_pair(
        0, slopes, qkv_ref, lse_ref, dctx_ref, dist_ref, acc_ref, dqt_ref, sums_ref
    )
    for i, value in enumerate(got):
        dqkv_ref[:, 128 * i : 128 * i + 128] = value


def attend_back_second(
    base, place_ref, slope_ref, qkv_ref, lse_ref, dctx_ref, x_t_ref, pair_ref, *rest
):
    even_ref, odd_ref, sums_ref, dqkv_ref, full_ref, dist_ref, acc_ref, dqt_ref = rest
    width = GROUP * HEAD
    fill_distance(dist_ref)
    slopes = [slope_ref[base + 2], slope_ref[base + 3]]
    got = attend_back_pair(
        1, slopes, qkv_ref, lse_ref, dctx_ref, dist_ref, acc_ref, dqt_ref, sums_ref
    )
    for i, value in enumerate(got):
        dqkv_ref[:, width * i : width * i + 128] = pair_ref[:, 128 * i : 128 * i + 128]
        dqkv_ref[:, width * i + 128 : width * i + 256] = value
    full_ref[...] = mm(x_t_ref[...], dqkv_ref[...]).astype(BF16)
    deal(place_ref, full_ref, even_ref, odd_ref)


def attend_scratch():
    return [
        pltpu.VMEM((2 * SEQ - AB, AB), F32),
        pltpu.VMEM((SEQ, 256), F32),
        pltpu.VMEM((128, SEQ), F32),
    ]


def attend_backward_first(group, slopes, qkv, lse, d_context):
    width = GROUP * HEAD
    return pl.pallas_call(
        functools.partial(attend_back_first, group * GROUP),
        grid=(1,),
        in_specs=[
            SMEM,
            whole(SEQ, 3 * width),
            whole(GROUP, SEQ),
            pl.BlockSpec((SEQ, width), lambda _: (0, group)),
        ],
        out_specs=[whole(SEQ, 3 * 128), whole(2, 128)],
        out_shape=[shaped(BF16, SEQ, 3 * 128), shaped(F32, 2, 128)],
        scratch_shapes=attend_scratch(),
        compiler_params=params(),
        cost_estimate=BRIEF,
        name="attend_backward_first",
    )(slopes, qkv, lse, d_context)


def attend_backward_second(group, place, slopes, qkv, lse, d_context, x_t, pair):
    width = GROUP * HEAD
    depth = x_t.shape[0]
    rows = depth // BLOCKS
    return pl.pallas_call(
        functools.partial(attend_back_second, group * GROUP),
        grid=(1,),
        in_specs=[
            SMEM,
            SMEM,
            whole(SEQ, 3 * width),
            whole(GROUP, SEQ),
            pl.BlockSpec((SEQ, width), lambda _: (0, group)),
            whole(depth, SEQ),
            whole(SEQ, 3 * 128),
        ],
        out_specs=[
            whole(BLOCKS // 2, rows, 3 * width),
            whole(BLOCKS // 2, rows, 3 * width),
            whole(2, 128),
            whole(SEQ, 3 * width),
        ],
        out_shape=[
            shaped(BF16, BLOCKS // 2, rows, 3 * width),
            shaped(BF16, BLOCKS // 2, rows, 3 * width),
            shaped(F32, 2, 128),
            shaped(BF16, SEQ, 3 * width),
        ],
        scratch_shapes=[pltpu.VMEM((depth, 3 * width), BF16)] + attend_scratch(),
        compiler_params=params(),
        cost_estimate=BRIEF,
        name="attend_backward_second",
    )(place, slopes, qkv, lse, d_context, x_t, pair)


def tokens_back_kernel(counts, place_ref, d_ref, *rest):
    groups = len(counts)
    dqkv_refs, rest = rest[:groups], rest[groups:]
    out_ref, *full_refs = rest[sum(counts) :]
    at = 0
    for count, full_ref in zip(counts, full_refs):
        assemble(place_ref, rest[at : at + count], full_ref)
        at += count
    for block in range(SEQ // AB):
        rows = slice(block * AB, (block + 1) * AB)
        total = d_ref[rows, :]
        for dqkv_ref, full_ref in zip(dqkv_refs, full_refs):
            total += mm(dqkv_ref[rows, :], full_ref[...], NT)
        out_ref[rows, :] = total.astype(BF16)


def tokens_backward(place, d_resid, dqkv, pieces):
    depth = d_resid.shape[1]
    lanes = dqkv[0].shape[1]
    return pl.pallas_call(
        functools.partial(tokens_back_kernel, [len(arrays) for arrays, _ in pieces]),
        grid=(1,),
        in_specs=[SMEM, whole(SEQ, depth)]
        + [whole(SEQ, lanes)] * len(dqkv)
        + [spec for group in pieces for spec in piece_specs(group)],
        out_specs=whole(SEQ, depth),
        out_shape=shaped(BF16, SEQ, depth),
        scratch_shapes=[pltpu.VMEM((depth, lanes), BF16)] * len(dqkv),
        compiler_params=params(),
        cost_estimate=BRIEF,
        name="tokens_backward",
    )(place, d_resid, *dqkv, *[array for arrays, _ in pieces for array in arrays])


def row_mean(value):
    return jnp.mean(value, axis=1, keepdims=True)


def normalize(resid):
    center = resid - row_mean(resid)
    inverse = lax.rsqrt(row_mean(center * center) + NORM_EPS)
    return center * inverse, inverse


def norm_pull(grad_rows, normed, inverse, gain):
    scaled = grad_rows * gain
    return inverse * (scaled - row_mean(scaled) - normed * row_mean(scaled * normed))


def add_sums(sums_ref, values, first):
    for place, value in enumerate(values):
        row = jnp.sum(value, axis=0, keepdims=True)
        if first:
            sums_ref[place : place + 1, :] = row
        else:
            sums_ref[place : place + 1, :] += row


def join_kernel(count, place_ref, x_ref, vec_ref, *rest):
    ctx_refs = rest[:3]
    piece_refs = rest[3 : 3 + count]
    normed_ref, inverse_ref, low_ref, low_t_ref, full_ref = rest[3 + count :]
    assemble(place_ref, piece_refs, full_ref)
    width = ctx_refs[0].shape[1]
    for block in range(SEQ // QB):
        rows = slice(block * QB, (block + 1) * QB)
        total = x_ref[rows, :].astype(F32) + vec_ref[0:1, :]
        for g, ctx_ref in enumerate(ctx_refs):
            total += mm(ctx_ref[rows, :], full_ref[:, g * width : (g + 1) * width], NT)
        normed, inverse = normalize(total)
        normed_ref[rows, :] = normed
        inverse_ref[rows, :] = jnp.broadcast_to(inverse, (QB, 128))
        low = normed * vec_ref[1:2, :] + vec_ref[2:3, :]
        low_ref[rows, :] = low.astype(BF16)
        low_t_ref[:, rows] = low.astype(BF16).T


def join(place, x, vec, ctx, pieces):
    depth = x.shape[1]
    rows = depth // BLOCKS
    return pl.pallas_call(
        functools.partial(join_kernel, len(pieces[0])),
        grid=(1,),
        in_specs=[SMEM, whole(SEQ, depth), whole(8, depth)]
        + [whole(SEQ, ctx[0].shape[1])] * 3
        + piece_specs(pieces),
        out_specs=[whole(SEQ, depth), whole(SEQ, 128), whole(SEQ, depth), whole(depth, SEQ)],
        out_shape=[
            shaped(F32, SEQ, depth),
            shaped(F32, SEQ, 128),
            shaped(BF16, SEQ, depth),
            shaped(BF16, depth, SEQ),
        ],
        scratch_shapes=[pltpu.VMEM((depth, depth), BF16)],
        compiler_params=params(),
        cost_estimate=BRIEF,
        name="join",
    )(place, x, vec, *ctx, *pieces[0])


def turn_kernel(ffn_ref, normed1_ref, cot_ref, vec_ref, out_ref, d_ref, low_ref, low_t_ref, sums_ref):
    for block in range(SEQ // QB):
        rows = slice(block * QB, (block + 1) * QB)
        hidden = normed1_ref[rows, :] * vec_ref[1:2, :] + vec_ref[2:3, :]
        normed, inverse = normalize(hidden + ffn_ref[rows, :] + vec_ref[3:4, :])
        out_ref[rows, :] = (normed * vec_ref[4:5, :] + vec_ref[5:6, :]).astype(BF16)
        grad = cot_ref[rows, :].astype(F32)
        d_resid = norm_pull(grad, normed, inverse, vec_ref[4:5, :])
        d_ref[rows, :] = d_resid
        low_ref[rows, :] = d_resid.astype(BF16)
        low_t_ref[:, rows] = d_resid.astype(BF16).T
        add_sums(sums_ref, (grad * normed, grad, d_resid), block == 0)


def turn(ffn, normed1, cot, vec):
    depth = cot.shape[1]
    return pl.pallas_call(
        turn_kernel,
        grid=(1,),
        in_specs=[whole(SEQ, depth)] * 3 + [whole(8, depth)],
        out_specs=[whole(SEQ, depth)] * 3 + [whole(depth, SEQ), whole(3, depth)],
        out_shape=[
            shaped(BF16, SEQ, depth),
            shaped(F32, SEQ, depth),
            shaped(BF16, SEQ, depth),
            shaped(BF16, depth, SEQ),
            shaped(F32, 3, depth),
        ],
        compiler_params=params(),
        cost_estimate=BRIEF,
        name="turn",
    )(ffn, normed1, cot, vec)


def rejoin_kernel(count, place_ref, d_hidden_ref, normed_ref, inverse_ref, vec_ref, *rest):
    ctx_refs = rest[:3]
    piece_refs = rest[3 : 3 + count]
    d_ref, dctx_ref, even_ref, odd_ref, sums_ref, full_ref, low_t_ref = rest[3 + count :]
    width = ctx_refs[0].shape[1]
    assemble(place_ref, piece_refs, full_ref)
    for block in range(SEQ // QB):
        rows = slice(block * QB, (block + 1) * QB)
        normed = normed_ref[rows, :]
        grad = d_hidden_ref[rows, :]
        d_resid = norm_pull(grad, normed, inverse_ref[rows, 0:1], vec_ref[1:2, :])
        d_ref[rows, :] = d_resid
        low = d_resid.astype(BF16)
        low_t_ref[:, rows] = d_resid.astype(BF16).T
        dctx_ref[rows, :] = mm(low, full_ref[...]).astype(BF16)
        add_sums(sums_ref, (grad * normed, grad, d_resid), block == 0)
    for g, ctx_ref in enumerate(ctx_refs):
        full_ref[:, g * width : (g + 1) * width] = mm(low_t_ref[...], ctx_ref[...]).astype(BF16)
    deal(place_ref, full_ref, even_ref, odd_ref)


def rejoin(place, d_hidden, normed, inverse, vec, ctx, pieces):
    depth = d_hidden.shape[1]
    rows = depth // BLOCKS
    return pl.pallas_call(
        functools.partial(rejoin_kernel, len(pieces[0])),
        grid=(1,),
        in_specs=[SMEM, whole(SEQ, depth), whole(SEQ, depth), whole(SEQ, 128), whole(8, depth)]
        + [whole(SEQ, ctx[0].shape[1])] * 3
        + piece_specs(pieces),
        out_specs=[
            whole(SEQ, depth),
            whole(SEQ, depth),
            whole(BLOCKS // 2, rows, depth),
            whole(BLOCKS // 2, rows, depth),
            whole(3, depth),
        ],
        out_shape=[
            shaped(F32, SEQ, depth),
            shaped(BF16, SEQ, depth),
            shaped(BF16, BLOCKS // 2, rows, depth),
            shaped(BF16, BLOCKS // 2, rows, depth),
            shaped(F32, 3, depth),
        ],
        scratch_shapes=[pltpu.VMEM((depth, depth), BF16), pltpu.VMEM((depth, SEQ), BF16)],
        compiler_params=params(),
        cost_estimate=BRIEF,
        name="rejoin",
    )(place, d_hidden, normed, inverse, vec, *ctx, *pieces[0])


def gelu_parts(gate):
    normal_cdf = 0.5 * (1.0 + lax.erf(gate * INV_ROOT_TWO))
    density = jnp.exp(-0.5 * gate * gate) * INV_ROOT_TWO_PI
    return gate * normal_cdf, normal_cdf + gate * density


def feed_kernel(first, count, place_ref, low_ref, *rest):
    if not first:
        acc_in_ref, *rest = rest
    piece_refs = rest[:count]
    acc_ref, gated_ref, slope_ref, active_ref, full_ref = rest[count:]
    part = gated_ref.shape[1]
    assemble(place_ref, piece_refs, full_ref)

    @pl.when(pl.program_id(0) == 0)
    def _():
        acc_ref[...] = jnp.zeros_like(acc_ref) if first else acc_in_ref[...]

    for block in range(SEQ // FEED_ROWS):
        rows = slice(block * FEED_ROWS, (block + 1) * FEED_ROWS)
        both = mm(low_ref[rows, :], full_ref[:, : 2 * part])
        up = both[:, part:]
        active, slope = gelu_parts(both[:, :part])
        gated = (active * up).astype(BF16)
        gated_ref[rows, :] = gated
        slope_ref[rows, :] = (slope * up).astype(BF16)
        active_ref[rows, :] = active.astype(BF16)
        acc_ref[rows, :] += mm(gated, full_ref[:, 2 * part :], NT)


def feed(place, low, acc, pieces):
    depth = low.shape[1]
    _, steps, rows, lanes = pieces[0][0].shape
    part = lanes // 3
    columns = pl.BlockSpec((SEQ, part), lambda m: (0, m))
    first = acc is None
    return pl.pallas_call(
        functools.partial(feed_kernel, first, len(pieces[0])),
        grid=(steps,),
        in_specs=[SMEM, whole(SEQ, depth)]
        + ([] if first else [whole(SEQ, depth)])
        + piece_specs(pieces),
        out_specs=[whole(SEQ, depth), columns, columns, columns],
        out_shape=[shaped(F32, SEQ, depth)] + [shaped(BF16, SEQ, steps * part)] * 3,
        scratch_shapes=[pltpu.VMEM((depth, lanes), BF16)],
        compiler_params=params(),
        cost_estimate=BRIEF,
        name="feed",
    )(place, low, *([] if first else [acc]), *pieces[0])


def feed_back_kernel(
    count, place_ref, d_ref, d_t_ref, low_t_ref, acc_in_ref, gated_ref, slope_ref, active_ref, *rest
):
    piece_refs = rest[:count]
    acc_ref, *target_refs, full_ref, gate_up_ref, keep_ref = rest[count:]
    part = gated_ref.shape[1]
    assemble(place_ref, piece_refs, full_ref)
    step = pl.program_id(0)
    at = pl.ds(pl.multiple_of(step * 2 * part, part), 2 * part)
    keep_ref[:, at] = full_ref[:, : 2 * part]
    for block in range(SEQ // QB):
        rows = slice(block * QB, (block + 1) * QB)
        d_gated = mm(d_ref[rows, :], full_ref[:, 2 * part :])
        d_gate = (d_gated * slope_ref[rows, :].astype(F32)).astype(BF16)
        d_up = (d_gated * active_ref[rows, :].astype(F32)).astype(BF16)
        gate_up_ref[rows, at] = jnp.concatenate([d_gate, d_up], axis=1)
    full_ref[:, : 2 * part] = mm(low_t_ref[...], gate_up_ref[:, at]).astype(BF16)
    full_ref[:, 2 * part :] = mm(d_t_ref[...], gated_ref[...]).astype(BF16)
    deal(place_ref, full_ref, *target_refs, base=BLOCKS)

    @pl.when(step == pl.num_programs(0) - 1)
    def _():
        for block in range(SEQ // QB):
            rows = slice(block * QB, (block + 1) * QB)
            acc_ref[rows, :] = acc_in_ref[rows, :] + mm(gate_up_ref[rows, :], keep_ref[...], NT)


def feed_back(order, halves_out, d_low, d_low_t, low_t, acc, gated, slope, active, pieces):
    depth = d_low.shape[1]
    _, steps, rows, lanes = pieces[0][0].shape
    part = lanes // 3
    columns = pl.BlockSpec((SEQ, part), lambda m, _: (0, m))
    each = BLOCKS // halves_out
    dealt = pl.BlockSpec(
        (each, None, rows, lanes), lambda m, order_ref: (0, order_ref[2 * BLOCKS + m], 0, 0)
    )
    gathered = [
        pl.BlockSpec((array.shape[0], None, rows, lanes), lambda m, _: (0, m, 0, 0))
        for array in pieces[0]
    ]
    return pl.pallas_call(
        functools.partial(feed_back_kernel, len(pieces[0])),
        grid_spec=pltpu.PrefetchScalarGridSpec(
            num_scalar_prefetch=1,
            grid=(steps,),
            in_specs=[whole(SEQ, depth), whole(depth, SEQ), whole(depth, SEQ), whole(SEQ, depth)]
            + [columns] * 3
            + gathered,
            out_specs=[whole(SEQ, depth)] + [dealt] * halves_out,
            scratch_shapes=[
                pltpu.VMEM((depth, lanes), BF16),
                pltpu.VMEM((SEQ, 2 * steps * part), BF16),
                pltpu.VMEM((depth, 2 * steps * part), BF16),
            ],
        ),
        out_shape=[shaped(F32, SEQ, depth)] + [shaped(BF16, each, steps, rows, lanes)] * halves_out,
        compiler_params=params(),
        cost_estimate=BRIEF,
        name="feed_back",
    )(order, d_low, d_low_t, low_t, acc, gated, slope, active, *pieces[0])


def halves(value, size):
    blocks = [value[:, i : i + size] for i in range(0, value.shape[1], size)]
    return jnp.concatenate(blocks[1::2], axis=1), jnp.concatenate(blocks[0::2], axis=1)


def four(mine, first, second, both):
    values = [item.astype(F32) for item in (mine, first, second, both)]
    return (values[0] + values[1]) + (values[2] + values[3])


def after(value, *earlier):
    earlier = jax.tree.leaves(earlier)
    if not earlier:
        return value
    return lax.optimization_barrier((value, *earlier))[0]


def after_all(values, tie):
    return [after(value, tie) for value in values]


def add_three(*values):
    values = [value.astype(F32) for value in values]
    return (values[0] + values[1] + values[2]).astype(BF16)


def add_low(left, right):
    return (left.astype(F32) + right.astype(F32)).astype(BF16)


def interleave(parts, size):
    lanes = parts[0].shape[1]
    return jnp.concatenate(
        [part[:, i : i + size] for i in range(0, lanes, size) for part in parts], axis=1
    )


def pick(value, size, at):
    return jnp.concatenate(
        [value[:, i : i + size] for i in range(at * size, value.shape[1], 4 * size)], axis=1
    )


class Layer:
    def __init__(self, values, order, places, orders):
        (
            self.tokens,
            self.qkv_weight,
            qv_bias,
            self.out_weight,
            out_bias,
            norm1_gain,
            norm1_shift,
            self.in_weight,
            self.down_weight,
            down_bias,
            norm2_gain,
            norm2_shift,
            self.cotangent,
        ) = values
        self.depth = self.tokens.shape[1]
        self.rows = self.qkv_weight.shape[0]
        self.groups = self.qkv_weight.shape[2] // HEAD
        self.part = self.in_weight.shape[2] // FF_CHUNKS
        self.n_tensor = order.shape[0]
        self.places = places
        self.orders = orders
        groups = self.groups
        head_ids = (order[None, :] * groups + jnp.arange(groups, dtype=jnp.int32)[:, None]).reshape(-1)
        powers = jnp.where(head_ids < 8, -(head_ids + 1).astype(F32), 7.5 - head_ids.astype(F32))
        self.slopes = jnp.exp2(powers)
        bias = qv_bias.reshape(2, self.n_tensor, groups, HEAD)[:, order].transpose(2, 0, 1, 3)
        bias = bias.reshape(groups, 2, self.n_tensor * HEAD)
        self.bias = jnp.concatenate([bias[:, 0], jnp.zeros_like(bias[:, 0]), bias[:, 1]], axis=1)
        self.vec = jnp.stack(
            [out_bias, norm1_gain, norm1_shift, down_bias, norm2_gain, norm2_shift, out_bias, out_bias]
        )
        self.tokens_t = self.tokens.T
        self.done = []
        self.bias_grads = []
        self.dqkv = []
        self.pieces = {}
        self.acc = None
        self.kept = {}

    def head_columns(self, g):
        return [self.qkv_weight[:, c, g * HEAD : (g + 1) * HEAD] for c in range(3)]

    def unit_columns(self, c, *ready):
        cols = slice(c * self.part, (c + 1) * self.part)
        in_weight, down_weight = after((self.in_weight, self.down_weight), *ready)
        return jnp.concatenate([in_weight[:, 0, cols], in_weight[:, 1, cols], down_weight[:, cols]], axis=1)

    def attend(self, g, *ready):
        got = attend_forward(
            g,
            self.places[g],
            self.slopes,
            after(self.tokens, *ready),
            self.bias[g : g + 1],
            self.pieces[g],
        )
        self.done.append(got)
        return got[2]

    def join(self, *ready):
        self.qkv, self.ctx, self.lse = zip(*self.done)
        tokens = after(self.tokens, *ready)
        self.normed1, self.inverse1, self.low, self.low_t = join(
            self.places["o"], tokens, self.vec, self.ctx, self.pieces["o"]
        )
        return self.inverse1

    def feed(self, c, *ready):
        low = after(self.low, *ready)
        name = f"u{c}"
        self.acc, *saved = feed(self.places[name], low, self.acc, self.pieces[name])
        self.kept[c] = saved
        return self.acc

    def turn(self):
        self.result, self.d_hidden, self.d_low, self.d_low_t, self.sums2 = turn(
            self.acc, self.normed1, self.cotangent, self.vec
        )

    def feed_back(self, c, halves_out, *ready):
        d_hidden = after(self.d_hidden, *ready)
        name = f"u{c}"
        self.d_hidden, *dealt = feed_back(
            self.orders[name],
            halves_out,
            self.d_low,
            self.d_low_t,
            self.low_t,
            d_hidden,
            *self.kept[c],
            self.pieces[name],
        )
        return *dealt, self.d_hidden

    def rejoin(self, *ready):
        d_hidden = after(self.d_hidden, *ready)
        self.d_tokens, self.d_context, even, odd, self.sums1 = rejoin(
            self.places["o"],
            d_hidden,
            self.normed1,
            self.inverse1,
            self.vec,
            self.ctx,
            self.pieces["o"],
        )
        return even, odd, self.d_tokens

    def attend_back_first(self, g, *ready):
        self.d_context = after(self.d_context, *ready)
        self.pair, self.pair_sums = attend_backward_first(
            g, self.slopes, self.qkv[g], self.lse[g], self.d_context
        )
        return self.pair

    def attend_back_second(self, g, *ready):
        even, odd, sums, dqkv = attend_backward_second(
            g,
            self.places[g],
            self.slopes,
            self.qkv[g],
            self.lse[g],
            self.d_context,
            self.tokens_t,
            after(self.pair, *ready),
        )
        sums = jnp.concatenate([self.pair_sums, sums], axis=1)
        self.bias_grads.append(sums.reshape(2, self.n_tensor, HEAD))
        self.dqkv.append(dqkv)
        return even, odd, sums

    def tokens_back(self, *ready):
        pieces = [self.pieces[g] for g in range(self.groups)]
        self.d_tokens = tokens_backward(
            self.places[0], after(self.d_tokens, *ready), self.dqkv, pieces
        )
        return self.d_tokens

    def small_sums(self, back):
        qv_grad = jnp.stack(self.bias_grads, axis=2)[:, back].reshape(2, self.depth)
        return jnp.concatenate([self.sums1, self.sums2, qv_grad])

    def outputs(self, grads, sums):
        part = self.part
        units = [grads[f"u{c}"] for c in range(FF_CHUNKS)]
        qkv = [grads[g].reshape(self.rows, 3, HEAD) for g in range(self.groups)]
        in_grad = jnp.stack(
            [
                jnp.concatenate([unit[:, i * part : (i + 1) * part] for unit in units], axis=1)
                for i in range(2)
            ],
            axis=1,
        )
        return (
            self.result,
            self.d_tokens,
            jnp.concatenate(qkv, axis=2),
            sums[6:],
            grads["o"],
            sums[2],
            sums[0],
            sums[1],
            in_grad,
            jnp.concatenate([unit[:, 2 * part :] for unit in units], axis=1),
            sums[5],
            sums[3],
            sums[4],
        )


def plain(*values):
    n_tensor = lax.axis_size("tensor")
    index = jnp.arange(n_tensor, dtype=jnp.int32)
    place = jnp.arange(BLOCKS, dtype=jnp.int32)
    names = [0, 1, 2, "o"] + [f"u{c}" for c in range(FF_CHUNKS)]
    layer = Layer(
        values,
        index,
        {name: place for name in names},
        {name: jnp.concatenate([place, place, index]) for name in names},
    )
    depth = layer.depth

    def heads(piece):
        rows, lanes = piece.shape
        columns = lax.all_gather(
            piece.reshape(rows, lanes // HEAD, 1, HEAD), "tensor", axis=2, tiled=True
        )
        columns = lax.all_gather(columns.reshape(rows, -1), "dp", axis=0, tiled=True)
        return ([columns.reshape(BLOCKS, depth // BLOCKS, -1)], None)

    def units(piece):
        columns = lax.all_gather(lax.all_gather(piece, "tensor", axis=0), "dp", axis=1, tiled=True)
        blocks = columns.reshape(n_tensor, BLOCKS, depth // BLOCKS, -1)
        return ([jnp.moveaxis(blocks, 0, 1)], "grid")

    def total_rows(even, odd):
        blocks = jnp.concatenate([even, odd]).astype(F32)
        blocks = jnp.moveaxis(blocks, 0, -3)
        blocks = blocks.reshape(blocks.shape[:-3] + (-1, blocks.shape[-1]))
        return lax.psum_scatter(blocks, "dp", scatter_dimension=blocks.ndim - 2, tiled=True)

    def total_heads(even, odd):
        mine = total_rows(even, odd)
        rows = mine.shape[0]
        mine = mine.reshape(rows, -1, n_tensor, HEAD)
        mine = lax.psum_scatter(mine, "tensor", scatter_dimension=2, tiled=True)
        return mine.reshape(rows, -1)

    def total_units(even, odd):
        return lax.psum_scatter(total_rows(even, odd), "tensor", scatter_dimension=0, tiled=False)

    for g in range(layer.groups):
        layer.pieces[g] = heads(jnp.concatenate(layer.head_columns(g), axis=1))
        layer.attend(g)
    layer.pieces["o"] = heads(layer.out_weight)
    layer.join()
    for c in range(FF_CHUNKS):
        layer.pieces[f"u{c}"] = units(layer.unit_columns(c))
        layer.feed(c)
    layer.turn()
    grads = {}
    for c in range(FF_CHUNKS):
        grads[f"u{c}"] = total_units(*layer.feed_back(c, 2)[:2])
    grads["o"] = total_heads(*layer.rejoin()[:2])
    for g in range(layer.groups):
        layer.attend_back_first(g)
        grads[g] = total_heads(*layer.attend_back_second(g)[:2])
    layer.tokens_back()
    return layer.outputs(grads, lax.psum(layer.small_sums(index), ("dp", "tensor")))


def paired(*values):
    me = lax.axis_index("dp")
    at = lax.axis_index("tensor")

    def dp(value, bit):
        return lax.ppermute(value, "dp", [(i, i ^ bit) for i in range(8)])

    def tp(value, bit):
        return lax.ppermute(value, "tensor", [(i, i ^ bit) for i in range(4)])

    def stacked(left, right):
        return jnp.stack([left, right])

    x, y, core = 2, 4, 1
    order = jnp.array([0, 2, 1, 3], jnp.int32) ^ at
    index = jnp.arange(4, dtype=jnp.int32)
    back = index ^ at
    back = (back & 1) * 2 + (back >> 1)
    place = jnp.array([0, x, y, x | y, 1, x | 1, y | 1, x | y | 1], jnp.int32) ^ me
    lined = jnp.arange(BLOCKS, dtype=jnp.int32)
    places = {name: place for name in [0, 1, 2, "o", "u0", "u1"]}
    places["u2"] = lined
    orders = {
        "u0": jnp.concatenate([place, lined, index]),
        "u1": jnp.concatenate([place, lined, index]),
        "u2": jnp.concatenate([lined, place, back]),
    }
    layer = Layer(values, order, places, orders)
    depth = layer.depth

    own = jnp.concatenate(layer.head_columns(0), axis=1)
    others = jnp.concatenate(layer.head_columns(1) + layer.head_columns(2) + [layer.out_weight], axis=1)
    got = [tp(own, 2), tp(own, 1), tp(own, 3)]
    q0 = interleave([own, *got], HEAD)[None]
    units = [layer.unit_columns(c, q0) for c in range(FF_CHUNKS)]
    u2 = lax.all_gather(units[2], ("dp", "tensor"), axis=0, tiled=True)
    layer.pieces["u2"] = ([u2.reshape(BLOCKS, 4, layer.rows, -1)], "grid")
    q0_got = [dp(q0, x), dp(q0, y), dp(q0, x | y)]
    far = tp(after(others, q0), 2)
    q0 = [q0, *q0_got]
    q0_core = [dp(value, core) for value in q0]
    others = interleave([others, after(far, q0_core)], HEAD)
    others = interleave([others, tp(others, 1)], 128)
    layer.pieces[0] = (q0 + q0_core, None)
    q = jnp.stack([others[:, i * depth : (i + 1) * depth] for i in range(3)])
    q_x, q_y, q1_xy = dp(q, x), dp(q, y), dp(q[:1], x | y)
    u = stacked(*after((units[0], units[1]), others))
    u_far = tp(u, 2)

    tie = layer.attend(0, q, u, layer.tokens_t)
    q_x, q_y, q1_xy = after(q_x, tie), after(q_y, tie), after(q1_xy, tie)
    q1 = [q[:1], q_x[:1], q_y[:1], q1_xy]
    layer.pieces[1] = (q1 + [dp(value, core) for value in q1], None)
    qo_xy = dp(q_x[1:], y)
    u = jnp.stack([u, after(u_far, tie)], axis=1)
    u_near = tp(u, 1)

    tie = layer.attend(1, u)
    qo = [q[1:], q_x[1:], q_y[1:], after(qo_xy, tie)]
    qo = [value[None] for value in qo + [dp(value, core) for value in qo]]
    layer.pieces[2], layer.pieces["o"] = (qo, 0), (qo, 1)
    u_near = after(u_near, tie)
    u0, u1 = [jnp.concatenate([u[c], u_near[c]]) for c in range(2)]
    u0_x, u0_y = dp(u0, x), dp(u0, y)

    tie = layer.attend(2, u0, u1)
    u0_x, u0_y = after(u0_x, tie), after(u0_y, tie)
    u1_x = dp(after(u1, tie), x)
    u0_core = [dp(value, core) for value in after((u0, u0_x, u0_y), tie)]

    tie = layer.join(u0_x, u0_y)
    u1_x = after(u1_x, tie)
    u0_core = after_all(u0_core, tie)
    u0_xy = dp(after(u0_y, u1_x), x)
    u1_y = dp(after(u1, u1_x), y)

    tie = layer.feed(2, u1_x)
    u0_xy, u1_y = after(u0_xy, tie), after(u1_y, tie)
    u0_core = u0_core + [dp(u0_xy, core)]
    layer.pieces["u0"] = ([value[None] for value in [u0, u0_x, u0_y, u0_xy, *u0_core]], "grid")
    u1_xy = dp(u1_y, x)
    u1_core = [dp(value, core) for value in after((u1, u1_x, u1_y), tie)]

    tie = layer.feed(0, u1_y)
    u1_xy = after(u1_xy, tie)
    u1_core = after_all(u1_core, tie) + [dp(u1_xy, core)]
    layer.pieces["u1"] = ([value[None] for value in [u1, u1_x, u1_y, u1_xy, *u1_core]], "grid")
    layer.feed(1)
    layer.turn()

    grads = {}

    def add_core(even, odd, tie, blocks):
        odd = after(odd, tie)
        return [add_low(even[i], odd[i]) for i in blocks]

    def over_dp(dealt):
        mine = dealt.reshape(-1, dealt.shape[-1])
        mine = lax.psum_scatter(mine, "dp", scatter_dimension=0, tiled=True)
        return mine.reshape(dealt.shape[1:])

    dealt, _ = layer.feed_back(0, 1)
    f0 = over_dp(dealt)
    dealt, _ = layer.feed_back(1, 1)
    f1 = over_dp(dealt)
    even2, odd2, _ = layer.feed_back(2, 2)
    odd2 = dp(odd2, core)

    even_o, odd_o, tie = layer.rejoin()
    odd2 = after(odd2, tie)
    f2_sent = [add_low(even2[i : i + 2, 2:], odd2[i : i + 2, 2:]) for i in (0, 2)]
    f2 = [add_low(even2[i : i + 2, :2], odd2[i : i + 2, :2]) for i in (0, 2)]
    f2_left = tp(f2_sent[0], 1)
    odd_o = dp(odd_o, core)

    tie = layer.attend_back_first(0, *f2, *f2_sent)
    f2_left = after(f2_left, tie)
    f2_left_sent, f2_left = add_low(f2[0][:, 1], f2_left[:, 1]), add_low(f2[0][:, 0], f2_left[:, 0])
    f2_right = tp(after(f2_sent[1], tie), 1)

    even_q0, odd_q0, tie = layer.attend_back_second(0, f2_left, f2_left_sent)
    f2_right = after(f2_right, tie)
    f2_right_sent, f2_right = add_low(f2[1][:, 1], f2_right[:, 1]), add_low(f2[1][:, 0], f2_right[:, 0])
    f2_left_far = tp(after(f2_left_sent, tie), 2)
    odd_q0 = dp(odd_q0, core)
    f0 = after(f0, tie)
    f0_near = tp(f0[2:], 1)

    tie = layer.attend_back_first(1, f2_right, f2_right_sent, f0)
    f0_near = after(f0_near, tie)
    f0_sent, f0 = add_low(f0[1], f0_near[1]), add_low(f0[0], f0_near[0])
    f0_far = tp(f0_sent, 2)
    f2_left = add_low(f2_left, after(f2_left_far, tie))
    f2_right_far = tp(after(f2_right_sent, tie), 2)
    odd_oq = after((odd_o, odd_q0), tie)
    oq_sent = jnp.stack([add_low(even[2:], odd[2:]) for even, odd in zip((even_o, even_q0), odd_oq)])
    oq = jnp.stack([add_low(even[:2], odd[:2]) for even, odd in zip((even_o, even_q0), odd_oq)])
    oq_first = dp(oq_sent, y)

    even_q1, odd_q1, tie = layer.attend_back_second(1, f2_left, oq_sent, oq, f0, f0_sent)
    grads["u0"] = f0.astype(F32) + after(f0_far, tie).astype(F32)
    f2_right = add_low(f2_right, after(f2_right_far, tie))
    f2_first = dp(f2_right, y)
    oq_first = after(oq_first, tie)
    oq_sent, oq = add_low(oq[:, 1], oq_first[:, 1]), add_low(oq[:, 0], oq_first[:, 0])
    oq_second = dp(oq_sent, x)
    odd_q1 = dp(odd_q1, core)

    tie = layer.attend_back_first(2, f2_right, oq_sent, oq)
    f2_first = after(f2_first, tie)
    f2 = [add_low(f2_left[0], f2_first[0]), add_low(f2_left[1], f2_first[1])]
    f2_second = dp(f2[1], x)
    oq = add_low(oq, after(oq_second, tie)).reshape(-1, depth)
    oq_sent, oq = halves(oq, 128)
    oq_near = tp(oq_sent, 1)
    f1 = after(f1, tie)
    f1_near = tp(f1[2:], 1)
    q1 = add_core(even_q1, odd_q1, tie, range(4))
    q1_sent = stacked(q1[2], q1[3])
    q1_first = dp(q1_sent, y)

    even_q2, odd_q2, tie = layer.attend_back_second(2, *f2, oq, oq_sent, q1_sent, q1[0], q1[1], f1)
    f1_near = after(f1_near, tie)
    f1_sent, f1 = add_low(f1[1], f1_near[1]), add_low(f1[0], f1_near[0])
    f1_far = tp(f1_sent, 2)
    odd_q2 = dp(odd_q2, core)
    sums = layer.small_sums(back)
    sums_got = dp(sums, core)
    q1_first = after(q1_first, tie)
    q1 = [add_low(q1[0], q1_first[0]), add_low(q1[1], q1_first[1])]
    q1_second = dp(q1[1], x)
    oq_sent, oq = halves(add_low(oq, after(oq_near, tie)), HEAD)
    oq_far = tp(oq_sent, 2)
    grads["u2"] = f2[0].astype(F32) + after(f2_second, tie).astype(F32)

    tie = [odd_q2]
    q2 = add_core(even_q2, odd_q2, tie, range(4))
    q2_got = [dp(q2[1], x), dp(q2[2], y), dp(q2[3], x | y)]
    tie = layer.tokens_back(q2)
    q2_got = after_all(q2_got, tie)
    grads["u1"] = f1.astype(F32) + after(f1_far, tie).astype(F32)
    sums = sums + after(sums_got, tie)
    sums_got = dp(sums, x)
    q1 = add_low(q1[0], after(q1_second, tie))
    q2 = four(q2[0], *q2_got).astype(BF16)
    last = jnp.stack([q1, q2]).reshape(-1, depth)
    last = [pick(last, HEAD, i) for i in range(4)]
    last_got = [tp(last[1], 2), tp(last[2], 1), tp(last[3], 3)]
    oq = (oq.astype(F32) + after(oq_far, last).astype(F32)).reshape(2, layer.rows, -1)
    grads["o"], grads[0] = oq[0], oq[1]
    sums = sums + after(sums_got, last)
    sums_got = dp(sums, y)
    sums = sums + sums_got
    last = four(last[0], last_got[1], last_got[0], last_got[2]).reshape(2, layer.rows, -1)
    grads[1], grads[2] = last[0], last[1]
    for bit in (1, 2):
        sums = sums + tp(sums, bit)
    return layer.outputs(grads, sums)


def local(suits, *values):
    return paired(*values) if suits else plain(*values)


def solution(mesh):
    rows_all = P(("dp", "tensor"), None)
    columns_3d = P("dp", None, "tensor")
    columns_2d = P("dp", "tensor")
    return jax.shard_map(
        functools.partial(local, dict(mesh.shape) == {"dp": 8, "tensor": 4}),
        mesh=mesh,
        in_specs=(
            rows_all,
            columns_3d,
            P(),
            columns_2d,
            P(),
            P(),
            P(),
            columns_3d,
            columns_2d,
            P(),
            P(),
            P(),
            rows_all,
        ),
        out_specs=(
            rows_all,
            rows_all,
            columns_3d,
            P(),
            columns_2d,
            P(),
            P(),
            P(),
            columns_3d,
            columns_2d,
            P(),
            P(),
            P(),
        ),
        check_vma=False,
    )
```

```python
import functools
import math

import jax
import jax.numpy as jnp
from jax import lax
from jax.experimental import pallas as pl
from jax.experimental.pallas import tpu as pltpu
from jax.sharding import PartitionSpec as P

HEAD = 64
SEQ = 1024
GROUP = 4
QB = 256
AB = 512
FEED_ROWS = 1024
BLOCKS = 8
LOG2E = 1.4426950408889634
INV_ROOT_HEAD = 1.0 / math.sqrt(HEAD)
SCALE = LOG2E * INV_ROOT_HEAD
NORM_EPS = 1e-12
INV_ROOT_TWO = 0.7071067811865476
INV_ROOT_TWO_PI = 0.3989422804014327
FF_CHUNKS = 3
NT = (((1,), (1,)), ((), ()))
NN = (((1,), (0,)), ((), ()))
BF16 = jnp.bfloat16
F32 = jnp.float32


def mm(left, right, dims=NN):
    return lax.dot_general(left, right, dims, preferred_element_type=F32)


def params(**more):
    return pltpu.CompilerParams(vmem_limit_bytes=56 << 20, **more)


BRIEF = pl.CostEstimate(flops=1 << 20, bytes_accessed=1 << 16, transcendentals=0)


SMEM = pl.BlockSpec(memory_space=pltpu.SMEM)


def whole(*shape):
    return pl.BlockSpec(shape, lambda *_: (0,) * len(shape))


def shaped(dtype, *shape):
    return jax.ShapeDtypeStruct(shape, dtype)


def assemble(place_ref, piece_refs, full_ref):
    at = 0
    for piece_ref in piece_refs:
        for i in range(piece_ref.shape[0]):
            rows = piece_ref.shape[1]
            start = pl.multiple_of(place_ref[at] * rows, rows)
            full_ref[pl.ds(start, rows), :] = piece_ref[i]
            at += 1


def deal(place_ref, full_ref, *target_refs, base=0):
    rows = full_ref.shape[0] // BLOCKS
    each = BLOCKS // len(target_refs)
    for at in range(BLOCKS):
        start = pl.multiple_of(place_ref[base + at] * rows, rows)
        target_refs[at // each][at % each] = full_ref[pl.ds(start, rows), :]


def piece_specs(pieces):
    arrays, column = pieces
    specs = []
    for array in arrays:
        if column is None:
            specs.append(whole(*array.shape))
        else:
            count, _, rows, lanes = array.shape
            at = (lambda m: (0, m, 0, 0)) if column == "grid" else (lambda _: (0, column, 0, 0))
            specs.append(pl.BlockSpec((count, None, rows, lanes), at))
    return specs


def fill_row_distance(dist_ref):
    row = lax.broadcasted_iota(jnp.int32, dist_ref.shape, 0)
    col = lax.broadcasted_iota(jnp.int32, dist_ref.shape, 1)
    dist_ref[...] = jnp.abs(row - col + (SEQ - AB)).astype(F32) * LOG2E


def fill_distance(dist_ref):
    row = lax.broadcasted_iota(jnp.int32, dist_ref.shape, 0)
    col = lax.broadcasted_iota(jnp.int32, dist_ref.shape, 1)
    dist_ref[...] = jnp.abs(row - col - (SEQ - AB)).astype(F32) * LOG2E


def attend_kernel(base, count, place_ref, slope_ref, x_ref, bias_ref, *rest):
    piece_refs = rest[:count]
    qkv_ref, ctx_ref, lse_ref, full_ref, dist_ref = rest[count:]
    width = GROUP * HEAD
    assemble(place_ref, piece_refs, full_ref)
    fill_row_distance(dist_ref)
    for block in range(SEQ // AB):
        rows = slice(block * AB, (block + 1) * AB)
        qkv_ref[rows, :] = (mm(x_ref[rows, :], full_ref[...]) + bias_ref[...]).astype(BF16)
    lane = lax.broadcasted_iota(jnp.int32, (1, 128), 1)
    for pair in range(GROUP // 2):
        keys = qkv_ref[:, width + 128 * pair : width + 128 * pair + 128]
        values = qkv_ref[:, 2 * width + 128 * pair : 2 * width + 128 * pair + 128]
        for block in range(SEQ // AB):
            rows = slice(block * AB, (block + 1) * AB)
            start = SEQ - AB - block * AB
            q = qkv_ref[rows, 128 * pair : 128 * pair + 128]
            parts = []
            stats = []
            for side in range(2):
                own = (lane < HEAD) if side == 0 else (lane >= HEAD)
                slope = slope_ref[base + 2 * pair + side]
                s = mm(jnp.where(own, q, jnp.zeros_like(q)), keys, NT) * SCALE
                s = s - slope * dist_ref[:, start : start + SEQ]
                top = jnp.max(s, axis=1, keepdims=True)
                w = jnp.exp2(s - top)
                total = jnp.sum(w, axis=1, keepdims=True)
                p = (w * (1.0 / total)).astype(BF16)
                parts.append(mm(p, values))
                stats.append(top + jnp.log2(total))
            ctx = jnp.where(lane < HEAD, parts[0], parts[1])
            ctx_ref[rows, 128 * pair : 128 * pair + 128] = ctx.astype(BF16)
            flipped = jnp.where(lane < HEAD, stats[0], stats[1]).T
            lse_ref[2 * pair : 2 * pair + 1, rows] = flipped[0:1, :]
            lse_ref[2 * pair + 1 : 2 * pair + 2, rows] = flipped[HEAD : HEAD + 1, :]


def attend_forward(group, place, slopes, x, bias, pieces):
    width = GROUP * HEAD
    depth = x.shape[1]
    return pl.pallas_call(
        functools.partial(attend_kernel, group * GROUP, len(pieces[0])),
        grid=(1,),
        in_specs=[SMEM, SMEM, whole(SEQ, depth), whole(1, 3 * width)]
        + piece_specs(pieces),
        out_specs=[whole(SEQ, 3 * width), whole(SEQ, width), whole(GROUP, SEQ)],
        out_shape=[
            shaped(BF16, SEQ, 3 * width),
            shaped(BF16, SEQ, width),
            shaped(F32, GROUP, SEQ),
        ],
        scratch_shapes=[
            pltpu.VMEM((depth, 3 * width), BF16),
            pltpu.VMEM((AB, 2 * SEQ - AB), F32),
        ],
        compiler_params=params(),
        cost_estimate=BRIEF,
        name="attend_forward",
    )(place, slopes, x, bias, *pieces[0])


def attend_back_pair(pair, slopes, qkv_ref, lse_ref, dctx_ref, dist_ref, acc_ref, dqt_ref, sums_ref):
    width = GROUP * HEAD
    lane = lax.broadcasted_iota(jnp.int32, (1, 128), 1)
    cols = slice(128 * pair, 128 * pair + 128)
    keys = qkv_ref[:, width + 128 * pair : width + 128 * pair + 128]
    values = qkv_ref[:, 2 * width + 128 * pair : 2 * width + 128 * pair + 128]
    keys_t = keys.T
    for side in range(2):
        own = (lane < HEAD) if side == 0 else (lane >= HEAD)
        own_rows = slice(HEAD * side, HEAD * side + HEAD)
        for block in range(SEQ // AB):
            rows = slice(block * AB, (block + 1) * AB)
            start = SEQ - AB - block * AB
            q = qkv_ref[rows, cols]
            q = jnp.where(own, q, jnp.zeros_like(q))
            do = dctx_ref[rows, cols]
            do = jnp.where(own, do, jnp.zeros_like(do))
            s = mm(keys, q, NT) * SCALE
            s = s - slopes[side] * dist_ref[start : start + SEQ, :]
            p = jnp.exp2(s - lse_ref[2 * pair + side : 2 * pair + side + 1, rows])
            dp = mm(values, do, NT)
            inner = jnp.sum(p * dp, axis=0, keepdims=True)
            ds = (p * (dp - inner)).astype(BF16)
            p = p.astype(BF16)
            dv = mm(p, do)
            dk = mm(ds, q)
            if block == 0 and side == 0:
                acc_ref[:, 0:128] = dk
                acc_ref[:, 128:256] = dv
            else:
                acc_ref[:, 0:128] += dk
                acc_ref[:, 128:256] += dv
            dqt_ref[own_rows, rows] = mm(keys_t[own_rows], ds)
    dq = dqt_ref[...].T * INV_ROOT_HEAD
    dk = acc_ref[:, 0:128] * INV_ROOT_HEAD
    dv = acc_ref[:, 128:256]
    sums_ref[0:1, :] = jnp.sum(dq, axis=0, keepdims=True)
    sums_ref[1:2, :] = jnp.sum(dv, axis=0, keepdims=True)
    return dq.astype(BF16), dk.astype(BF16), dv.astype(BF16)


def attend_back_first(
    base, slope_ref, qkv_ref, lse_ref, dctx_ref, dqkv_ref, sums_ref, dist_ref, acc_ref, dqt_ref
):
    fill_distance(dist_ref)
    slopes = [slope_ref[base], slope_ref[base + 1]]
    got = attend_back_pair(
        0, slopes, qkv_ref, lse_ref, dctx_ref, dist_ref, acc_ref, dqt_ref, sums_ref
    )
    for i, value in enumerate(got):
        dqkv_ref[:, 128 * i : 128 * i + 128] = value


def attend_back_second(
    base, place_ref, slope_ref, qkv_ref, lse_ref, dctx_ref, x_t_ref, pair_ref, *rest
):
    even_ref, odd_ref, sums_ref, dqkv_ref, full_ref, dist_ref, acc_ref, dqt_ref = rest
    width = GROUP * HEAD
    fill_distance(dist_ref)
    slopes = [slope_ref[base + 2], slope_ref[base + 3]]
    got = attend_back_pair(
        1, slopes, qkv_ref, lse_ref, dctx_ref, dist_ref, acc_ref, dqt_ref, sums_ref
    )
    for i, value in enumerate(got):
        dqkv_ref[:, width * i : width * i + 128] = pair_ref[:, 128 * i : 128 * i + 128]
        dqkv_ref[:, width * i + 128 : width * i + 256] = value
    full_ref[...] = mm(x_t_ref[...], dqkv_ref[...]).astype(BF16)
    deal(place_ref, full_ref, even_ref, odd_ref)


def attend_scratch():
    return [
        pltpu.VMEM((2 * SEQ - AB, AB), F32),
        pltpu.VMEM((SEQ, 256), F32),
        pltpu.VMEM((128, SEQ), F32),
    ]


def attend_backward_first(group, slopes, qkv, lse, d_context):
    width = GROUP * HEAD
    return pl.pallas_call(
        functools.partial(attend_back_first, group * GROUP),
        grid=(1,),
        in_specs=[
            SMEM,
            whole(SEQ, 3 * width),
            whole(GROUP, SEQ),
            pl.BlockSpec((SEQ, width), lambda _: (0, group)),
        ],
        out_specs=[whole(SEQ, 3 * 128), whole(2, 128)],
        out_shape=[shaped(BF16, SEQ, 3 * 128), shaped(F32, 2, 128)],
        scratch_shapes=attend_scratch(),
        compiler_params=params(),
        cost_estimate=BRIEF,
        name="attend_backward_first",
    )(slopes, qkv, lse, d_context)


def attend_backward_second(group, place, slopes, qkv, lse, d_context, x_t, pair):
    width = GROUP * HEAD
    depth = x_t.shape[0]
    rows = depth // BLOCKS
    return pl.pallas_call(
        functools.partial(attend_back_second, group * GROUP),
        grid=(1,),
        in_specs=[
            SMEM,
            SMEM,
            whole(SEQ, 3 * width),
            whole(GROUP, SEQ),
            pl.BlockSpec((SEQ, width), lambda _: (0, group)),
            whole(depth, SEQ),
            whole(SEQ, 3 * 128),
        ],
        out_specs=[
            whole(BLOCKS // 2, rows, 3 * width),
            whole(BLOCKS // 2, rows, 3 * width),
            whole(2, 128),
            whole(SEQ, 3 * width),
        ],
        out_shape=[
            shaped(BF16, BLOCKS // 2, rows, 3 * width),
            shaped(BF16, BLOCKS // 2, rows, 3 * width),
            shaped(F32, 2, 128),
            shaped(BF16, SEQ, 3 * width),
        ],
        scratch_shapes=[pltpu.VMEM((depth, 3 * width), BF16)] + attend_scratch(),
        compiler_params=params(),
        cost_estimate=BRIEF,
        name="attend_backward_second",
    )(place, slopes, qkv, lse, d_context, x_t, pair)


def tokens_back_kernel(counts, place_ref, d_ref, *rest):
    groups = len(counts)
    dqkv_refs, rest = rest[:groups], rest[groups:]
    out_ref, *full_refs = rest[sum(counts) :]
    at = 0
    for count, full_ref in zip(counts, full_refs):
        assemble(place_ref, rest[at : at + count], full_ref)
        at += count
    for block in range(SEQ // AB):
        rows = slice(block * AB, (block + 1) * AB)
        total = d_ref[rows, :]
        for dqkv_ref, full_ref in zip(dqkv_refs, full_refs):
            total += mm(dqkv_ref[rows, :], full_ref[...], NT)
        out_ref[rows, :] = total.astype(BF16)


def tokens_backward(place, d_resid, dqkv, pieces):
    depth = d_resid.shape[1]
    lanes = dqkv[0].shape[1]
    return pl.pallas_call(
        functools.partial(tokens_back_kernel, [len(arrays) for arrays, _ in pieces]),
        grid=(1,),
        in_specs=[SMEM, whole(SEQ, depth)]
        + [whole(SEQ, lanes)] * len(dqkv)
        + [spec for group in pieces for spec in piece_specs(group)],
        out_specs=whole(SEQ, depth),
        out_shape=shaped(BF16, SEQ, depth),
        scratch_shapes=[pltpu.VMEM((depth, lanes), BF16)] * len(dqkv),
        compiler_params=params(),
        cost_estimate=BRIEF,
        name="tokens_backward",
    )(place, d_resid, *dqkv, *[array for arrays, _ in pieces for array in arrays])


def row_mean(value):
    return jnp.mean(value, axis=1, keepdims=True)


def normalize(resid):
    center = resid - row_mean(resid)
    inverse = lax.rsqrt(row_mean(center * center) + NORM_EPS)
    return center * inverse, inverse


def norm_pull(grad_rows, normed, inverse, gain):
    scaled = grad_rows * gain
    return inverse * (scaled - row_mean(scaled) - normed * row_mean(scaled * normed))


def add_sums(sums_ref, values, first):
    for place, value in enumerate(values):
        row = jnp.sum(value, axis=0, keepdims=True)
        if first:
            sums_ref[place : place + 1, :] = row
        else:
            sums_ref[place : place + 1, :] += row


def join_kernel(count, place_ref, x_ref, vec_ref, *rest):
    ctx_refs = rest[:3]
    piece_refs = rest[3 : 3 + count]
    normed_ref, inverse_ref, low_ref, low_t_ref, full_ref = rest[3 + count :]
    assemble(place_ref, piece_refs, full_ref)
    width = ctx_refs[0].shape[1]
    for block in range(SEQ // QB):
        rows = slice(block * QB, (block + 1) * QB)
        total = x_ref[rows, :].astype(F32) + vec_ref[0:1, :]
        for g, ctx_ref in enumerate(ctx_refs):
            total += mm(ctx_ref[rows, :], full_ref[:, g * width : (g + 1) * width], NT)
        normed, inverse = normalize(total)
        normed_ref[rows, :] = normed
        inverse_ref[rows, :] = jnp.broadcast_to(inverse, (QB, 128))
        low = normed * vec_ref[1:2, :] + vec_ref[2:3, :]
        low_ref[rows, :] = low.astype(BF16)
        low_t_ref[:, rows] = low.astype(BF16).T


def join(place, x, vec, ctx, pieces):
    depth = x.shape[1]
    rows = depth // BLOCKS
    return pl.pallas_call(
        functools.partial(join_kernel, len(pieces[0])),
        grid=(1,),
        in_specs=[SMEM, whole(SEQ, depth), whole(8, depth)]
        + [whole(SEQ, ctx[0].shape[1])] * 3
        + piece_specs(pieces),
        out_specs=[whole(SEQ, depth), whole(SEQ, 128), whole(SEQ, depth), whole(depth, SEQ)],
        out_shape=[
            shaped(F32, SEQ, depth),
            shaped(F32, SEQ, 128),
            shaped(BF16, SEQ, depth),
            shaped(BF16, depth, SEQ),
        ],
        scratch_shapes=[pltpu.VMEM((depth, depth), BF16)],
        compiler_params=params(),
        cost_estimate=BRIEF,
        name="join",
    )(place, x, vec, *ctx, *pieces[0])


def turn_kernel(ffn_ref, normed1_ref, cot_ref, vec_ref, out_ref, d_ref, low_ref, low_t_ref, sums_ref):
    for block in range(SEQ // QB):
        rows = slice(block * QB, (block + 1) * QB)
        hidden = normed1_ref[rows, :] * vec_ref[1:2, :] + vec_ref[2:3, :]
        normed, inverse = normalize(hidden + ffn_ref[rows, :] + vec_ref[3:4, :])
        out_ref[rows, :] = (normed * vec_ref[4:5, :] + vec_ref[5:6, :]).astype(BF16)
        grad = cot_ref[rows, :].astype(F32)
        d_resid = norm_pull(grad, normed, inverse, vec_ref[4:5, :])
        d_ref[rows, :] = d_resid
        low_ref[rows, :] = d_resid.astype(BF16)
        low_t_ref[:, rows] = d_resid.astype(BF16).T
        add_sums(sums_ref, (grad * normed, grad, d_resid), block == 0)


def turn(ffn, normed1, cot, vec):
    depth = cot.shape[1]
    return pl.pallas_call(
        turn_kernel,
        grid=(1,),
        in_specs=[whole(SEQ, depth)] * 3 + [whole(8, depth)],
        out_specs=[whole(SEQ, depth)] * 3 + [whole(depth, SEQ), whole(3, depth)],
        out_shape=[
            shaped(BF16, SEQ, depth),
            shaped(F32, SEQ, depth),
            shaped(BF16, SEQ, depth),
            shaped(BF16, depth, SEQ),
            shaped(F32, 3, depth),
        ],
        compiler_params=params(),
        cost_estimate=BRIEF,
        name="turn",
    )(ffn, normed1, cot, vec)


def rejoin_kernel(count, place_ref, d_hidden_ref, normed_ref, inverse_ref, vec_ref, *rest):
    ctx_refs = rest[:3]
    piece_refs = rest[3 : 3 + count]
    d_ref, dctx_ref, even_ref, odd_ref, sums_ref, full_ref, low_t_ref = rest[3 + count :]
    width = ctx_refs[0].shape[1]
    assemble(place_ref, piece_refs, full_ref)
    for block in range(SEQ // QB):
        rows = slice(block * QB, (block + 1) * QB)
        normed = normed_ref[rows, :]
        grad = d_hidden_ref[rows, :]
        d_resid = norm_pull(grad, normed, inverse_ref[rows, 0:1], vec_ref[1:2, :])
        d_ref[rows, :] = d_resid
        low = d_resid.astype(BF16)
        low_t_ref[:, rows] = d_resid.astype(BF16).T
        dctx_ref[rows, :] = mm(low, full_ref[...]).astype(BF16)
        add_sums(sums_ref, (grad * normed, grad, d_resid), block == 0)
    for g, ctx_ref in enumerate(ctx_refs):
        full_ref[:, g * width : (g + 1) * width] = mm(low_t_ref[...], ctx_ref[...]).astype(BF16)
    deal(place_ref, full_ref, even_ref, odd_ref)


def rejoin(place, d_hidden, normed, inverse, vec, ctx, pieces):
    depth = d_hidden.shape[1]
    rows = depth // BLOCKS
    return pl.pallas_call(
        functools.partial(rejoin_kernel, len(pieces[0])),
        grid=(1,),
        in_specs=[SMEM, whole(SEQ, depth), whole(SEQ, depth), whole(SEQ, 128), whole(8, depth)]
        + [whole(SEQ, ctx[0].shape[1])] * 3
        + piece_specs(pieces),
        out_specs=[
            whole(SEQ, depth),
            whole(SEQ, depth),
            whole(BLOCKS // 2, rows, depth),
            whole(BLOCKS // 2, rows, depth),
            whole(3, depth),
        ],
        out_shape=[
            shaped(F32, SEQ, depth),
            shaped(BF16, SEQ, depth),
            shaped(BF16, BLOCKS // 2, rows, depth),
            shaped(BF16, BLOCKS // 2, rows, depth),
            shaped(F32, 3, depth),
        ],
        scratch_shapes=[pltpu.VMEM((depth, depth), BF16), pltpu.VMEM((depth, SEQ), BF16)],
        compiler_params=params(),
        cost_estimate=BRIEF,
        name="rejoin",
    )(place, d_hidden, normed, inverse, vec, *ctx, *pieces[0])


def gelu_parts(gate):
    normal_cdf = 0.5 * (1.0 + lax.erf(gate * INV_ROOT_TWO))
    density = jnp.exp(-0.5 * gate * gate) * INV_ROOT_TWO_PI
    return gate * normal_cdf, normal_cdf + gate * density


def feed_kernel(first, count, place_ref, low_ref, *rest):
    if not first:
        acc_in_ref, *rest = rest
    piece_refs = rest[:count]
    acc_ref, gated_ref, slope_ref, active_ref, full_ref = rest[count:]
    part = gated_ref.shape[1]
    assemble(place_ref, piece_refs, full_ref)

    @pl.when(pl.program_id(0) == 0)
    def _():
        acc_ref[...] = jnp.zeros_like(acc_ref) if first else acc_in_ref[...]

    for block in range(SEQ // FEED_ROWS):
        rows = slice(block * FEED_ROWS, (block + 1) * FEED_ROWS)
        both = mm(low_ref[rows, :], full_ref[:, : 2 * part])
        up = both[:, part:]
        active, slope = gelu_parts(both[:, :part])
        gated = (active * up).astype(BF16)
        gated_ref[rows, :] = gated
        slope_ref[rows, :] = (slope * up).astype(BF16)
        active_ref[rows, :] = active.astype(BF16)
        acc_ref[rows, :] += mm(gated, full_ref[:, 2 * part :], NT)


def feed(place, low, acc, pieces):
    depth = low.shape[1]
    _, steps, rows, lanes = pieces[0][0].shape
    part = lanes // 3
    columns = pl.BlockSpec((SEQ, part), lambda m: (0, m))
    first = acc is None
    return pl.pallas_call(
        functools.partial(feed_kernel, first, len(pieces[0])),
        grid=(steps,),
        in_specs=[SMEM, whole(SEQ, depth)]
        + ([] if first else [whole(SEQ, depth)])
        + piece_specs(pieces),
        out_specs=[whole(SEQ, depth), columns, columns, columns],
        out_shape=[shaped(F32, SEQ, depth)] + [shaped(BF16, SEQ, steps * part)] * 3,
        scratch_shapes=[pltpu.VMEM((depth, lanes), BF16)],
        compiler_params=params(),
        cost_estimate=BRIEF,
        name="feed",
    )(place, low, *([] if first else [acc]), *pieces[0])


def feed_back_kernel(
    count, steps, place_ref, d_ref, d_t_ref, low_t_ref, acc_in_ref, gated_ref, slope_ref, active_ref, *rest
):
    piece_refs = rest[:count]
    acc_ref, *target_refs, full_ref, gate_up_ref, keep_ref = rest[count:]
    part = gated_ref.shape[1]
    step = pl.program_id(0)

    @pl.when(step < steps)
    def _():
        assemble(place_ref, piece_refs, full_ref)
        at = pl.ds(pl.multiple_of(step * 2 * part, part), 2 * part)
        keep_ref[:, at] = full_ref[:, : 2 * part]
        for block in range(SEQ // QB):
            rows = slice(block * QB, (block + 1) * QB)
            d_gated = mm(d_ref[rows, :], full_ref[:, 2 * part :])
            d_gate = (d_gated * slope_ref[rows, :].astype(F32)).astype(BF16)
            d_up = (d_gated * active_ref[rows, :].astype(F32)).astype(BF16)
            gate_up_ref[rows, at] = jnp.concatenate([d_gate, d_up], axis=1)
        full_ref[:, : 2 * part] = mm(low_t_ref[...], gate_up_ref[:, at]).astype(BF16)
        full_ref[:, 2 * part :] = mm(d_t_ref[...], gated_ref[...]).astype(BF16)
        deal(place_ref, full_ref, *target_refs, base=BLOCKS)

    @pl.when(step >= steps)
    def _():
        rows = pl.ds(pl.multiple_of((step - steps) * QB, QB), QB)
        acc_ref[...] = acc_in_ref[...] + mm(gate_up_ref[rows, :], keep_ref[...], NT)


def feed_back(order, halves_out, d_low, d_low_t, low_t, acc, gated, slope, active, pieces):
    depth = d_low.shape[1]
    _, steps, rows, lanes = pieces[0][0].shape
    part = lanes // 3
    columns = pl.BlockSpec((SEQ, part), lambda m, _: (0, jnp.minimum(m, steps - 1)))
    some = pl.BlockSpec((QB, depth), lambda m, _: (jnp.maximum(m - steps, 0), 0))
    each = BLOCKS // halves_out
    dealt = pl.BlockSpec(
        (each, None, rows, lanes), lambda m, order_ref: (0, order_ref[2 * BLOCKS + jnp.minimum(m, steps - 1)], 0, 0)
    )
    gathered = [
        pl.BlockSpec((array.shape[0], None, rows, lanes), lambda m, _: (0, jnp.minimum(m, steps - 1), 0, 0))
        for array in pieces[0]
    ]
    return pl.pallas_call(
        functools.partial(feed_back_kernel, len(pieces[0]), steps),
        grid_spec=pltpu.PrefetchScalarGridSpec(
            num_scalar_prefetch=1,
            grid=(steps + SEQ // QB,),
            in_specs=[whole(SEQ, depth), whole(depth, SEQ), whole(depth, SEQ), some]
            + [columns] * 3
            + gathered,
            out_specs=[some] + [dealt] * halves_out,
            scratch_shapes=[
                pltpu.VMEM((depth, lanes), BF16),
                pltpu.VMEM((SEQ, 2 * steps * part), BF16),
                pltpu.VMEM((depth, 2 * steps * part), BF16),
            ],
        ),
        out_shape=[shaped(F32, SEQ, depth)] + [shaped(BF16, each, steps, rows, lanes)] * halves_out,
        compiler_params=params(),
        cost_estimate=BRIEF,
        name="feed_back",
    )(order, d_low, d_low_t, low_t, acc, gated, slope, active, *pieces[0])


def halves(value, size):
    blocks = [value[:, i : i + size] for i in range(0, value.shape[1], size)]
    return jnp.concatenate(blocks[1::2], axis=1), jnp.concatenate(blocks[0::2], axis=1)


def four(mine, first, second, both):
    values = [item.astype(F32) for item in (mine, first, second, both)]
    return (values[0] + values[1]) + (values[2] + values[3])


def after(value, *earlier):
    earlier = jax.tree.leaves(earlier)
    if not earlier:
        return value
    return lax.optimization_barrier((value, *earlier))[0]


def after_all(values, tie):
    return [after(value, tie) for value in values]


def add_three(*values):
    values = [value.astype(F32) for value in values]
    return (values[0] + values[1] + values[2]).astype(BF16)


def add_low(left, right):
    return (left.astype(F32) + right.astype(F32)).astype(BF16)


def interleave(parts, size):
    lanes = parts[0].shape[1]
    return jnp.concatenate(
        [part[:, i : i + size] for i in range(0, lanes, size) for part in parts], axis=1
    )


def pick(value, size, at):
    return jnp.concatenate(
        [value[:, i : i + size] for i in range(at * size, value.shape[1], 4 * size)], axis=1
    )


class Layer:
    def __init__(self, values, order, places, orders):
        (
            self.tokens,
            self.qkv_weight,
            qv_bias,
            self.out_weight,
            out_bias,
            norm1_gain,
            norm1_shift,
            self.in_weight,
            self.down_weight,
            down_bias,
            norm2_gain,
            norm2_shift,
            self.cotangent,
        ) = values
        self.depth = self.tokens.shape[1]
        self.rows = self.qkv_weight.shape[0]
        self.groups = self.qkv_weight.shape[2] // HEAD
        self.part = self.in_weight.shape[2] // FF_CHUNKS
        self.n_tensor = order.shape[0]
        self.places = places
        self.orders = orders
        groups = self.groups
        head_ids = (order[None, :] * groups + jnp.arange(groups, dtype=jnp.int32)[:, None]).reshape(-1)
        powers = jnp.where(head_ids < 8, -(head_ids + 1).astype(F32), 7.5 - head_ids.astype(F32))
        self.slopes = jnp.exp2(powers)
        bias = qv_bias.reshape(2, self.n_tensor, groups, HEAD)[:, order].transpose(2, 0, 1, 3)
        bias = bias.reshape(groups, 2, self.n_tensor * HEAD)
        self.bias = jnp.concatenate([bias[:, 0], jnp.zeros_like(bias[:, 0]), bias[:, 1]], axis=1)
        self.vec = jnp.stack(
            [out_bias, norm1_gain, norm1_shift, down_bias, norm2_gain, norm2_shift, out_bias, out_bias]
        )
        self.tokens_t = self.tokens.T
        self.done = []
        self.bias_grads = []
        self.dqkv = []
        self.pieces = {}
        self.acc = None
        self.kept = {}

    def head_columns(self, g):
        return [self.qkv_weight[:, c, g * HEAD : (g + 1) * HEAD] for c in range(3)]

    def unit_columns(self, c, *ready):
        cols = slice(c * self.part, (c + 1) * self.part)
        in_weight, down_weight = after((self.in_weight, self.down_weight), *ready)
        return jnp.concatenate([in_weight[:, 0, cols], in_weight[:, 1, cols], down_weight[:, cols]], axis=1)

    def attend(self, g, *ready):
        got = attend_forward(
            g,
            self.places[g],
            self.slopes,
            after(self.tokens, *ready),
            self.bias[g : g + 1],
            self.pieces[g],
        )
        self.done.append(got)
        return got[2]

    def join(self, *ready):
        self.qkv, self.ctx, self.lse = zip(*self.done)
        tokens = after(self.tokens, *ready)
        self.normed1, self.inverse1, self.low, self.low_t = join(
            self.places["o"], tokens, self.vec, self.ctx, self.pieces["o"]
        )
        return self.inverse1

    def feed(self, c, *ready):
        low = after(self.low, *ready)
        name = f"u{c}"
        self.acc, *saved = feed(self.places[name], low, self.acc, self.pieces[name])
        self.kept[c] = saved
        return self.acc

    def turn(self):
        self.result, self.d_hidden, self.d_low, self.d_low_t, self.sums2 = turn(
            self.acc, self.normed1, self.cotangent, self.vec
        )

    def feed_back(self, c, halves_out, *ready):
        d_hidden = after(self.d_hidden, *ready)
        name = f"u{c}"
        self.d_hidden, *dealt = feed_back(
            self.orders[name],
            halves_out,
            self.d_low,
            self.d_low_t,
            self.low_t,
            d_hidden,
            *self.kept[c],
            self.pieces[name],
        )
        return *dealt, self.d_hidden

    def rejoin(self, *ready):
        d_hidden = after(self.d_hidden, *ready)
        self.d_tokens, self.d_context, even, odd, self.sums1 = rejoin(
            self.places["o"],
            d_hidden,
            self.normed1,
            self.inverse1,
            self.vec,
            self.ctx,
            self.pieces["o"],
        )
        return even, odd, self.d_tokens

    def attend_back_first(self, g, *ready):
        self.d_context = after(self.d_context, *ready)
        self.pair, self.pair_sums = attend_backward_first(
            g, self.slopes, self.qkv[g], self.lse[g], self.d_context
        )
        return self.pair

    def attend_back_second(self, g, *ready):
        even, odd, sums, dqkv = attend_backward_second(
            g,
            self.places[g],
            self.slopes,
            self.qkv[g],
            self.lse[g],
            self.d_context,
            self.tokens_t,
            after(self.pair, *ready),
        )
        sums = jnp.concatenate([self.pair_sums, sums], axis=1)
        self.bias_grads.append(sums.reshape(2, self.n_tensor, HEAD))
        self.dqkv.append(dqkv)
        return even, odd, sums

    def tokens_back(self, *ready):
        pieces = [self.pieces[g] for g in range(self.groups)]
        self.d_tokens = tokens_backward(
            self.places[0], after(self.d_tokens, *ready), self.dqkv, pieces
        )
        return self.d_tokens

    def small_sums(self, back):
        qv_grad = jnp.stack(self.bias_grads, axis=2)[:, back].reshape(2, self.depth)
        return jnp.concatenate([self.sums1, self.sums2, qv_grad])

    def outputs(self, grads, sums):
        part = self.part
        units = [grads[f"u{c}"] for c in range(FF_CHUNKS)]
        qkv = [grads[g].reshape(self.rows, 3, HEAD) for g in range(self.groups)]
        in_grad = jnp.stack(
            [
                jnp.concatenate([unit[:, i * part : (i + 1) * part] for unit in units], axis=1)
                for i in range(2)
            ],
            axis=1,
        )
        return (
            self.result,
            self.d_tokens,
            jnp.concatenate(qkv, axis=2),
            sums[6:],
            grads["o"],
            sums[2],
            sums[0],
            sums[1],
            in_grad,
            jnp.concatenate([unit[:, 2 * part :] for unit in units], axis=1),
            sums[5],
            sums[3],
            sums[4],
        )


def plain(*values):
    n_tensor = lax.axis_size("tensor")
    index = jnp.arange(n_tensor, dtype=jnp.int32)
    place = jnp.arange(BLOCKS, dtype=jnp.int32)
    names = [0, 1, 2, "o"] + [f"u{c}" for c in range(FF_CHUNKS)]
    layer = Layer(
        values,
        index,
        {name: place for name in names},
        {name: jnp.concatenate([place, place, index]) for name in names},
    )
    depth = layer.depth

    def heads(piece):
        rows, lanes = piece.shape
        columns = lax.all_gather(
            piece.reshape(rows, lanes // HEAD, 1, HEAD), "tensor", axis=2, tiled=True
        )
        columns = lax.all_gather(columns.reshape(rows, -1), "dp", axis=0, tiled=True)
        return ([columns.reshape(BLOCKS, depth // BLOCKS, -1)], None)

    def units(piece):
        columns = lax.all_gather(lax.all_gather(piece, "tensor", axis=0), "dp", axis=1, tiled=True)
        blocks = columns.reshape(n_tensor, BLOCKS, depth // BLOCKS, -1)
        return ([jnp.moveaxis(blocks, 0, 1)], "grid")

    def total_rows(even, odd):
        blocks = jnp.concatenate([even, odd]).astype(F32)
        blocks = jnp.moveaxis(blocks, 0, -3)
        blocks = blocks.reshape(blocks.shape[:-3] + (-1, blocks.shape[-1]))
        return lax.psum_scatter(blocks, "dp", scatter_dimension=blocks.ndim - 2, tiled=True)

    def total_heads(even, odd):
        mine = total_rows(even, odd)
        rows = mine.shape[0]
        mine = mine.reshape(rows, -1, n_tensor, HEAD)
        mine = lax.psum_scatter(mine, "tensor", scatter_dimension=2, tiled=True)
        return mine.reshape(rows, -1)

    def total_units(even, odd):
        return lax.psum_scatter(total_rows(even, odd), "tensor", scatter_dimension=0, tiled=False)

    for g in range(layer.groups):
        layer.pieces[g] = heads(jnp.concatenate(layer.head_columns(g), axis=1))
        layer.attend(g)
    layer.pieces["o"] = heads(layer.out_weight)
    layer.join()
    for c in range(FF_CHUNKS):
        layer.pieces[f"u{c}"] = units(layer.unit_columns(c))
        layer.feed(c)
    layer.turn()
    grads = {}
    for c in range(FF_CHUNKS):
        grads[f"u{c}"] = total_units(*layer.feed_back(c, 2)[:2])
    grads["o"] = total_heads(*layer.rejoin()[:2])
    for g in range(layer.groups):
        layer.attend_back_first(g)
        grads[g] = total_heads(*layer.attend_back_second(g)[:2])
    layer.tokens_back()
    return layer.outputs(grads, lax.psum(layer.small_sums(index), ("dp", "tensor")))


def paired(*values):
    me = lax.axis_index("dp")
    at = lax.axis_index("tensor")

    def dp(value, bit):
        return lax.ppermute(value, "dp", [(i, i ^ bit) for i in range(8)])

    def tp(value, bit):
        return lax.ppermute(value, "tensor", [(i, i ^ bit) for i in range(4)])

    def stacked(left, right):
        return jnp.stack([left, right])

    x, y, core = 2, 4, 1
    order = jnp.array([0, 2, 1, 3], jnp.int32) ^ at
    index = jnp.arange(4, dtype=jnp.int32)
    back = index ^ at
    back = (back & 1) * 2 + (back >> 1)
    place = jnp.array([0, x, y, x | y, 1, x | 1, y | 1, x | y | 1], jnp.int32) ^ me
    lined = jnp.arange(BLOCKS, dtype=jnp.int32)
    places = {name: place for name in [0, 1, 2, "o", "u0", "u1"]}
    places["u2"] = lined
    orders = {
        "u0": jnp.concatenate([place, lined, index]),
        "u1": jnp.concatenate([place, lined, index]),
        "u2": jnp.concatenate([lined, place, back]),
    }
    layer = Layer(values, order, places, orders)
    depth = layer.depth

    own = jnp.concatenate(layer.head_columns(0), axis=1)
    others = jnp.concatenate(layer.head_columns(1) + layer.head_columns(2) + [layer.out_weight], axis=1)
    got = [tp(own, 2), tp(own, 1), tp(own, 3)]
    q0 = interleave([own, *got], HEAD)[None]
    units = [layer.unit_columns(c, q0) for c in range(FF_CHUNKS)]
    q0_got = [dp(q0, x), dp(q0, y), dp(q0, x | y)]
    far = tp(after(others, q0), 2)
    q0 = [q0, *q0_got]
    q0_core = [dp(value, core) for value in q0]
    others = interleave([others, after(far, q0_core)], HEAD)
    near, *units = lax.optimization_barrier((tp(others, 1), *units))
    others = interleave([others, near], 128)
    u2 = lax.all_gather(units[2], ("dp", "tensor"), axis=0, tiled=True)
    layer.pieces["u2"] = ([u2.reshape(BLOCKS, 4, layer.rows, -1)], "grid")
    layer.pieces[0] = (q0 + q0_core, None)
    q = jnp.stack([others[:, i * depth : (i + 1) * depth] for i in range(3)])
    q_x, q_y, q1_xy = dp(q, x), dp(q, y), dp(q[:1], x | y)
    u = stacked(units[0], units[1])
    u_far = tp(u, 2)

    tie = layer.attend(0, q, u, layer.tokens_t)
    q_x, q_y, q1_xy = after(q_x, tie), after(q_y, tie), after(q1_xy, tie)
    q1 = [q[:1], q_x[:1], q_y[:1], q1_xy]
    layer.pieces[1] = (q1 + [dp(value, core) for value in q1], None)
    qo_xy = dp(q_x[1:], y)
    u = jnp.stack([u, after(u_far, tie)], axis=1)
    u_near = tp(u, 1)

    tie = layer.attend(1, u)
    qo = [q[1:], q_x[1:], q_y[1:], after(qo_xy, tie)]
    qo = [value[None] for value in qo + [dp(value, core) for value in qo]]
    layer.pieces[2], layer.pieces["o"] = (qo, 0), (qo, 1)
    u_near = after(u_near, tie)
    u0, u1 = [jnp.concatenate([u[c], u_near[c]]) for c in range(2)]
    u0_x, u0_y = dp(u0, x), dp(u0, y)

    tie = layer.attend(2, u0, u1)
    u0_x, u0_y = after(u0_x, tie), after(u0_y, tie)
    u1_x = dp(after(u1, tie), x)
    u0_core = [dp(value, core) for value in after((u0, u0_x, u0_y), tie)]

    tie = layer.join(u0_x, u0_y)
    u1_x = after(u1_x, tie)
    u0_core = after_all(u0_core, tie)
    u0_xy = dp(after(u0_y, u1_x), x)
    u1_y = dp(after(u1, u1_x), y)

    tie = layer.feed(2, u1_x)
    u0_xy, u1_y = after(u0_xy, tie), after(u1_y, tie)
    u0_core = u0_core + [dp(u0_xy, core)]
    layer.pieces["u0"] = ([value[None] for value in [u0, u0_x, u0_y, u0_xy, *u0_core]], "grid")
    u1_xy = dp(u1_y, x)
    u1_core = [dp(value, core) for value in after((u1, u1_x, u1_y), tie)]

    tie = layer.feed(0, u1_y)
    u1_xy = after(u1_xy, tie)
    u1_core = after_all(u1_core, tie) + [dp(u1_xy, core)]
    layer.pieces["u1"] = ([value[None] for value in [u1, u1_x, u1_y, u1_xy, *u1_core]], "grid")
    layer.feed(1)
    layer.turn()

    grads = {}

    def add_core(even, odd, tie, blocks):
        odd = after(odd, tie)
        return [add_low(even[i], odd[i]) for i in blocks]

    def over_dp(dealt):
        mine = dealt.reshape(-1, dealt.shape[-1])
        mine = lax.psum_scatter(mine, "dp", scatter_dimension=0, tiled=True)
        return mine.reshape(dealt.shape[1:])

    dealt, _ = layer.feed_back(0, 1)
    f0 = over_dp(dealt)
    dealt, _ = layer.feed_back(1, 1)
    f1 = over_dp(dealt)
    even2, odd2, _ = layer.feed_back(2, 2)
    odd2 = dp(odd2, core)

    even_o, odd_o, tie = layer.rejoin()
    odd2 = after(odd2, tie)
    f2_sent = [add_low(even2[i : i + 2, 2:], odd2[i : i + 2, 2:]) for i in (0, 2)]
    f2 = [add_low(even2[i : i + 2, :2], odd2[i : i + 2, :2]) for i in (0, 2)]
    f2_left = tp(f2_sent[0], 1)
    odd_o = dp(odd_o, core)

    tie = layer.attend_back_first(0, *f2, *f2_sent)
    f2_left = after(f2_left, tie)
    f2_left_sent, f2_left = add_low(f2[0][:, 1], f2_left[:, 1]), add_low(f2[0][:, 0], f2_left[:, 0])
    f2_right = tp(after(f2_sent[1], tie), 1)

    even_q0, odd_q0, tie = layer.attend_back_second(0, f2_left, f2_left_sent)
    f2_right = after(f2_right, tie)
    f2_right_sent, f2_right = add_low(f2[1][:, 1], f2_right[:, 1]), add_low(f2[1][:, 0], f2_right[:, 0])
    f2_left_far = tp(after(f2_left_sent, tie), 2)
    odd_q0 = dp(odd_q0, core)
    f0 = after(f0, tie)
    f0_near = tp(f0[2:], 1)

    tie = layer.attend_back_first(1, f2_right, f2_right_sent, f0)
    f0_near = after(f0_near, tie)
    f0_sent, f0 = add_low(f0[1], f0_near[1]), add_low(f0[0], f0_near[0])
    f0_far = tp(f0_sent, 2)
    f2_left = add_low(f2_left, after(f2_left_far, tie))
    f2_right_far = tp(after(f2_right_sent, tie), 2)
    odd_oq = after((odd_o, odd_q0), tie)
    oq_sent = jnp.stack([add_low(even[2:], odd[2:]) for even, odd in zip((even_o, even_q0), odd_oq)])
    oq = jnp.stack([add_low(even[:2], odd[:2]) for even, odd in zip((even_o, even_q0), odd_oq)])
    oq_first = dp(oq_sent, y)

    even_q1, odd_q1, tie = layer.attend_back_second(1, f2_left, oq_sent, oq, f0, f0_sent)
    grads["u0"] = f0.astype(F32) + after(f0_far, tie).astype(F32)
    f2_right = add_low(f2_right, after(f2_right_far, tie))
    f2_first = dp(f2_right, y)
    oq_first = after(oq_first, tie)
    oq_sent, oq = add_low(oq[:, 1], oq_first[:, 1]), add_low(oq[:, 0], oq_first[:, 0])
    oq_second = dp(oq_sent, x)
    odd_q1 = dp(odd_q1, core)

    tie = layer.attend_back_first(2, f2_right, oq_sent, oq)
    f2_first = after(f2_first, tie)
    f2 = [add_low(f2_left[0], f2_first[0]), add_low(f2_left[1], f2_first[1])]
    f2_second = dp(f2[1], x)
    oq = add_low(oq, after(oq_second, tie)).reshape(-1, depth)
    oq_sent, oq = halves(oq, 128)
    oq_near = tp(oq_sent, 1)
    f1 = after(f1, tie)
    f1_near = tp(f1[2:], 1)
    q1 = add_core(even_q1, odd_q1, tie, range(4))
    q1_sent = stacked(q1[2], q1[3])
    q1_first = dp(q1_sent, y)

    even_q2, odd_q2, tie = layer.attend_back_second(2, *f2, oq, oq_sent, q1_sent, q1[0], q1[1], f1)
    f1_near = after(f1_near, tie)
    f1_sent, f1 = add_low(f1[1], f1_near[1]), add_low(f1[0], f1_near[0])
    f1_far = tp(f1_sent, 2)
    odd_q2 = dp(odd_q2, core)
    sums = layer.small_sums(back)
    sums_got = dp(sums, core)
    q1_first = after(q1_first, tie)
    q1 = [add_low(q1[0], q1_first[0]), add_low(q1[1], q1_first[1])]
    q1_second = dp(q1[1], x)
    oq_sent, oq = halves(add_low(oq, after(oq_near, tie)), HEAD)
    oq_far = tp(oq_sent, 2)
    grads["u2"] = f2[0].astype(F32) + after(f2_second, tie).astype(F32)

    tie = [odd_q2]
    q2 = add_core(even_q2, odd_q2, tie, range(4))
    q2_got = [dp(q2[1], x), dp(q2[2], y), dp(q2[3], x | y)]
    tie = layer.tokens_back(q2)
    q2_got = after_all(q2_got, tie)
    grads["u1"] = f1.astype(F32) + after(f1_far, tie).astype(F32)
    sums = sums + after(sums_got, tie)
    sums_got = dp(sums, x)
    q1 = add_low(q1[0], after(q1_second, tie))
    q2 = four(q2[0], *q2_got).astype(BF16)
    last = jnp.stack([q1, q2]).reshape(-1, depth)
    last = [pick(last, HEAD, i) for i in range(4)]
    last_got = [tp(last[1], 2), tp(last[2], 1), tp(last[3], 3)]
    oq = (oq.astype(F32) + after(oq_far, last).astype(F32)).reshape(2, layer.rows, -1)
    grads["o"], grads[0] = oq[0], oq[1]
    sums = sums + after(sums_got, last)
    sums_got = dp(sums, y)
    sums = sums + sums_got
    last = four(last[0], last_got[1], last_got[0], last_got[2]).reshape(2, layer.rows, -1)
    grads[1], grads[2] = last[0], last[1]
    for bit in (1, 2):
        sums = sums + tp(sums, bit)
    return layer.outputs(grads, sums)


def local(suits, *values):
    return paired(*values) if suits else plain(*values)


def solution(mesh):
    rows_all = P(("dp", "tensor"), None)
    columns_3d = P("dp", None, "tensor")
    columns_2d = P("dp", "tensor")
    return jax.shard_map(
        functools.partial(local, dict(mesh.shape) == {"dp": 8, "tensor": 4}),
        mesh=mesh,
        in_specs=(
            rows_all,
            columns_3d,
            P(),
            columns_2d,
            P(),
            P(),
            P(),
            columns_3d,
            columns_2d,
            P(),
            P(),
            P(),
            rows_all,
        ),
        out_specs=(
            rows_all,
            rows_all,
            columns_3d,
            P(),
            columns_2d,
            P(),
            P(),
            P(),
            columns_3d,
            columns_2d,
            P(),
            P(),
            P(),
        ),
        check_vma=False,
    )
```
